32 devices in a mesh: wide: 8 (over z, core), narrow: 4 (over y, x).
Axes of the slice: x: 2, y: 2, z: 4, core: 2. Of those that a mesh axis runs over, the one named last changes fastest.
Arguments:
- tokens: bfloat16 [8192, 2304], P(('wide', 'narrow')), may hold values from -6 to 6
- target: bfloat16 [8192, 2304], P(('wide', 'narrow')), may hold values from -6 to 6
- combine: bfloat16 [8192], P(('wide', 'narrow')), may hold values from 0.25 to 1
- filled: int32 [8], P('wide'), may hold values from 512 to 1024, as said below
- w_gate: bfloat16 [2304, 2048], P(None, 'narrow'), may hold values from -0.125 to 0.125
- w_up: bfloat16 [2304, 2048], P(None, 'narrow'), may hold values from -0.125 to 0.125
- w_down: bfloat16 [2048, 2304], P('narrow'), may hold values from -0.125 to 0.125
- momentum: float32 [8, 2048, 2304], P('wide', 'narrow'), may hold values from -6 to 6
Outputs:
- momentum_out: float32 [8, 2048, 2304], P('wide', 'narrow')
- update: bfloat16 [2048, 2304], P('narrow')
The draws below stay inside these ranges and needn't reach their ends.
Inputs may be any that keep to these rules, and one draw needn't show every extreme that they name: `filled`: rows of a replica at or after its count are empty buffer slots; some replica's buffer is full in every draw.
All inputs are finite; a program needn't handle non-finite values.
Results may differ from the reference program's by a relative error of at most 0.015.
Values may be sent and summed in bfloat16 or wider, within the bound.
A program may use at most 128 MiB of HBM per device.

```python
import math
import jax
import jax.numpy as jnp
from jax import lax

D = 2304
F = 2048
SPAN = 64
BAND = 16
TOK_DEV = 1024
TOKENS = 8192
N_WIDE = 8
N_NARROW = 4


def draw_filled(key, part):
    counts = jax.random.randint(key, (N_WIDE,), TOK_DEV // 2, TOK_DEV + 1)
    full_index = jax.random.randint(jax.random.fold_in(key, 11), (), 0, N_WIDE)
    return jnp.where(jnp.arange(N_WIDE) == full_index, TOK_DEV, counts).astype(jnp.int32)


def block_scale(key, shape, cuts, smallest, top_value):
    level = 1.0
    for axis_at, parts in cuts:
        heights = jax.random.uniform(jax.random.fold_in(jax.random.fold_in(key, 6), axis_at), (parts,), jnp.float32, smallest / len(cuts), top_value / len(cuts))
        level = level * jnp.repeat(jnp.exp(heights), shape[axis_at] // parts).reshape((-1,) + (1,) * (len(shape) - 1 - axis_at))
    return level


def gaussian(rng, shape, scale, limit, cuts=(), held_as=jnp.bfloat16):
    result = jax.random.normal(rng, shape, jnp.float32) * scale
    if len(cuts) > 0:
        result = block_scale(rng, shape, cuts, -0.22, 0.18) * result
    return jnp.clip(result, min=-limit, max=limit).astype(held_as)


def setup_inputs(seed: int = 0) -> dict:
    splits = jax.random.split(jax.random.key(seed), 9)
    tokens = gaussian(splits[0], (TOKENS, D), 1.0, 6.0, ((0, 32),))
    target = gaussian(splits[1], (TOKENS, D), 1.0, 6.0, ((0, 32),))
    combine = jnp.clip(0.25 + 0.75 * jax.random.uniform(splits[2], (TOKENS,), jnp.float32) ** block_scale(splits[2], (TOKENS,), ((0, 32),), -0.2, 0.2), 0.25, 1.0).astype(jnp.bfloat16)
    filled = draw_filled(jax.random.fold_in(splits[8], 71), 0)
    w_gate = gaussian(splits[4], (D, F), D ** -0.5, 0.125, ((1, 4),))
    w_up = gaussian(splits[5], (D, F), D ** -0.5, 0.125, ((1, 4),))
    w_down = gaussian(splits[6], (F, D), F ** -0.5, 0.125, ((0, 4),))
    momentum = gaussian(splits[7], (N_WIDE, F, D), 1.0, 6.0, ((0, 8), (1, 4)), jnp.float32)
    return dict(tokens=tokens, target=target, combine=combine, filled=filled, w_gate=w_gate, w_up=w_up, w_down=w_down, momentum=momentum)


def cosine_table():
    freq_index = jnp.arange(BAND)[:, None].astype(jnp.float32)
    cell_index = jnp.arange(SPAN)[None, :].astype(jnp.float32)
    factor = jnp.where(freq_index == 0, math.sqrt(1.0 / SPAN), math.sqrt(2.0 / SPAN))
    return factor * jnp.cos(math.pi * (2.0 * cell_index + 1.0) * freq_index / (2.0 * SPAN))

def encode(matrix, table):
    height, breadth = matrix.shape
    blocks = matrix.reshape(height // SPAN, SPAN, breadth // SPAN, SPAN)
    return jnp.einsum('kn,anbm,lm->abkl', table, blocks, table, precision=lax.Precision.HIGHEST)

def decode(band_coef, table):
    across, down_count = (band_coef.shape[0], band_coef.shape[1])
    blocks = jnp.einsum('kn,abkl,lm->anbm', table, band_coef, table, precision=lax.Precision.HIGHEST)
    return blocks.reshape(across * SPAN, down_count * SPAN)

def reference(tokens, target, combine, filled, w_gate, w_up, w_down, momentum):
    table = cosine_table()
    factor = 1.0 / math.sqrt(TOK_DEV)
    group_units = F // N_NARROW

    def replica(index):
        first_row = index * TOK_DEV
        rows_in = lax.dynamic_slice_in_dim(tokens, first_row, TOK_DEV, 0)
        rows_target = lax.dynamic_slice_in_dim(target, first_row, TOK_DEV, 0).astype(jnp.float32)
        weight = lax.dynamic_slice_in_dim(combine, first_row, TOK_DEV, 0).astype(jnp.float32)[:, None]
        gate_proj = jnp.dot(rows_in, w_gate, preferred_element_type=jnp.float32)
        up_proj = jnp.dot(rows_in, w_up, preferred_element_type=jnp.float32)
        hidden = (jax.nn.silu(gate_proj) * up_proj).astype(jnp.bfloat16)
        grouped = jnp.einsum('tnf,nfd->ntd', hidden.reshape(TOK_DEV, N_NARROW, group_units).astype(jnp.float32), w_down.reshape(N_NARROW, group_units, D).astype(jnp.float32))
        summed = lax.optimization_barrier(jnp.sum(lax.optimization_barrier(grouped.astype(jnp.bfloat16)).astype(jnp.float32), axis=0))
        expert_out = weight * summed
        live_rows = jnp.arange(TOK_DEV, dtype=jnp.int32) < filled[index]
        error = jnp.where(live_rows[:, None], weight * (expert_out - rows_target), 0.0).astype(jnp.bfloat16)
        grad = jnp.dot(hidden.T, error, preferred_element_type=jnp.float32) * factor
        moved = 0.999 * momentum[index] + grad
        band_coef = encode(moved, table)
        residue = moved - decode(band_coef, table)
        return (residue, band_coef)
    momentum_out, bands = lax.map(replica, jnp.arange(N_WIDE, dtype=jnp.int32))
    update = (decode(lax.optimization_barrier(jnp.sum(bands, axis=0)), table) / N_WIDE).astype(jnp.bfloat16)
    return (momentum_out, update)
```

```python
import functools
import math

import jax
import jax.numpy as jnp
import numpy as np
from jax import lax
from jax.experimental import pallas as pl
from jax.experimental.pallas import tpu as pltpu
from jax.sharding import PartitionSpec as P

SPAN = 64
BAND = 16
TILE = 256
BF = jnp.bfloat16
F32 = jnp.float32


def block_table(blocks):
    row = np.arange(blocks * BAND)[:, None]
    col = np.arange(blocks * SPAN)[None, :]
    factor = np.where(row % BAND == 0, math.sqrt(1.0 / SPAN), math.sqrt(2.0 / SPAN))
    value = factor * np.cos(math.pi * (2.0 * (col % SPAN) + 1.0) * (row % BAND) / (2.0 * SPAN))
    return np.where(row // BAND == col // SPAN, value, 0.0).astype(np.float32)


def halves(value):
    high = value.astype(BF)
    return high, (value - high.astype(F32)).astype(BF)


def dot3(left, right, contract):
    dims = (((contract[0],), (contract[1],)), ((), ()))
    dot = functools.partial(lax.dot_general, dimension_numbers=dims, preferred_element_type=F32)
    return dot(left[0], right[0]) + (dot(left[1], right[0]) + dot(left[0], right[1]))


def decode_tile(band, tables):
    wide = dot3(halves(band), tables[3], (1, 0))
    return dot3(tables[1], halves(wide), (1, 0))


def read_tables(refs):
    return [(refs[2 * k][...], refs[2 * k + 1][...]) for k in range(4)]


def grad_kernel(factor, subs, hidden_t, error, momentum, *refs):
    residue, band_t = refs[8:]
    tables = read_tables(refs)
    kept_t = TILE // SPAN * BAND
    for k in range(subs):
        at = slice(k * TILE, (k + 1) * TILE)
        grad = jnp.dot(hidden_t[...], error[:, at], preferred_element_type=F32)
        moved = 0.999 * momentum[0, :, at] + factor * grad
        squeezed = dot3(tables[0], halves(moved), (1, 0))
        band = dot3(halves(squeezed), tables[2], (1, 0))
        band_t[k * kept_t : (k + 1) * kept_t, :] = band.T
        residue[0, :, at] = moved - decode_tile(band, tables)


def whole(a):
    return pl.BlockSpec(a.shape, lambda i: (0,) * a.ndim)


def grad_step(hidden_t, error, momentum, tables, factor):
    units, rows = hidden_t.shape
    width = error.shape[1]
    subs = 3 if width // TILE % 3 == 0 else 1
    step = TILE * subs
    tiles = width // step
    kept = units // SPAN * BAND
    kept_t = step // SPAN * BAND
    return pl.pallas_call(
        functools.partial(grad_kernel, factor, subs),
        grid=(tiles,),
        in_specs=[
            whole(hidden_t),
            pl.BlockSpec((rows, step), lambda i: (0, i)),
            pl.BlockSpec((1, units, step), lambda i: (0, 0, i)),
        ]
        + [whole(t) for t in tables],
        out_specs=[
            pl.BlockSpec((1, units, step), lambda i: (0, 0, i)),
            pl.BlockSpec((kept_t, kept), lambda i: (i, 0)),
        ],
        out_shape=[
            jax.ShapeDtypeStruct((1, units, width), F32),
            jax.ShapeDtypeStruct((tiles * kept_t, kept), F32),
        ],
        name="grad_step",
    )(hidden_t, error, momentum, *tables)


def update_kernel(replicas, subs, bands, *refs):
    update = refs[8]
    tables = read_tables(refs)
    kept_t = TILE // SPAN * BAND
    for k in range(subs):
        band = bands[k * kept_t : (k + 1) * kept_t, :].T
        tile = decode_tile(band, tables) * (1.0 / replicas)
        update[:, k * TILE : (k + 1) * TILE] = tile.astype(BF)


def update_step(bands, tables, units, width, replicas):
    rows_t, kept = bands.shape
    subs = 3 if width // TILE % 3 == 0 else 1
    step = TILE * subs
    tiles = width // step
    return pl.pallas_call(
        functools.partial(update_kernel, replicas, subs),
        grid=(tiles,),
        in_specs=[pl.BlockSpec((rows_t // tiles, kept), lambda i: (i, 0))]
        + [whole(t) for t in tables],
        out_specs=pl.BlockSpec((units, step), lambda i: (0, i)),
        out_shape=jax.ShapeDtypeStruct((units, width), BF),
        name="update_step",
    )(bands, *tables)


def make_tables(units):
    left = block_table(units // SPAN)
    right = block_table(TILE // SPAN)
    pieces = []
    for table in (left, left.T, right.T, right):
        high = table.astype(BF)
        pieces += [high, (table - high.astype(np.float32)).astype(BF)]
    return [jnp.asarray(np.ascontiguousarray(p)) for p in pieces]


def remote(src, dst, send, recv, index, axis, peer):
    return pltpu.make_async_remote_copy(
        src_ref=src,
        dst_ref=dst,
        send_sem=send.at[index],
        recv_sem=recv.at[index],
        device_id={axis: peer},
        device_id_type=pl.DeviceIdType.MESH,
    )


def greet(axis, peers):
    barrier = pltpu.get_barrier_semaphore()
    for peer in peers:
        pl.semaphore_signal(
            barrier, inc=1, device_id={axis: peer}, device_id_type=pl.DeviceIdType.MESH
        )
    pl.semaphore_wait(barrier, len(peers))


def split_kernel(
    factor, tokens_hbm, target_hbm, combine, filled, gate_hbm, up_hbm, down_hbm, momentum_hbm, *refs
):
    tables_hbm, (residue_hbm, band_t) = refs[:8], refs[8:10]
    (
        tok, target, weight, gate, up, gate_y, up_y, down, hidden, hidden_t, lent_t,
        kept, sent, came, errors, state,
    ) = refs[10:26]
    tables_vmem = refs[26:34]
    send, recv, local = refs[34:37]
    me, place = lax.axis_index("narrow"), lax.axis_index("wide")
    x_peer = me + 1 - 2 * (me % 2)
    y_peer = (me + 2) % 4
    twin = place + 1 - 2 * (place % 2)
    z_peer = place + 2 - 4 * (place // 2 % 2)
    quarter = place % 4
    rows, width = target.shape
    units = gate.shape[1]
    deep, flat = width // 4, units // 4
    half = deep // 2
    chunks = width // TILE
    parts = 4 * (units // TILE)

    sizes = [2] + [parts] * 4 + [chunks] * 4 + [units // TILE] + [chunks] * 4
    starts = [sum(sizes[:k]) for k in range(len(sizes) + 1)]

    def link(kind, index, src, dst, axis, peer):
        return remote(src, dst, send, recv, starts[kind] + index, axis, peer)

    def cols(c):
        if isinstance(c, int):
            return pl.ds(c * TILE, TILE)
        return pl.ds(pl.multiple_of(c * TILE, TILE), TILE)

    def token_copy(k):
        part = rows // 2
        src = tokens_hbm.at[pl.ds(k * part, part)]
        return link(0, k, src, tok.at[pl.ds(rows + k * part, part)], "narrow", x_peer)

    def piece(k, ref, owner):
        first = pl.multiple_of(owner * deep + k % 2 * half, 32)
        return ref.at[pl.ds(first, half), cols(k // 4)]

    def weight_copy(kind, k):
        mine, theirs = ((gate_hbm, gate_y), (up_hbm, up_y))[k // 2 % 2]
        if kind == 1:
            return link(1, k, piece(k, mine, quarter), piece(k, theirs, quarter), "narrow", y_peer)
        if kind == 4:
            there = piece(k, theirs, (quarter + 2) % 4)
            return link(4, k, there, there, "wide", twin)
        here = piece(k, theirs, quarter)
        return link(kind, k, here, here, "wide", z_peer if kind == 2 else twin)

    def down_piece(c, ref, first, owner):
        return ref.at[pl.ds(pl.multiple_of(first + owner * flat, 32), flat), cols(c)]

    def down_copy(kind, c):
        if kind == 5:
            src = down_piece(c, down_hbm, 0, quarter)
            return link(5, c, src, down_piece(c, down, units, quarter), "narrow", y_peer)
        if kind == 8:
            there = down_piece(c, down, units, (quarter + 2) % 4)
            return link(8, c, there, there, "wide", twin)
        here = down_piece(c, down, units, quarter)
        return link(kind, c, here, here, "wide", z_peer if kind == 6 else twin)

    def lend_copy(t):
        at = pl.ds(t * TILE, TILE)
        dst = hidden_t.at[at, pl.ds(2 * rows, 2 * rows)]
        return link(9, t, lent_t.at[at], dst, "narrow", y_peer)

    def sum_copy(c):
        return link(10, c, sent.at[:, cols(c)], came.at[:, cols(c)], "narrow", x_peer)

    def slot(k, c):
        return errors.at[pl.ds(k * rows, rows), cols(c)]

    def error_x(c):
        return link(11, c, slot(0, c), slot(1, c), "narrow", x_peer)

    def error_y(c):
        return link(12, c, slot(0, c), slot(2, c), "narrow", y_peer)

    def relay_by_y(c):
        return link(13, c, slot(1, c), slot(3, c), "narrow", y_peer)

    def relay_by_x(c):
        return link(13, c, slot(2, c), slot(3, c), "narrow", x_peer)

    def load(k, src, dst):
        return pltpu.make_async_copy(src, dst, local.at[k])

    barrier = pltpu.get_barrier_semaphore()
    for axis, peer in (("narrow", x_peer), ("narrow", y_peer), ("wide", twin), ("wide", z_peer)):
        pl.semaphore_signal(
            barrier, inc=1, device_id={axis: peer}, device_id_type=pl.DeviceIdType.MESH
        )
    loads = [
        load(0, tokens_hbm, tok.at[pl.ds(0, rows)]),
        load(1, gate_hbm, gate),
        load(2, up_hbm, up),
        load(3, down_hbm, down.at[pl.ds(0, units)]),
        load(4, target_hbm, target),
        load(5, momentum_hbm.at[0], state),
    ]
    loads += [load(6 + k, s, d) for k, (s, d) in enumerate(zip(tables_hbm, tables_vmem))]
    for copy in loads:
        copy.start()
    pl.semaphore_wait(barrier, 4)
    for k in range(2):
        token_copy(k).start()
    for k in range(parts):
        weight_copy(1, k).start()

    @pl.loop(0, chunks)
    def _(c):
        down_copy(5, c).start()

    row_ids = me * rows + lax.broadcasted_iota(jnp.int32, combine.shape, 1)
    live = jnp.where(row_ids < filled[0], combine[...].astype(F32), 0.0)
    weight[...] = jnp.broadcast_to(live, (weight.shape[1], rows)).T

    def expert(first, count, gates, ups, base, turned, t):
        block = tok[first : first + count, :]
        gated = jnp.dot(block, gates[:, cols(t)], preferred_element_type=F32)
        raised = jnp.dot(block, ups[:, cols(t)], preferred_element_type=F32)
        value = gated / (1.0 + jnp.exp(-gated)) * raised
        hidden[first : first + count, base + t * TILE : base + (t + 1) * TILE] = value.astype(BF)
        turned[t * TILE : (t + 1) * TILE, first : first + count] = value.T.astype(BF)

    def pass_weight(k):
        weight_copy(1, k).wait_recv()
        weight_copy(2, k).start()
        weight_copy(3, k).start()

    def share_weight(k):
        weight_copy(2, k).wait_recv()
        weight_copy(4, k).start()

    def take_weights(first, count):
        for k in range(first, first + count):
            weight_copy(3, k).wait_recv()
            weight_copy(4, k).wait_recv()

    def pass_down(c):
        down_copy(5, c).wait_recv()
        down_copy(6, c).start()
        down_copy(7, c).start()

    def share_down(c):
        down_copy(6, c).wait_recv()
        down_copy(8, c).start()

    def take_down(c):
        down_copy(7, c).wait_recv()
        down_copy(8, c).wait_recv()

    def partial(c):
        part = jnp.dot(hidden[...], down[:, cols(c)], preferred_element_type=F32)
        kept[:, cols(c)] = part[:rows]
        sent[:, cols(c)] = part[rows:].astype(BF)
        sum_copy(c).start()

    def error(c):
        sum_copy(c).wait_recv()
        total = kept[:, cols(c)] + came[:, cols(c)].astype(F32)
        scale = jnp.concatenate([weight[...]] * (TILE // weight.shape[1]), axis=1)
        value = scale * (scale * total - target[:, cols(c)].astype(F32))
        errors[pl.ds(0, rows), cols(c)] = value.astype(BF)
        error_x(c).start()
        error_y(c).start()

    def relay(c):
        @pl.when(c % 3 != 2)
        def _():
            error_x(c).wait_recv()
            relay_by_y(c).start()

        @pl.when(c % 3 == 2)
        def _():
            error_y(c).wait_recv()
            relay_by_x(c).start()

    tables = lambda: [(tables_vmem[2 * k][...], tables_vmem[2 * k + 1][...]) for k in range(4)]

    def store(c):
        return pltpu.make_async_copy(
            state.at[:, cols(c)], residue_hbm.at[0, :, cols(c)], local.at[14 + c]
        )

    kept_t = TILE // SPAN * BAND

    def gradient(c):
        @pl.when(c % 3 != 2)
        def _():
            error_y(c).wait_recv()

        @pl.when(c % 3 == 2)
        def _():
            error_x(c).wait_recv()

        relay_by_y(c).wait_recv()
        grad = jnp.dot(hidden_t[...], errors[:, cols(c)], preferred_element_type=F32)
        moved = 0.999 * state[:, cols(c)] + factor * grad
        table = tables()
        squeezed = dot3(table[0], halves(moved), (1, 0))
        band = dot3(halves(squeezed), table[2], (1, 0))
        band_t[pl.ds(pl.multiple_of(c * kept_t, kept_t), kept_t), :] = band.T
        state[:, cols(c)] = moved - decode_tile(band, table)
        store(c).start()

    for k in range(3):
        loads[k].wait()
    for t in range(units // TILE):
        expert(0, rows, gate, up, 0, hidden_t, t)
    pass_weight(0)
    for k in range(1, 6):
        pass_weight(k)
        if k < 5:
            share_weight(k - 1)
    take_weights(0, 4)
    expert(0, rows, gate_y, up_y, units, lent_t, 0)
    share_weight(4)
    pass_weight(6)
    share_weight(5)
    pass_weight(7)
    for k in range(2):
        token_copy(k).wait_recv()
    for t in range(units // TILE):
        expert(rows, rows, gate, up, 0, hidden_t, t)
    share_weight(6)
    expert(rows, rows, gate_y, up_y, units, lent_t, 0)
    lend_copy(0).start()
    share_weight(7)
    for c in range(3):
        pass_down(c)
    share_down(0)
    take_weights(4, 4)
    expert(0, 2 * rows, gate_y, up_y, units, lent_t, 1)
    lend_copy(1).start()
    for copy in loads[3:]:
        copy.wait()
    share_down(1)
    take_down(0)
    pass_down(3)
    partial(0)
    share_down(2)
    take_down(1)
    pass_down(4)
    partial(1)

    lag = 3

    @pl.loop(0, chunks + lag)
    def _(c):
        @pl.when(c < chunks)
        def _():
            error(c)

        @pl.when((c >= 1) & (c <= chunks))
        def _():
            relay(c - 1)

        @pl.when(c + 5 < chunks)
        def _():
            pass_down(c + 5)

        @pl.when(c + 3 < chunks)
        def _():
            share_down(c + 3)

        @pl.when(c + 2 < chunks)
        def _():
            take_down(c + 2)
            partial(c + 2)

        @pl.when(c == 0)
        def _():
            for t in range(units // TILE):
                lend_copy(t).wait_recv()

        @pl.when(c >= lag)
        def _():
            gradient(c - lag)

    for k in range(2):
        token_copy(k).wait_send()
    for k in range(parts):
        for kind in range(1, 5):
            weight_copy(kind, k).wait_send()
    for t in range(units // TILE):
        lend_copy(t).wait_send()

    @pl.loop(0, chunks)
    def _(c):
        for kind in range(5, 9):
            down_copy(kind, c).wait_send()
        sum_copy(c).wait_send()
        error_x(c).wait_send()
        error_y(c).wait_send()
        relay_by_y(c).wait_send()
        store(c).wait()


def split_step(tokens, target, combine, filled, w_gate, w_up, w_down, momentum, tables, factor):
    rows, width = tokens.shape
    units = w_down.shape[0]
    vmem = pl.BlockSpec(memory_space=pltpu.VMEM)
    hbm = pl.BlockSpec(memory_space=pl.ANY)
    block = lambda *shape: pltpu.VMEM(shape, BF)
    chunks = width // TILE
    tiles = units // TILE
    count = 2 + 16 * tiles + 8 * chunks + tiles
    return pl.pallas_call(
        functools.partial(split_kernel, factor),
        in_specs=[hbm, hbm, vmem, pl.BlockSpec(memory_space=pltpu.SMEM)] + [hbm] * 12,
        out_specs=[hbm, vmem],
        out_shape=[
            jax.ShapeDtypeStruct((1, units, width), F32),
            jax.ShapeDtypeStruct((width // SPAN * BAND, units // SPAN * BAND), F32),
        ],
        scratch_shapes=[
            block(2 * rows, width), block(rows, width), pltpu.VMEM((rows, 128), F32),
            block(width, units), block(width, units), block(width, units), block(width, units),
            block(2 * units, width), block(2 * rows, 2 * units), block(units, 4 * rows),
            block(units, 2 * rows), pltpu.VMEM((rows, width), F32), block(rows, width),
            block(rows, width), block(4 * rows, width), pltpu.VMEM((units, width), F32),
        ]
        + [block(*t.shape) for t in tables]
        + [
            pltpu.SemaphoreType.DMA((count,)), pltpu.SemaphoreType.DMA((count,)),
            pltpu.SemaphoreType.DMA((14 + chunks,)),
        ],
        compiler_params=pltpu.CompilerParams(
            collective_id=0, has_side_effects=True, vmem_limit_bytes=60 << 20
        ),
        name="split_step",
    )(
        tokens, target, combine.reshape(1, rows), filled, w_gate, w_up, w_down, momentum, *tables
    )


def band_kernel(count, band, total, outgoing, arrived, summed, gathered, send, recv):
    me = lax.axis_index("wide")
    peers = [(me + k) % count for k in range(1, count)]
    greet("wide", peers)
    share = band.shape[0] // count
    outgoing[...] = band[...].reshape(count, share, band.shape[1]).astype(BF)
    first = [
        remote(outgoing.at[p], arrived.at[k], send, recv, k, "wide", p)
        for k, p in enumerate(peers)
    ]
    for copy in first:
        copy.start()
    amount = outgoing[me].astype(F32)
    for k, copy in enumerate(first):
        copy.wait_recv()
        amount = amount + arrived[k].astype(F32)
    summed[...] = amount.astype(BF)
    second = [
        remote(summed, gathered.at[me], send, recv, count + k, "wide", p)
        for k, p in enumerate(peers)
    ]
    for copy in second:
        copy.start()
    for copy in second:
        copy.wait_recv()
    for copy in first + second:
        copy.wait_send()
    gathered[me] = summed[...]
    total[...] = gathered[...].astype(F32).reshape(band.shape)


def band_sum(band, count):
    share = band.shape[0] // count
    vmem = pl.BlockSpec(memory_space=pltpu.VMEM)
    block = lambda *shape: pltpu.VMEM(shape + (share, band.shape[1]), BF)
    return pl.pallas_call(
        functools.partial(band_kernel, count),
        in_specs=[vmem],
        out_specs=vmem,
        out_shape=jax.ShapeDtypeStruct(band.shape, F32),
        scratch_shapes=[
            block(count), block(count - 1), block(), block(count),
            pltpu.SemaphoreType.DMA((2 * count,)), pltpu.SemaphoreType.DMA((2 * count,)),
        ],
        compiler_params=pltpu.CompilerParams(collective_id=1, has_side_effects=True),
        name="band_sum",
    )(band)


def forward(tokens, target, combine, filled, w_gate, w_up, w_down):
    local_rows = tokens.shape[0]
    piece = lax.all_gather(tokens, "narrow", axis=0, tiled=True)
    gate_proj = jnp.dot(piece, w_gate, preferred_element_type=F32)
    up_proj = jnp.dot(piece, w_up, preferred_element_type=F32)
    hidden = (jax.nn.silu(gate_proj) * up_proj).astype(BF)
    summed = lax.psum_scatter(
        jnp.dot(hidden, w_down, preferred_element_type=F32).astype(BF),
        "narrow",
        scatter_dimension=0,
        tiled=True,
    ).astype(F32)
    weight = combine.astype(F32)[:, None]
    row_ids = lax.axis_index("narrow") * local_rows + jnp.arange(local_rows, dtype=jnp.int32)
    error = jnp.where(
        (row_ids < filled[0])[:, None], weight * (weight * summed - target.astype(F32)), 0.0
    ).astype(BF)
    return hidden.T, lax.all_gather(error, "narrow", axis=0, tiled=True)


def body(tokens, target, combine, filled, w_gate, w_up, w_down, momentum):
    units, width = w_down.shape
    narrow, replicas = lax.axis_size("narrow"), lax.axis_size("wide")
    total_rows = tokens.shape[0] * narrow
    tables = make_tables(units)
    factor = 1.0 / math.sqrt(total_rows)
    fits = units == 2 * TILE and width % TILE == 0 and tokens.shape[0] % 128 == 0
    if narrow == 4 and replicas % 4 == 0 and fits:
        residue, band = split_step(
            tokens, target, combine, filled, w_gate, w_up, w_down, momentum, tables, factor
        )
        total = band_sum(band, replicas)
    else:
        hidden_t, errors = forward(tokens, target, combine, filled, w_gate, w_up, w_down)
        residue, band = grad_step(hidden_t, errors, momentum, tables, factor)
        bands = lax.all_gather(band.astype(BF)[None], "wide", axis=0, tiled=True)
        total = jnp.sum(bands.astype(F32), axis=0)
    return residue, update_step(total, tables, units, width, replicas)


def solution(mesh):
    in_specs = (
        P(("wide", "narrow"), None),
        P(("wide", "narrow"), None),
        P(("wide", "narrow")),
        P("wide"),
        P(None, "narrow"),
        P(None, "narrow"),
        P("narrow", None),
        P("wide", "narrow", None),
    )
    out_specs = (P("wide", "narrow", None), P("narrow", None))
    return jax.shard_map(body, mesh=mesh, in_specs=in_specs, out_specs=out_specs, check_vma=False)
```

```python
import functools
import math

import jax
import jax.numpy as jnp
import numpy as np
from jax import lax
from jax.experimental import pallas as pl
from jax.experimental.pallas import tpu as pltpu
from jax.sharding import PartitionSpec as P

SPAN = 64
BAND = 16
TILE = 256
BF = jnp.bfloat16
F32 = jnp.float32


def block_table(blocks):
    row = np.arange(blocks * BAND)[:, None]
    col = np.arange(blocks * SPAN)[None, :]
    factor = np.where(row % BAND == 0, math.sqrt(1.0 / SPAN), math.sqrt(2.0 / SPAN))
    value = factor * np.cos(math.pi * (2.0 * (col % SPAN) + 1.0) * (row % BAND) / (2.0 * SPAN))
    return np.where(row // BAND == col // SPAN, value, 0.0).astype(np.float32)


def halves(value):
    high = value.astype(BF)
    return high, (value - high.astype(F32)).astype(BF)


def dot3(left, right, contract):
    dims = (((contract[0],), (contract[1],)), ((), ()))
    dot = functools.partial(lax.dot_general, dimension_numbers=dims, preferred_element_type=F32)
    return dot(left[0], right[0]) + (dot(left[1], right[0]) + dot(left[0], right[1]))


def decode_tile(band, tables):
    wide = dot3(halves(band), tables[3], (1, 0))
    return dot3(tables[1], halves(wide), (1, 0))


def read_tables(refs):
    return [(refs[2 * k][...], refs[2 * k + 1][...]) for k in range(4)]


def grad_kernel(factor, subs, hidden_t, error, momentum, *refs):
    residue, band_t = refs[8:]
    tables = read_tables(refs)
    kept_t = TILE // SPAN * BAND
    for k in range(subs):
        at = slice(k * TILE, (k + 1) * TILE)
        grad = jnp.dot(hidden_t[...], error[:, at], preferred_element_type=F32)
        moved = 0.999 * momentum[0, :, at] + factor * grad
        squeezed = dot3(tables[0], halves(moved), (1, 0))
        band = dot3(halves(squeezed), tables[2], (1, 0))
        band_t[k * kept_t : (k + 1) * kept_t, :] = band.T
        residue[0, :, at] = moved - decode_tile(band, tables)


def whole(a):
    return pl.BlockSpec(a.shape, lambda i: (0,) * a.ndim)


def grad_step(hidden_t, error, momentum, tables, factor):
    units, rows = hidden_t.shape
    width = error.shape[1]
    subs = 3 if width // TILE % 3 == 0 else 1
    step = TILE * subs
    tiles = width // step
    kept = units // SPAN * BAND
    kept_t = step // SPAN * BAND
    return pl.pallas_call(
        functools.partial(grad_kernel, factor, subs),
        grid=(tiles,),
        in_specs=[
            whole(hidden_t),
            pl.BlockSpec((rows, step), lambda i: (0, i)),
            pl.BlockSpec((1, units, step), lambda i: (0, 0, i)),
        ]
        + [whole(t) for t in tables],
        out_specs=[
            pl.BlockSpec((1, units, step), lambda i: (0, 0, i)),
            pl.BlockSpec((kept_t, kept), lambda i: (i, 0)),
        ],
        out_shape=[
            jax.ShapeDtypeStruct((1, units, width), F32),
            jax.ShapeDtypeStruct((tiles * kept_t, kept), F32),
        ],
        name="grad_step",
    )(hidden_t, error, momentum, *tables)


def update_kernel(replicas, subs, bands, *refs):
    update = refs[8]
    tables = read_tables(refs)
    kept_t = TILE // SPAN * BAND
    for k in range(subs):
        band = bands[k * kept_t : (k + 1) * kept_t, :].T
        tile = decode_tile(band, tables) * (1.0 / replicas)
        update[:, k * TILE : (k + 1) * TILE] = tile.astype(BF)


def update_step(bands, tables, units, width, replicas):
    rows_t, kept = bands.shape
    subs = 3 if width // TILE % 3 == 0 else 1
    step = TILE * subs
    tiles = width // step
    return pl.pallas_call(
        functools.partial(update_kernel, replicas, subs),
        grid=(tiles,),
        in_specs=[pl.BlockSpec((rows_t // tiles, kept), lambda i: (i, 0))]
        + [whole(t) for t in tables],
        out_specs=pl.BlockSpec((units, step), lambda i: (0, i)),
        out_shape=jax.ShapeDtypeStruct((units, width), BF),
        name="update_step",
    )(bands, *tables)


def make_tables(units):
    left = block_table(units // SPAN)
    right = block_table(TILE // SPAN)
    pieces = []
    for table in (left, left.T, right.T, right):
        high = table.astype(BF)
        pieces += [high, (table - high.astype(np.float32)).astype(BF)]
    return [jnp.asarray(np.ascontiguousarray(p)) for p in pieces]


def remote(src, dst, send, recv, index, axis, peer):
    return pltpu.make_async_remote_copy(
        src_ref=src,
        dst_ref=dst,
        send_sem=send.at[index],
        recv_sem=recv.at[index],
        device_id={axis: peer},
        device_id_type=pl.DeviceIdType.MESH,
    )


def split_kernel(
    factor, replicas, tokens_hbm, target_hbm, combine, filled, gate_hbm, up_hbm, down_hbm, momentum_hbm, *refs
):
    tables_hbm, (residue_hbm, update_hbm) = refs[:8], refs[8:10]
    (
        tok, target, weight, gate, up, gate_y, up_y, down, hidden, hidden_t, lent_t,
        kept, sent, came, errors, state, bands, update,
    ) = refs[10:28]
    tables_vmem = refs[28:36]
    send, recv, local = refs[36:39]
    me, place = lax.axis_index("narrow"), lax.axis_index("wide")
    x_peer = me + 1 - 2 * (me % 2)
    y_peer = (me + 2) % 4
    twin = place + 1 - 2 * (place % 2)
    z_peer = place + 2 - 4 * (place // 2 % 2)
    quarter = place % 4
    rows, width = target.shape
    units = gate.shape[1]
    deep, flat = width // 4, units // 4
    half = deep // 2
    chunks = width // TILE
    parts = 4 * (units // TILE)

    sizes = [2] + [parts] * 4 + [chunks] * 4 + [units // TILE] + [chunks] * 4 + [chunks] * (replicas - 1)
    starts = [sum(sizes[:k]) for k in range(len(sizes) + 1)]

    def link(kind, index, src, dst, axis, peer):
        return remote(src, dst, send, recv, starts[kind] + index, axis, peer)

    def cols(c):
        if isinstance(c, int):
            return pl.ds(c * TILE, TILE)
        return pl.ds(pl.multiple_of(c * TILE, TILE), TILE)

    def token_copy(k):
        part = rows // 2
        src = tokens_hbm.at[pl.ds(k * part, part)]
        return link(0, k, src, tok.at[pl.ds(rows + k * part, part)], "narrow", x_peer)

    def piece(k, ref, owner):
        first = pl.multiple_of(owner * deep + k % 2 * half, 32)
        return ref.at[pl.ds(first, half), cols(k // 4)]

    def weight_copy(kind, k):
        mine, theirs = ((gate_hbm, gate_y), (up_hbm, up_y))[k // 2 % 2]
        if kind == 1:
            return link(1, k, piece(k, mine, quarter), piece(k, theirs, quarter), "narrow", y_peer)
        if kind == 4:
            there = piece(k, theirs, (quarter + 2) % 4)
            return link(4, k, there, there, "wide", twin)
        here = piece(k, theirs, quarter)
        return link(kind, k, here, here, "wide", z_peer if kind == 2 else twin)

    def down_piece(c, ref, first, owner):
        return ref.at[pl.ds(pl.multiple_of(first + owner * flat, 32), flat), cols(c)]

    def down_copy(kind, c):
        if kind == 5:
            src = down_piece(c, down_hbm, 0, quarter)
            return link(5, c, src, down_piece(c, down, units, quarter), "narrow", y_peer)
        if kind == 8:
            there = down_piece(c, down, units, (quarter + 2) % 4)
            return link(8, c, there, there, "wide", twin)
        here = down_piece(c, down, units, quarter)
        return link(kind, c, here, here, "wide", z_peer if kind == 6 else twin)

    def lend_copy(t):
        at = pl.ds(t * TILE, TILE)
        dst = hidden_t.at[at, pl.ds(2 * rows, 2 * rows)]
        return link(9, t, lent_t.at[at], dst, "narrow", y_peer)

    def sum_copy(c):
        return link(10, c, sent.at[:, cols(c)], came.at[:, cols(c)], "narrow", x_peer)

    def slot(k, c):
        return errors.at[pl.ds(k * rows, rows), cols(c)]

    def error_x(c):
        return link(11, c, slot(0, c), slot(1, c), "narrow", x_peer)

    def error_y(c):
        return link(12, c, slot(0, c), slot(2, c), "narrow", y_peer)

    def relay_by_y(c):
        return link(13, c, slot(1, c), slot(3, c), "narrow", y_peer)

    def relay_by_x(c):
        return link(13, c, slot(2, c), slot(3, c), "narrow", x_peer)

    kept_t = TILE // SPAN * BAND

    def band_rows(c):
        return pl.ds(pl.multiple_of(c * kept_t, kept_t), kept_t)

    def band_copy(k, c):
        mine = bands.at[place, band_rows(c)]
        return link(14 + k, c, mine, mine, "wide", others[k])

    def load(k, src, dst):
        return pltpu.make_async_copy(src, dst, local.at[k])

    barrier = pltpu.get_barrier_semaphore()
    others = [(place + k) % replicas for k in range(1, replicas)]
    for axis, peer in [("narrow", x_peer), ("narrow", y_peer)] + [("wide", p) for p in others]:
        pl.semaphore_signal(
            barrier, inc=1, device_id={axis: peer}, device_id_type=pl.DeviceIdType.MESH
        )
    loads = [
        load(0, tokens_hbm, tok.at[pl.ds(0, rows)]),
        load(1, gate_hbm, gate),
        load(2, up_hbm, up),
        load(3, down_hbm, down.at[pl.ds(0, units)]),
        load(4, target_hbm, target),
        load(5, momentum_hbm.at[0], state),
    ]
    loads += [load(6 + k, s, d) for k, (s, d) in enumerate(zip(tables_hbm, tables_vmem))]
    for copy in loads:
        copy.start()
    pl.semaphore_wait(barrier, 1 + replicas)
    for k in range(2):
        token_copy(k).start()
    for k in range(parts):
        weight_copy(1, k).start()

    @pl.loop(0, chunks)
    def _(c):
        down_copy(5, c).start()

    row_ids = me * rows + lax.broadcasted_iota(jnp.int32, combine.shape, 1)
    live = jnp.where(row_ids < filled[0], combine[...].astype(F32), 0.0)
    weight[...] = jnp.broadcast_to(live, (weight.shape[1], rows)).T

    def expert(first, count, gates, ups, base, turned, t):
        block = tok[first : first + count, :]
        gated = jnp.dot(block, gates[:, cols(t)], preferred_element_type=F32)
        raised = jnp.dot(block, ups[:, cols(t)], preferred_element_type=F32)
        value = gated / (1.0 + jnp.exp(-gated)) * raised
        hidden[first : first + count, base + t * TILE : base + (t + 1) * TILE] = value.astype(BF)
        turned[t * TILE : (t + 1) * TILE, first : first + count] = value.T.astype(BF)

    def pass_weight(k):
        weight_copy(1, k).wait_recv()
        weight_copy(2, k).start()
        weight_copy(3, k).start()

    def share_weight(k):
        weight_copy(2, k).wait_recv()
        weight_copy(4, k).start()

    def take_weights(first, count):
        for k in range(first, first + count):
            weight_copy(3, k).wait_recv()
            weight_copy(4, k).wait_recv()

    def pass_down(c):
        down_copy(5, c).wait_recv()
        down_copy(6, c).start()
        down_copy(7, c).start()

    def share_down(c):
        down_copy(6, c).wait_recv()
        down_copy(8, c).start()

    def take_down(c):
        down_copy(7, c).wait_recv()
        down_copy(8, c).wait_recv()

    def partial(c):
        part = jnp.dot(hidden[...], down[:, cols(c)], preferred_element_type=F32)
        kept[:, cols(c)] = part[:rows]
        sent[:, cols(c)] = part[rows:].astype(BF)
        sum_copy(c).start()

    def error(c):
        sum_copy(c).wait_recv()
        total = kept[:, cols(c)] + came[:, cols(c)].astype(F32)
        scale = jnp.concatenate([weight[...]] * (TILE // weight.shape[1]), axis=1)
        value = scale * (scale * total - target[:, cols(c)].astype(F32))
        errors[pl.ds(0, rows), cols(c)] = value.astype(BF)
        error_x(c).start()
        error_y(c).start()

    def relay(c):
        @pl.when(c % 3 != 2)
        def _():
            error_x(c).wait_recv()
            relay_by_y(c).start()

        @pl.when(c % 3 == 2)
        def _():
            error_y(c).wait_recv()
            relay_by_x(c).start()

    tables = lambda: [(tables_vmem[2 * k][...], tables_vmem[2 * k + 1][...]) for k in range(4)]

    def store(c):
        return pltpu.make_async_copy(
            state.at[:, cols(c)], residue_hbm.at[0, :, cols(c)], local.at[14 + c]
        )

    def store_update(c):
        return pltpu.make_async_copy(
            update.at[:, cols(c)], update_hbm.at[:, cols(c)], local.at[14 + chunks + c]
        )

    def gradient(c):
        @pl.when(c % 3 != 2)
        def _():
            error_y(c).wait_recv()

        @pl.when(c % 3 == 2)
        def _():
            error_x(c).wait_recv()

        relay_by_y(c).wait_recv()
        grad = jnp.dot(hidden_t[...], errors[:, cols(c)], preferred_element_type=F32)
        moved = 0.999 * state[:, cols(c)] + factor * grad
        table = tables()
        squeezed = dot3(table[0], halves(moved), (1, 0))
        band = dot3(halves(squeezed), table[2], (1, 0))
        bands[place, band_rows(c), :] = band.T.astype(BF)
        for k in range(replicas - 1):
            band_copy(k, c).start()
        state[:, cols(c)] = moved - decode_tile(band, table)
        store(c).start()

    def shared(c):
        for k in range(replicas - 1):
            band_copy(k, c).wait_recv()
        total = bands[0, band_rows(c), :].astype(F32)
        for k in range(1, replicas):
            total = total + bands[k, band_rows(c), :].astype(F32)
        tile = decode_tile(total.T, tables()) * (1.0 / replicas)
        update[:, cols(c)] = tile.astype(BF)
        store_update(c).start()

    for k in range(3):
        loads[k].wait()
    for t in range(units // TILE):
        expert(0, rows, gate, up, 0, hidden_t, t)
    pass_weight(0)
    for k in range(1, 6):
        pass_weight(k)
        if k < 5:
            share_weight(k - 1)
    take_weights(0, 4)
    expert(0, rows, gate_y, up_y, units, lent_t, 0)
    share_weight(4)
    pass_weight(6)
    share_weight(5)
    pass_weight(7)
    for k in range(2):
        token_copy(k).wait_recv()
    for t in range(units // TILE):
        expert(rows, rows, gate, up, 0, hidden_t, t)
    share_weight(6)
    expert(rows, rows, gate_y, up_y, units, lent_t, 0)
    lend_copy(0).start()
    share_weight(7)
    for c in range(3):
        pass_down(c)
    share_down(0)
    take_weights(4, 4)
    expert(0, 2 * rows, gate_y, up_y, units, lent_t, 1)
    lend_copy(1).start()
    for copy in loads[3:]:
        copy.wait()
    share_down(1)
    take_down(0)
    pass_down(3)
    partial(0)
    share_down(2)
    take_down(1)
    pass_down(4)
    partial(1)

    lag = 3

    @pl.loop(0, chunks + lag + 1)
    def _(c):
        @pl.when(c < chunks)
        def _():
            error(c)

        @pl.when((c >= 1) & (c <= chunks))
        def _():
            relay(c - 1)

        @pl.when(c + 5 < chunks)
        def _():
            pass_down(c + 5)

        @pl.when(c + 3 < chunks)
        def _():
            share_down(c + 3)

        @pl.when(c + 2 < chunks)
        def _():
            take_down(c + 2)
            partial(c + 2)

        @pl.when(c == 0)
        def _():
            for t in range(units // TILE):
                lend_copy(t).wait_recv()

        @pl.when((c >= lag) & (c < chunks + lag))
        def _():
            gradient(c - lag)

        @pl.when(c > lag)
        def _():
            shared(c - lag - 1)

    for k in range(2):
        token_copy(k).wait_send()
    for k in range(parts):
        for kind in range(1, 5):
            weight_copy(kind, k).wait_send()
    for t in range(units // TILE):
        lend_copy(t).wait_send()

    @pl.loop(0, chunks)
    def _(c):
        for kind in range(5, 9):
            down_copy(kind, c).wait_send()
        sum_copy(c).wait_send()
        error_x(c).wait_send()
        error_y(c).wait_send()
        relay_by_y(c).wait_send()
        for k in range(replicas - 1):
            band_copy(k, c).wait_send()
        store(c).wait()
        store_update(c).wait()


def split_step(tokens, target, combine, filled, w_gate, w_up, w_down, momentum, tables, factor, replicas):
    rows, width = tokens.shape
    units = w_down.shape[0]
    vmem = pl.BlockSpec(memory_space=pltpu.VMEM)
    hbm = pl.BlockSpec(memory_space=pl.ANY)
    block = lambda *shape: pltpu.VMEM(shape, BF)
    chunks = width // TILE
    tiles = units // TILE
    count = 2 + 16 * tiles + 8 * chunks + tiles + (replicas - 1) * chunks
    return pl.pallas_call(
        functools.partial(split_kernel, factor, replicas),
        in_specs=[hbm, hbm, vmem, pl.BlockSpec(memory_space=pltpu.SMEM)] + [hbm] * 12,
        out_specs=[hbm, hbm],
        out_shape=[
            jax.ShapeDtypeStruct((1, units, width), F32),
            jax.ShapeDtypeStruct((units, width), BF),
        ],
        scratch_shapes=[
            block(2 * rows, width), block(rows, width), pltpu.VMEM((rows, 128), F32),
            block(width, units), block(width, units), block(width, units), block(width, units),
            block(2 * units, width), block(2 * rows, 2 * units), block(units, 4 * rows),
            block(units, 2 * rows), pltpu.VMEM((rows, width), F32), block(rows, width),
            block(rows, width), block(4 * rows, width), pltpu.VMEM((units, width), F32),
            block(replicas, width // SPAN * BAND, units // SPAN * BAND), block(units, width),
        ]
        + [block(*t.shape) for t in tables]
        + [
            pltpu.SemaphoreType.DMA((count,)), pltpu.SemaphoreType.DMA((count,)),
            pltpu.SemaphoreType.DMA((14 + 2 * chunks,)),
        ],
        compiler_params=pltpu.CompilerParams(
            collective_id=0, has_side_effects=True, vmem_limit_bytes=60 << 20
        ),
        name="split_step",
    )(
        tokens, target, combine.reshape(1, rows), filled, w_gate, w_up, w_down, momentum, *tables
    )


def forward(tokens, target, combine, filled, w_gate, w_up, w_down):
    local_rows = tokens.shape[0]
    piece = lax.all_gather(tokens, "narrow", axis=0, tiled=True)
    gate_proj = jnp.dot(piece, w_gate, preferred_element_type=F32)
    up_proj = jnp.dot(piece, w_up, preferred_element_type=F32)
    hidden = (jax.nn.silu(gate_proj) * up_proj).astype(BF)
    summed = lax.psum_scatter(
        jnp.dot(hidden, w_down, preferred_element_type=F32).astype(BF),
        "narrow",
        scatter_dimension=0,
        tiled=True,
    ).astype(F32)
    weight = combine.astype(F32)[:, None]
    row_ids = lax.axis_index("narrow") * local_rows + jnp.arange(local_rows, dtype=jnp.int32)
    error = jnp.where(
        (row_ids < filled[0])[:, None], weight * (weight * summed - target.astype(F32)), 0.0
    ).astype(BF)
    return hidden.T, lax.all_gather(error, "narrow", axis=0, tiled=True)


def body(tokens, target, combine, filled, w_gate, w_up, w_down, momentum):
    units, width = w_down.shape
    narrow, replicas = lax.axis_size("narrow"), lax.axis_size("wide")
    total_rows = tokens.shape[0] * narrow
    tables = make_tables(units)
    factor = 1.0 / math.sqrt(total_rows)
    fits = units == 2 * TILE and width % TILE == 0 and tokens.shape[0] % 128 == 0
    if narrow == 4 and replicas % 4 == 0 and fits:
        return split_step(
            tokens, target, combine, filled, w_gate, w_up, w_down, momentum, tables, factor,
            replicas,
        )
    hidden_t, errors = forward(tokens, target, combine, filled, w_gate, w_up, w_down)
    residue, band = grad_step(hidden_t, errors, momentum, tables, factor)
    bands = lax.all_gather(band.astype(BF)[None], "wide", axis=0, tiled=True)
    total = jnp.sum(bands.astype(F32), axis=0)
    return residue, update_step(total, tables, units, width, replicas)


def solution(mesh):
    in_specs = (
        P(("wide", "narrow"), None),
        P(("wide", "narrow"), None),
        P(("wide", "narrow")),
        P("wide"),
        P(None, "narrow"),
        P(None, "narrow"),
        P("narrow", None),
        P("wide", "narrow", None),
    )
    out_specs = (P("wide", "narrow", None), P("narrow", None))
    return jax.shard_map(body, mesh=mesh, in_specs=in_specs, out_specs=out_specs, check_vma=False)
```

```python
import functools
import math

import jax
import jax.numpy as jnp
import numpy as np
from jax import lax
from jax.experimental import pallas as pl
from jax.experimental.pallas import tpu as pltpu
from jax.sharding import PartitionSpec as P

SPAN = 64
BAND = 16
TILE = 256
CUTS = 4
BF = jnp.bfloat16
F32 = jnp.float32


def block_table(blocks):
    row = np.arange(blocks * BAND)[:, None]
    col = np.arange(blocks * SPAN)[None, :]
    factor = np.where(row % BAND == 0, math.sqrt(1.0 / SPAN), math.sqrt(2.0 / SPAN))
    value = factor * np.cos(math.pi * (2.0 * (col % SPAN) + 1.0) * (row % BAND) / (2.0 * SPAN))
    return np.where(row // BAND == col // SPAN, value, 0.0).astype(np.float32)


def halves(value):
    high = value.astype(BF)
    return high, (value - high.astype(F32)).astype(BF)


def dot3(left, right, contract):
    dims = (((contract[0],), (contract[1],)), ((), ()))
    dot = functools.partial(lax.dot_general, dimension_numbers=dims, preferred_element_type=F32)
    return dot(left[0], right[0]) + (dot(left[1], right[0]) + dot(left[0], right[1]))


def decode_tile(band, tables):
    wide = dot3(halves(band), tables[3], (1, 0))
    return dot3(tables[1], halves(wide), (1, 0))


def read_tables(refs):
    return [(refs[2 * k][...], refs[2 * k + 1][...]) for k in range(4)]


def grad_kernel(factor, subs, hidden_t, error, momentum, *refs):
    residue, band_t = refs[8:]
    tables = read_tables(refs)
    kept_t = TILE // SPAN * BAND
    for k in range(subs):
        at = slice(k * TILE, (k + 1) * TILE)
        grad = jnp.dot(hidden_t[...], error[:, at], preferred_element_type=F32)
        moved = 0.999 * momentum[0, :, at] + factor * grad
        squeezed = dot3(tables[0], halves(moved), (1, 0))
        band = dot3(halves(squeezed), tables[2], (1, 0))
        band_t[k * kept_t : (k + 1) * kept_t, :] = band.T
        residue[0, :, at] = moved - decode_tile(band, tables)


def whole(a):
    return pl.BlockSpec(a.shape, lambda i: (0,) * a.ndim)


def grad_step(hidden_t, error, momentum, tables, factor):
    units, rows = hidden_t.shape
    width = error.shape[1]
    subs = 3 if width // TILE % 3 == 0 else 1
    step = TILE * subs
    tiles = width // step
    kept = units // SPAN * BAND
    kept_t = step // SPAN * BAND
    return pl.pallas_call(
        functools.partial(grad_kernel, factor, subs),
        grid=(tiles,),
        in_specs=[
            whole(hidden_t),
            pl.BlockSpec((rows, step), lambda i: (0, i)),
            pl.BlockSpec((1, units, step), lambda i: (0, 0, i)),
        ]
        + [whole(t) for t in tables],
        out_specs=[
            pl.BlockSpec((1, units, step), lambda i: (0, 0, i)),
            pl.BlockSpec((kept_t, kept), lambda i: (i, 0)),
        ],
        out_shape=[
            jax.ShapeDtypeStruct((1, units, width), F32),
            jax.ShapeDtypeStruct((tiles * kept_t, kept), F32),
        ],
        name="grad_step",
    )(hidden_t, error, momentum, *tables)


def update_kernel(replicas, subs, bands, *refs):
    update = refs[8]
    tables = read_tables(refs)
    kept_t = TILE // SPAN * BAND
    for k in range(subs):
        band = bands[k * kept_t : (k + 1) * kept_t, :].T
        tile = decode_tile(band, tables) * (1.0 / replicas)
        update[:, k * TILE : (k + 1) * TILE] = tile.astype(BF)


def update_step(bands, tables, units, width, replicas):
    rows_t, kept = bands.shape
    subs = 3 if width // TILE % 3 == 0 else 1
    step = TILE * subs
    tiles = width // step
    return pl.pallas_call(
        functools.partial(update_kernel, replicas, subs),
        grid=(tiles,),
        in_specs=[pl.BlockSpec((rows_t // tiles, kept), lambda i: (i, 0))]
        + [whole(t) for t in tables],
        out_specs=pl.BlockSpec((units, step), lambda i: (0, i)),
        out_shape=jax.ShapeDtypeStruct((units, width), BF),
        name="update_step",
    )(bands, *tables)


def make_tables(units):
    left = block_table(units // SPAN)
    right = block_table(TILE // SPAN)
    pieces = []
    for table in (left, left.T, right.T, right):
        high = table.astype(BF)
        pieces += [high, (table - high.astype(np.float32)).astype(BF)]
    return [jnp.asarray(np.ascontiguousarray(p)) for p in pieces]


def remote(src, dst, send, recv, index, axis, peer):
    return pltpu.make_async_remote_copy(
        src_ref=src,
        dst_ref=dst,
        send_sem=send.at[index],
        recv_sem=recv.at[index],
        device_id={axis: peer},
        device_id_type=pl.DeviceIdType.MESH,
    )


def split_kernel(
    factor, replicas, tokens_hbm, target_hbm, combine_hbm, filled, gate_hbm, up_hbm, down_hbm,
    momentum_hbm, *refs
):
    tables_hbm, (residue_hbm, update_hbm) = refs[:8], refs[8:10]
    (
        tok, target, combine, combine_x, weight, gate, up, gate_y, up_y, down, hidden, hidden_t,
        kept, sent, came, lent, given, state, bands, update,
    ) = refs[10:30]
    tables_vmem = refs[30:38]
    send, recv, local = refs[38:41]
    me, place = lax.axis_index("narrow"), lax.axis_index("wide")
    x_peer = me + 1 - 2 * (me % 2)
    y_peer = (me + 2) % 4
    twin = place + 1 - 2 * (place % 2)
    z_peer = place + 2 - 4 * (place // 2 % 2)
    others = [(place + k) % replicas for k in range(1, replicas)]
    quarter = place % 4
    rows, width = target.shape
    units = gate.shape[1]
    deep, flat = width // 4, units // 4
    cut = deep // CUTS
    chunks = width // TILE
    tiles = units // TILE
    parts = 2 * CUTS * tiles

    sizes = [2, 1] + [parts] * 4 + [chunks] * (7 + replicas - 1)
    starts = [sum(sizes[:k]) for k in range(len(sizes) + 1)]

    def link(kind, index, src, dst, axis, peer):
        return remote(src, dst, send, recv, starts[kind] + index, axis, peer)

    def cols(c):
        if isinstance(c, int):
            return pl.ds(c * TILE, TILE)
        return pl.ds(pl.multiple_of(c * TILE, TILE), TILE)

    def token_copy(k):
        part = rows // 2
        src = tokens_hbm.at[pl.ds(k * part, part)]
        return link(0, k, src, tok.at[pl.ds(rows + k * part, part)], "narrow", x_peer)

    def combine_copy():
        return link(1, 0, combine_hbm, combine_x, "narrow", x_peer)

    def piece(k, ref, owner):
        first = pl.multiple_of(owner * deep + k % CUTS * cut, 16)
        return ref.at[pl.ds(first, cut), cols(k // (2 * CUTS))]

    def weight_copy(kind, k):
        mine, theirs = ((gate_hbm, gate_y), (up_hbm, up_y))[k // CUTS % 2]
        if kind == 2:
            return link(2, k, piece(k, mine, quarter), piece(k, theirs, quarter), "narrow", y_peer)
        if kind == 5:
            there = piece(k, theirs, (quarter + 2) % 4)
            return link(5, k, there, there, "wide", twin)
        here = piece(k, theirs, quarter)
        return link(kind, k, here, here, "wide", z_peer if kind == 3 else twin)

    def down_piece(c, ref, first, owner):
        return ref.at[pl.ds(pl.multiple_of(first + owner * flat, 16), flat), cols(c)]

    def down_copy(kind, c):
        if kind == 6:
            src = down_piece(c, down_hbm, 0, quarter)
            return link(6, c, src, down_piece(c, down, units, quarter), "narrow", y_peer)
        if kind == 9:
            there = down_piece(c, down, units, (quarter + 2) % 4)
            return link(9, c, there, there, "wide", twin)
        here = down_piece(c, down, units, quarter)
        return link(kind, c, here, here, "wide", z_peer if kind == 7 else twin)

    def half_copy(k, c):
        src, dst = sent.at[pl.ds(k * rows, rows), cols(c)], came.at[pl.ds(k * rows, rows), cols(c)]
        return link(10 + k, c, src, dst, "narrow", x_peer)

    def grad_copy(c):
        return link(12, c, lent.at[:, cols(c)], given.at[:, cols(c)], "narrow", y_peer)

    kept_t = TILE // SPAN * BAND

    def band_rows(c):
        return pl.ds(pl.multiple_of(c * kept_t, kept_t), kept_t)

    def band_copy(k, c):
        mine = bands.at[place, band_rows(c)]
        return link(13 + k, c, mine, mine, "wide", others[k])

    def load(k, src, dst):
        return pltpu.make_async_copy(src, dst, local.at[k])

    def store(c):
        return load(15 + c, state.at[:, cols(c)], residue_hbm.at[0, :, cols(c)])

    def store_update(c):
        return load(15 + chunks + c, update.at[:, cols(c)], update_hbm.at[:, cols(c)])

    barrier = pltpu.get_barrier_semaphore()
    for axis, peer in [("narrow", x_peer), ("narrow", y_peer)] + [("wide", p) for p in others]:
        pl.semaphore_signal(
            barrier, inc=1, device_id={axis: peer}, device_id_type=pl.DeviceIdType.MESH
        )
    loads = [
        load(0, tokens_hbm, tok.at[pl.ds(0, rows)]),
        load(1, gate_hbm, gate),
        load(2, up_hbm, up),
        load(3, combine_hbm, combine),
        load(4, down_hbm, down.at[pl.ds(0, units)]),
        load(5, target_hbm, target),
        load(6, momentum_hbm.at[0], state),
    ]
    loads += [load(7 + k, s, d) for k, (s, d) in enumerate(zip(tables_hbm, tables_vmem))]
    for copy in loads:
        copy.start()
    pl.semaphore_wait(barrier, 1 + replicas)
    combine_copy().start()
    for k in range(2):
        token_copy(k).start()
    for k in range(parts):
        weight_copy(2, k).start()

    @pl.loop(0, chunks)
    def _(c):
        down_copy(6, c).start()

    def expert(first, count, gates, ups, base, t):
        block = tok[first : first + count, :]
        gated = jnp.dot(block, gates[:, cols(t)], preferred_element_type=F32)
        raised = jnp.dot(block, ups[:, cols(t)], preferred_element_type=F32)
        value = gated / (1.0 + jnp.exp(-gated)) * raised
        at = slice(base + t * TILE, base + (t + 1) * TILE)
        hidden[first : first + count, at] = value.astype(BF)
        hidden_t[at, first : first + count] = value.T.astype(BF)

    def pass_weight(k):
        weight_copy(2, k).wait_recv()
        weight_copy(3, k).start()
        weight_copy(4, k).start()

    def share_weight(k):
        weight_copy(3, k).wait_recv()
        weight_copy(5, k).start()

    def take_weights(first, last):
        for k in range(first, last):
            weight_copy(4, k).wait_recv()
            weight_copy(5, k).wait_recv()

    def pass_down(c):
        down_copy(6, c).wait_recv()
        down_copy(7, c).start()
        down_copy(8, c).start()

    def share_down(c):
        down_copy(7, c).wait_recv()
        down_copy(9, c).start()

    def take_down(c):
        down_copy(8, c).wait_recv()
        down_copy(9, c).wait_recv()

    def wide_weight(k):
        return jnp.concatenate([weight[k]] * (TILE // weight.shape[2]), axis=1)

    def peer_half(c):
        part = jnp.dot(hidden[rows:, :], down[:, cols(c)], preferred_element_type=F32)
        sent[rows:, cols(c)] = part.astype(BF)
        half_copy(1, c).start()
        scale = wide_weight(1)
        kept[rows:, cols(c)] = scale * (scale * part)

    def own_half(c):
        part = jnp.dot(hidden[:rows, :], down[:, cols(c)], preferred_element_type=F32)
        scale = wide_weight(0)
        value = scale * (scale * part - target[:, cols(c)].astype(F32))
        sent[:rows, cols(c)] = value.astype(BF)
        half_copy(0, c).start()
        kept[:rows, cols(c)] = value

    def lend(c):
        half_copy(1, c).wait_recv()
        scale = wide_weight(0)
        mine = kept[:rows, cols(c)] + scale * (scale * came[rows:, cols(c)].astype(F32))
        half_copy(0, c).wait_recv()
        theirs = kept[rows:, cols(c)] + came[:rows, cols(c)].astype(F32)
        error = jnp.concatenate([mine.astype(BF), theirs.astype(BF)], axis=0)
        grad = jnp.dot(hidden_t[units:, :], error, preferred_element_type=F32)
        lent[:, cols(c)] = (factor * grad).astype(BF)
        grad_copy(c).start()
        grad = jnp.dot(hidden_t[:units, :], error, preferred_element_type=F32)
        state[:, cols(c)] = 0.999 * state[:, cols(c)] + factor * grad

    tables = lambda: [(tables_vmem[2 * k][...], tables_vmem[2 * k + 1][...]) for k in range(4)]

    def gradient(c):
        grad_copy(c).wait_recv()
        moved = state[:, cols(c)] + given[:, cols(c)].astype(F32)
        table = tables()
        squeezed = dot3(table[0], halves(moved), (1, 0))
        band = dot3(halves(squeezed), table[2], (1, 0))
        bands[place, band_rows(c), :] = band.T.astype(BF)
        for k in range(replicas - 1):
            band_copy(k, c).start()
        state[:, cols(c)] = moved - decode_tile(band, table)
        store(c).start()

    def shared(c):
        for k in range(replicas - 1):
            band_copy(k, c).wait_recv()
        total = bands[0, band_rows(c), :].astype(F32)
        for k in range(1, replicas):
            total = total + bands[k, band_rows(c), :].astype(F32)
        tile = decode_tile(total.T, tables()) * (1.0 / replicas)
        update[:, cols(c)] = tile.astype(BF)
        store_update(c).start()

    for k in range(3):
        loads[k].wait()
    for t in range(tiles):
        expert(0, rows, gate, up, 0, t)
    first = parts // 2
    behind = 2
    for k in range(first + behind):
        pass_weight(k)
        if k >= behind:
            share_weight(k - behind)
    take_weights(0, first)
    expert(0, rows, gate_y, up_y, units, 0)
    for k in range(first + behind, parts - 1):
        share_weight(k - behind)
        pass_weight(k)
    share_weight(parts - 1 - behind)
    loads[3].wait()
    combine_copy().wait_recv()
    for k, (owner, ref) in enumerate(((me, combine), (x_peer, combine_x))):
        row_ids = owner * rows + lax.broadcasted_iota(jnp.int32, (1, rows), 1)
        value = ref[...].astype(F32).reshape(1, rows)
        live = jnp.where(row_ids < filled[0], value, 0.0)
        weight[k] = jnp.broadcast_to(live, (weight.shape[2], rows)).T
    for k in range(2):
        token_copy(k).wait_recv()
    expert(rows, rows, gate, up, 0, 0)
    pass_weight(parts - 1)
    share_weight(parts - behind)
    expert(rows, rows, gate, up, 0, 1)
    pass_down(0)
    expert(rows, rows, gate_y, up_y, units, 0)
    share_weight(parts - 1)
    pass_down(1)
    take_weights(first, parts)
    expert(rows, rows, gate_y, up_y, units, 1)
    for copy in loads[4:]:
        copy.wait()
    pass_down(2)
    share_down(0)
    take_down(0)
    peer_half(0)
    expert(0, rows, gate_y, up_y, units, 1)
    own_half(0)
    share_down(1)
    pass_down(3)
    take_down(1)
    peer_half(1)
    own_half(1)
    share_down(2)

    lag = 2

    @pl.loop(0, chunks + lag + 1)
    def _(c):
        @pl.when(c < chunks)
        def _():
            lend(c)

        @pl.when(c + 4 < chunks)
        def _():
            pass_down(c + 4)

        @pl.when(c + 3 < chunks)
        def _():
            share_down(c + 3)

        @pl.when(c + 2 < chunks)
        def _():
            take_down(c + 2)
            peer_half(c + 2)
            own_half(c + 2)

        @pl.when((c >= lag) & (c < chunks + lag))
        def _():
            gradient(c - lag)

        @pl.when(c > lag)
        def _():
            shared(c - lag - 1)

    combine_copy().wait_send()
    for k in range(2):
        token_copy(k).wait_send()
    for k in range(parts):
        for kind in range(2, 6):
            weight_copy(kind, k).wait_send()

    @pl.loop(0, chunks)
    def _(c):
        for kind in range(6, 10):
            down_copy(kind, c).wait_send()
        for k in range(2):
            half_copy(k, c).wait_send()
        grad_copy(c).wait_send()
        for k in range(replicas - 1):
            band_copy(k, c).wait_send()
        store(c).wait()
        store_update(c).wait()


def split_step(
    tokens, target, combine, filled, w_gate, w_up, w_down, momentum, tables, factor, replicas
):
    rows, width = tokens.shape
    units = w_down.shape[0]
    hbm = pl.BlockSpec(memory_space=pl.ANY)
    block = lambda *shape: pltpu.VMEM(shape, BF)
    chunks = width // TILE
    count = 3 + 8 * CUTS * (units // TILE) + (6 + replicas) * chunks
    return pl.pallas_call(
        functools.partial(split_kernel, factor, replicas),
        in_specs=[hbm] * 3 + [pl.BlockSpec(memory_space=pltpu.SMEM)] + [hbm] * 12,
        out_specs=[hbm, hbm],
        out_shape=[
            jax.ShapeDtypeStruct((1, units, width), F32),
            jax.ShapeDtypeStruct((units, width), BF),
        ],
        scratch_shapes=[
            block(2 * rows, width), block(rows, width), block(rows), block(rows),
            pltpu.VMEM((2, rows, 128), F32),
            block(width, units), block(width, units), block(width, units), block(width, units),
            block(2 * units, width), block(2 * rows, 2 * units), block(2 * units, 2 * rows),
            pltpu.VMEM((2 * rows, width), F32), block(2 * rows, width), block(2 * rows, width),
            block(units, width), block(units, width), pltpu.VMEM((units, width), F32),
            block(replicas, width // SPAN * BAND, units // SPAN * BAND), block(units, width),
        ]
        + [block(*t.shape) for t in tables]
        + [
            pltpu.SemaphoreType.DMA((count,)), pltpu.SemaphoreType.DMA((count,)),
            pltpu.SemaphoreType.DMA((15 + 2 * chunks,)),
        ],
        compiler_params=pltpu.CompilerParams(
            collective_id=0, has_side_effects=True, vmem_limit_bytes=60 << 20
        ),
        name="split_step",
    )(tokens, target, combine, filled, w_gate, w_up, w_down, momentum, *tables)


def forward(tokens, target, combine, filled, w_gate, w_up, w_down):
    local_rows = tokens.shape[0]
    piece = lax.all_gather(tokens, "narrow", axis=0, tiled=True)
    gate_proj = jnp.dot(piece, w_gate, preferred_element_type=F32)
    up_proj = jnp.dot(piece, w_up, preferred_element_type=F32)
    hidden = (jax.nn.silu(gate_proj) * up_proj).astype(BF)
    summed = lax.psum_scatter(
        jnp.dot(hidden, w_down, preferred_element_type=F32).astype(BF),
        "narrow",
        scatter_dimension=0,
        tiled=True,
    ).astype(F32)
    weight = combine.astype(F32)[:, None]
    row_ids = lax.axis_index("narrow") * local_rows + jnp.arange(local_rows, dtype=jnp.int32)
    error = jnp.where(
        (row_ids < filled[0])[:, None], weight * (weight * summed - target.astype(F32)), 0.0
    ).astype(BF)
    return hidden.T, lax.all_gather(error, "narrow", axis=0, tiled=True)


def body(tokens, target, combine, filled, w_gate, w_up, w_down, momentum):
    units, width = w_down.shape
    narrow, replicas = lax.axis_size("narrow"), lax.axis_size("wide")
    total_rows = tokens.shape[0] * narrow
    tables = make_tables(units)
    factor = 1.0 / math.sqrt(total_rows)
    fits = units == 2 * TILE and width % (64 * CUTS) == 0 and tokens.shape[0] % 128 == 0
    if narrow == 4 and replicas % 4 == 0 and fits:
        return split_step(
            tokens, target, combine, filled, w_gate, w_up, w_down, momentum, tables, factor,
            replicas,
        )
    hidden_t, errors = forward(tokens, target, combine, filled, w_gate, w_up, w_down)
    residue, band = grad_step(hidden_t, errors, momentum, tables, factor)
    bands = lax.all_gather(band.astype(BF)[None], "wide", axis=0, tiled=True)
    total = jnp.sum(bands.astype(F32), axis=0)
    return residue, update_step(total, tables, units, width, replicas)


def solution(mesh):
    in_specs = (
        P(("wide", "narrow"), None),
        P(("wide", "narrow"), None),
        P(("wide", "narrow")),
        P("wide"),
        P(None, "narrow"),
        P(None, "narrow"),
        P("narrow", None),
        P("wide", "narrow", None),
    )
    out_specs = (P("wide", "narrow", None), P("narrow", None))
    return jax.shard_map(body, mesh=mesh, in_specs=in_specs, out_specs=out_specs, check_vma=False)
```

```python
import functools
import math

import jax
import jax.numpy as jnp
import numpy as np
from jax import lax
from jax.experimental import pallas as pl
from jax.experimental.pallas import tpu as pltpu
from jax.sharding import PartitionSpec as P

SPAN = 64
BAND = 16
TILE = 256
CUTS = 4
BF = jnp.bfloat16
F32 = jnp.float32


def block_table(blocks):
    row = np.arange(blocks * BAND)[:, None]
    col = np.arange(blocks * SPAN)[None, :]
    factor = np.where(row % BAND == 0, math.sqrt(1.0 / SPAN), math.sqrt(2.0 / SPAN))
    value = factor * np.cos(math.pi * (2.0 * (col % SPAN) + 1.0) * (row % BAND) / (2.0 * SPAN))
    return np.where(row // BAND == col // SPAN, value, 0.0).astype(np.float32)


def halves(value):
    high = value.astype(BF)
    return high, (value - high.astype(F32)).astype(BF)


def dot3(left, right, contract):
    dims = (((contract[0],), (contract[1],)), ((), ()))
    dot = functools.partial(lax.dot_general, dimension_numbers=dims, preferred_element_type=F32)
    return dot(left[0], right[0]) + (dot(left[1], right[0]) + dot(left[0], right[1]))


def decode_tile(band, tables):
    wide = dot3(halves(band), tables[3], (1, 0))
    return dot3(tables[1], halves(wide), (1, 0))


def read_tables(refs):
    return [(refs[2 * k][...], refs[2 * k + 1][...]) for k in range(4)]


def grad_kernel(factor, subs, hidden_t, error, momentum, *refs):
    residue, band_t = refs[8:]
    tables = read_tables(refs)
    kept_t = TILE // SPAN * BAND
    for k in range(subs):
        at = slice(k * TILE, (k + 1) * TILE)
        grad = jnp.dot(hidden_t[...], error[:, at], preferred_element_type=F32)
        moved = 0.999 * momentum[0, :, at] + factor * grad
        squeezed = dot3(tables[0], halves(moved), (1, 0))
        band = dot3(halves(squeezed), tables[2], (1, 0))
        band_t[k * kept_t : (k + 1) * kept_t, :] = band.T
        residue[0, :, at] = moved - decode_tile(band, tables)


def whole(a):
    return pl.BlockSpec(a.shape, lambda i: (0,) * a.ndim)


def grad_step(hidden_t, error, momentum, tables, factor):
    units, rows = hidden_t.shape
    width = error.shape[1]
    subs = 3 if width // TILE % 3 == 0 else 1
    step = TILE * subs
    tiles = width // step
    kept = units // SPAN * BAND
    kept_t = step // SPAN * BAND
    return pl.pallas_call(
        functools.partial(grad_kernel, factor, subs),
        grid=(tiles,),
        in_specs=[
            whole(hidden_t),
            pl.BlockSpec((rows, step), lambda i: (0, i)),
            pl.BlockSpec((1, units, step), lambda i: (0, 0, i)),
        ]
        + [whole(t) for t in tables],
        out_specs=[
            pl.BlockSpec((1, units, step), lambda i: (0, 0, i)),
            pl.BlockSpec((kept_t, kept), lambda i: (i, 0)),
        ],
        out_shape=[
            jax.ShapeDtypeStruct((1, units, width), F32),
            jax.ShapeDtypeStruct((tiles * kept_t, kept), F32),
        ],
        name="grad_step",
    )(hidden_t, error, momentum, *tables)


def update_kernel(replicas, subs, bands, *refs):
    update = refs[8]
    tables = read_tables(refs)
    kept_t = TILE // SPAN * BAND
    for k in range(subs):
        band = bands[k * kept_t : (k + 1) * kept_t, :].T
        tile = decode_tile(band, tables) * (1.0 / replicas)
        update[:, k * TILE : (k + 1) * TILE] = tile.astype(BF)


def update_step(bands, tables, units, width, replicas):
    rows_t, kept = bands.shape
    subs = 3 if width // TILE % 3 == 0 else 1
    step = TILE * subs
    tiles = width // step
    return pl.pallas_call(
        functools.partial(update_kernel, replicas, subs),
        grid=(tiles,),
        in_specs=[pl.BlockSpec((rows_t // tiles, kept), lambda i: (i, 0))]
        + [whole(t) for t in tables],
        out_specs=pl.BlockSpec((units, step), lambda i: (0, i)),
        out_shape=jax.ShapeDtypeStruct((units, width), BF),
        name="update_step",
    )(bands, *tables)


def make_tables(units):
    left = block_table(units // SPAN)
    right = block_table(TILE // SPAN)
    pieces = []
    for table in (left, left.T, right.T, right):
        high = table.astype(BF)
        pieces += [high, (table - high.astype(np.float32)).astype(BF)]
    return [jnp.asarray(np.ascontiguousarray(p)) for p in pieces]


def remote(src, dst, send, recv, index, axis, peer):
    return pltpu.make_async_remote_copy(
        src_ref=src,
        dst_ref=dst,
        send_sem=send.at[index],
        recv_sem=recv.at[index],
        device_id={axis: peer},
        device_id_type=pl.DeviceIdType.MESH,
    )


def split_kernel(
    factor, replicas, tokens_hbm, target_hbm, combine_hbm, filled, gate_hbm, up_hbm, down_hbm,
    momentum_hbm, *refs
):
    tables_hbm, (state, update) = refs[:8], refs[8:10]
    (
        tok, target, combine, combine_x, weight, gate, up, gate_y, up_y, down, hidden, hidden_t,
        kept, sent, came, lent, given, bands,
    ) = refs[10:28]
    tables_vmem = refs[28:36]
    send, recv, local = refs[36:39]
    me, place = lax.axis_index("narrow"), lax.axis_index("wide")
    x_peer = me + 1 - 2 * (me % 2)
    y_peer = (me + 2) % 4
    twin = place + 1 - 2 * (place % 2)
    z_peer = place + 2 - 4 * (place // 2 % 2)
    others = [(place + k) % replicas for k in range(1, replicas)]
    quarter = place % 4
    rows, width = target.shape
    units = gate.shape[1]
    deep, flat = width // 4, units // 4
    cut = deep // CUTS
    chunks = width // TILE
    tiles = units // TILE
    parts = 2 * CUTS * tiles

    sizes = [2, 1] + [parts] * 4 + [chunks] * (7 + replicas - 1)
    starts = [sum(sizes[:k]) for k in range(len(sizes) + 1)]

    def link(kind, index, src, dst, axis, peer):
        return remote(src, dst, send, recv, starts[kind] + index, axis, peer)

    def cols(c):
        if isinstance(c, int):
            return pl.ds(c * TILE, TILE)
        return pl.ds(pl.multiple_of(c * TILE, TILE), TILE)

    def token_copy(k):
        part = rows // 2
        src = tokens_hbm.at[pl.ds(k * part, part)]
        return link(0, k, src, tok.at[pl.ds(rows + k * part, part)], "narrow", x_peer)

    def combine_copy():
        return link(1, 0, combine_hbm, combine_x, "narrow", x_peer)

    def piece(k, ref, owner):
        first = pl.multiple_of(owner * deep + k % CUTS * cut, 16)
        return ref.at[pl.ds(first, cut), cols(k // (2 * CUTS))]

    def weight_copy(kind, k):
        mine, theirs = ((gate_hbm, gate_y), (up_hbm, up_y))[k // CUTS % 2]
        if kind == 2:
            return link(2, k, piece(k, mine, quarter), piece(k, theirs, quarter), "narrow", y_peer)
        if kind == 5:
            there = piece(k, theirs, (quarter + 2) % 4)
            return link(5, k, there, there, "wide", twin)
        here = piece(k, theirs, quarter)
        return link(kind, k, here, here, "wide", z_peer if kind == 3 else twin)

    def down_piece(c, ref, first, owner):
        return ref.at[pl.ds(pl.multiple_of(first + owner * flat, 16), flat), cols(c)]

    def down_copy(kind, c):
        if kind == 6:
            src = down_piece(c, down_hbm, 0, quarter)
            return link(6, c, src, down_piece(c, down, units, quarter), "narrow", y_peer)
        if kind == 9:
            there = down_piece(c, down, units, (quarter + 2) % 4)
            return link(9, c, there, there, "wide", twin)
        here = down_piece(c, down, units, quarter)
        return link(kind, c, here, here, "wide", z_peer if kind == 7 else twin)

    def half_copy(k, c):
        src, dst = sent.at[pl.ds(k * rows, rows), cols(c)], came.at[pl.ds(k * rows, rows), cols(c)]
        return link(10 + k, c, src, dst, "narrow", x_peer)

    def grad_copy(c):
        return link(12, c, lent.at[:, cols(c)], given.at[:, cols(c)], "narrow", y_peer)

    kept_t = TILE // SPAN * BAND

    def band_rows(c):
        return pl.ds(pl.multiple_of(c * kept_t, kept_t), kept_t)

    def band_copy(k, c):
        mine = bands.at[place, band_rows(c)]
        return link(13 + k, c, mine, mine, "wide", others[k])

    def load(k, src, dst):
        return pltpu.make_async_copy(src, dst, local.at[k])

    barrier = pltpu.get_barrier_semaphore()
    for axis, peer in [("narrow", x_peer), ("narrow", y_peer)] + [("wide", p) for p in others]:
        pl.semaphore_signal(
            barrier, inc=1, device_id={axis: peer}, device_id_type=pl.DeviceIdType.MESH
        )
    loads = [
        load(0, tokens_hbm, tok.at[pl.ds(0, rows)]),
        load(1, gate_hbm, gate),
        load(2, up_hbm, up),
        load(3, combine_hbm, combine),
        load(4, down_hbm, down.at[pl.ds(0, units)]),
        load(5, target_hbm, target),
        load(6, momentum_hbm, state),
    ]
    loads += [load(7 + k, s, d) for k, (s, d) in enumerate(zip(tables_hbm, tables_vmem))]
    for copy in loads:
        copy.start()
    pl.semaphore_wait(barrier, 1 + replicas)
    combine_copy().start()
    for k in range(2):
        token_copy(k).start()
    for k in range(parts):
        weight_copy(2, k).start()

    @pl.loop(0, chunks)
    def _(c):
        down_copy(6, c).start()

    def expert(first, count, gates, ups, base, t):
        block = tok[first : first + count, :]
        gated = jnp.dot(block, gates[:, cols(t)], preferred_element_type=F32)
        raised = jnp.dot(block, ups[:, cols(t)], preferred_element_type=F32)
        value = gated / (1.0 + jnp.exp(-gated)) * raised
        at = slice(base + t * TILE, base + (t + 1) * TILE)
        hidden[first : first + count, at] = value.astype(BF)
        hidden_t[at, first : first + count] = value.T.astype(BF)

    def pass_weight(k):
        weight_copy(2, k).wait_recv()
        weight_copy(3, k).start()
        weight_copy(4, k).start()

    def share_weight(k):
        weight_copy(3, k).wait_recv()
        weight_copy(5, k).start()

    def take_weights(first, last):
        for k in range(first, last):
            weight_copy(4, k).wait_recv()
            weight_copy(5, k).wait_recv()

    def pass_down(c):
        down_copy(6, c).wait_recv()
        down_copy(7, c).start()
        down_copy(8, c).start()

    def share_down(c):
        down_copy(7, c).wait_recv()
        down_copy(9, c).start()

    def take_down(c):
        down_copy(8, c).wait_recv()
        down_copy(9, c).wait_recv()

    def wide_weight(k):
        return jnp.concatenate([weight[k]] * (TILE // weight.shape[2]), axis=1)

    def peer_half(c):
        part = jnp.dot(hidden[rows:, :], down[:, cols(c)], preferred_element_type=F32)
        sent[rows:, cols(c)] = part.astype(BF)
        half_copy(1, c).start()
        scale = wide_weight(1)
        kept[rows:, cols(c)] = scale * (scale * part)

    def own_half(c):
        part = jnp.dot(hidden[:rows, :], down[:, cols(c)], preferred_element_type=F32)
        scale = wide_weight(0)
        value = scale * (scale * part - target[:, cols(c)].astype(F32))
        sent[:rows, cols(c)] = value.astype(BF)
        half_copy(0, c).start()
        kept[:rows, cols(c)] = value

    def lend(c):
        half_copy(1, c).wait_recv()
        scale = wide_weight(0)
        mine = kept[:rows, cols(c)] + scale * (scale * came[rows:, cols(c)].astype(F32))
        half_copy(0, c).wait_recv()
        theirs = kept[rows:, cols(c)] + came[:rows, cols(c)].astype(F32)
        error = jnp.concatenate([mine.astype(BF), theirs.astype(BF)], axis=0)
        grad = jnp.dot(hidden_t[units:, :], error, preferred_element_type=F32)
        lent[:, cols(c)] = (factor * grad).astype(BF)
        grad_copy(c).start()
        grad = jnp.dot(hidden_t[:units, :], error, preferred_element_type=F32)
        state[0, :, cols(c)] = 0.999 * state[0, :, cols(c)] + factor * grad

    tables = lambda: [(tables_vmem[2 * k][...], tables_vmem[2 * k + 1][...]) for k in range(4)]

    def gradient(c):
        grad_copy(c).wait_recv()
        moved = state[0, :, cols(c)] + given[:, cols(c)].astype(F32)
        table = tables()
        squeezed = dot3(table[0], halves(moved), (1, 0))
        band = dot3(halves(squeezed), table[2], (1, 0))
        bands[place, band_rows(c), :] = band.T.astype(BF)
        for k in range(replicas - 1):
            band_copy(k, c).start()
        state[0, :, cols(c)] = moved - decode_tile(band, table)

    def shared(c):
        for k in range(replicas - 1):
            band_copy(k, c).wait_recv()
        total = bands[0, band_rows(c), :].astype(F32)
        for k in range(1, replicas):
            total = total + bands[k, band_rows(c), :].astype(F32)
        tile = decode_tile(total.T, tables()) * (1.0 / replicas)
        update[:, cols(c)] = tile.astype(BF)
        for k in range(replicas - 1):
            band_copy(k, c).wait_send()

    for k in range(3):
        loads[k].wait()
    for t in range(tiles):
        expert(0, rows, gate, up, 0, t)
    first = parts // 2
    behind = 3
    for k in range(first + behind):
        pass_weight(k)
        if k >= behind:
            share_weight(k - behind)
    take_weights(0, first)
    expert(0, rows, gate_y, up_y, units, 0)
    for k in range(first + behind, parts - 1):
        share_weight(k - behind)
        pass_weight(k)
    share_weight(parts - 1 - behind)
    loads[3].wait()
    combine_copy().wait_recv()
    for k, (owner, ref) in enumerate(((me, combine), (x_peer, combine_x))):
        row_ids = owner * rows + lax.broadcasted_iota(jnp.int32, (1, rows), 1)
        value = ref[...].astype(F32).reshape(1, rows)
        live = jnp.where(row_ids < filled[0], value, 0.0)
        weight[k] = jnp.broadcast_to(live, (weight.shape[2], rows)).T
    for k in range(2):
        token_copy(k).wait_recv()
    expert(rows, rows, gate, up, 0, 0)
    pass_weight(parts - 1)
    share_weight(parts - 3)
    share_weight(parts - 2)
    expert(rows, rows, gate, up, 0, 1)
    pass_down(0)
    expert(rows, rows, gate_y, up_y, units, 0)
    share_weight(parts - 1)
    pass_down(1)
    take_weights(first, parts)
    expert(rows, rows, gate_y, up_y, units, 1)
    for copy in loads[4:]:
        copy.wait()
    pass_down(2)
    share_down(0)
    take_down(0)
    peer_half(0)
    expert(0, rows, gate_y, up_y, units, 1)
    own_half(0)
    share_down(1)
    pass_down(3)
    take_down(1)
    peer_half(1)
    own_half(1)
    share_down(2)

    combine_copy().wait_send()
    for k in range(2):
        token_copy(k).wait_send()
    for k in range(parts):
        for kind in range(2, 6):
            weight_copy(kind, k).wait_send()

    lag, rest = 1, 2

    @pl.loop(0, chunks + lag + rest)
    def _(c):
        @pl.when((c >= 2) & (c < chunks + 2))
        def _():
            for kind in range(6, 10):
                down_copy(kind, c - 2).wait_send()
            for k in range(2):
                half_copy(k, c - 2).wait_send()
            grad_copy(c - 2).wait_send()

        @pl.when(c < chunks)
        def _():
            lend(c)

        @pl.when(c + 4 < chunks)
        def _():
            pass_down(c + 4)

        @pl.when(c + 3 < chunks)
        def _():
            share_down(c + 3)

        @pl.when(c + 2 < chunks)
        def _():
            take_down(c + 2)
            peer_half(c + 2)
            own_half(c + 2)

        @pl.when((c >= lag) & (c < chunks + lag))
        def _():
            gradient(c - lag)

        @pl.when(c >= lag + rest)
        def _():
            shared(c - lag - rest)


def split_step(
    tokens, target, combine, filled, w_gate, w_up, w_down, momentum, tables, factor, replicas
):
    rows, width = tokens.shape
    units = w_down.shape[0]
    hbm = pl.BlockSpec(memory_space=pl.ANY)
    block = lambda *shape: pltpu.VMEM(shape, BF)
    chunks = width // TILE
    count = 3 + 8 * CUTS * (units // TILE) + (6 + replicas) * chunks
    return pl.pallas_call(
        functools.partial(split_kernel, factor, replicas),
        in_specs=[hbm] * 3 + [pl.BlockSpec(memory_space=pltpu.SMEM)] + [hbm] * 12,
        out_specs=[pl.BlockSpec(memory_space=pltpu.VMEM)] * 2,
        out_shape=[pltpu.VMEM((1, units, width), F32), block(units, width)],
        scratch_shapes=[
            block(2 * rows, width), block(rows, width), block(rows), block(rows),
            pltpu.VMEM((2, rows, 128), F32),
            block(width, units), block(width, units), block(width, units), block(width, units),
            block(2 * units, width), block(2 * rows, 2 * units), block(2 * units, 2 * rows),
            pltpu.VMEM((2 * rows, width), F32), block(2 * rows, width), block(2 * rows, width),
            block(units, width), block(units, width),
            block(replicas, width // SPAN * BAND, units // SPAN * BAND),
        ]
        + [block(*t.shape) for t in tables]
        + [
            pltpu.SemaphoreType.DMA((count,)), pltpu.SemaphoreType.DMA((count,)),
            pltpu.SemaphoreType.DMA((15,)),
        ],
        compiler_params=pltpu.CompilerParams(
            collective_id=0, has_side_effects=True, vmem_limit_bytes=48 << 20
        ),
        name="split_step",
    )(tokens, target, combine, filled, w_gate, w_up, w_down, momentum, *tables)


def forward(tokens, target, combine, filled, w_gate, w_up, w_down):
    local_rows = tokens.shape[0]
    piece = lax.all_gather(tokens, "narrow", axis=0, tiled=True)
    gate_proj = jnp.dot(piece, w_gate, preferred_element_type=F32)
    up_proj = jnp.dot(piece, w_up, preferred_element_type=F32)
    hidden = (jax.nn.silu(gate_proj) * up_proj).astype(BF)
    summed = lax.psum_scatter(
        jnp.dot(hidden, w_down, preferred_element_type=F32).astype(BF),
        "narrow",
        scatter_dimension=0,
        tiled=True,
    ).astype(F32)
    weight = combine.astype(F32)[:, None]
    row_ids = lax.axis_index("narrow") * local_rows + jnp.arange(local_rows, dtype=jnp.int32)
    error = jnp.where(
        (row_ids < filled[0])[:, None], weight * (weight * summed - target.astype(F32)), 0.0
    ).astype(BF)
    return hidden.T, lax.all_gather(error, "narrow", axis=0, tiled=True)


def body(tokens, target, combine, filled, w_gate, w_up, w_down, momentum):
    units, width = w_down.shape
    narrow, replicas = lax.axis_size("narrow"), lax.axis_size("wide")
    total_rows = tokens.shape[0] * narrow
    tables = make_tables(units)
    factor = 1.0 / math.sqrt(total_rows)
    fits = units == 2 * TILE and width % (64 * CUTS) == 0 and tokens.shape[0] % 128 == 0
    if narrow == 4 and replicas % 4 == 0 and fits:
        return split_step(
            tokens, target, combine, filled, w_gate, w_up, w_down, momentum, tables, factor,
            replicas,
        )
    hidden_t, errors = forward(tokens, target, combine, filled, w_gate, w_up, w_down)
    residue, band = grad_step(hidden_t, errors, momentum, tables, factor)
    bands = lax.all_gather(band.astype(BF)[None], "wide", axis=0, tiled=True)
    total = jnp.sum(bands.astype(F32), axis=0)
    return residue, update_step(total, tables, units, width, replicas)


def solution(mesh):
    in_specs = (
        P(("wide", "narrow"), None),
        P(("wide", "narrow"), None),
        P(("wide", "narrow")),
        P("wide"),
        P(None, "narrow"),
        P(None, "narrow"),
        P("narrow", None),
        P("wide", "narrow", None),
    )
    out_specs = (P("wide", "narrow", None), P("narrow", None))
    return jax.shard_map(body, mesh=mesh, in_specs=in_specs, out_specs=out_specs, check_vma=False)
```

```python
import functools
import math

import jax
import jax.numpy as jnp
import numpy as np
from jax import lax
from jax.experimental import pallas as pl
from jax.experimental.pallas import tpu as pltpu
from jax.sharding import PartitionSpec as P

SPAN = 64
BAND = 16
TILE = 256
CUTS = 4
BF = jnp.bfloat16
F32 = jnp.float32


def block_table(blocks):
    row = np.arange(blocks * BAND)[:, None]
    col = np.arange(blocks * SPAN)[None, :]
    factor = np.where(row % BAND == 0, math.sqrt(1.0 / SPAN), math.sqrt(2.0 / SPAN))
    value = factor * np.cos(math.pi * (2.0 * (col % SPAN) + 1.0) * (row % BAND) / (2.0 * SPAN))
    return np.where(row // BAND == col // SPAN, value, 0.0).astype(np.float32)


def halves(value):
    high = value.astype(BF)
    return high, (value - high.astype(F32)).astype(BF)


def dot3(left, right, contract):
    dims = (((contract[0],), (contract[1],)), ((), ()))
    dot = functools.partial(lax.dot_general, dimension_numbers=dims, preferred_element_type=F32)
    return dot(left[0], right[0]) + (dot(left[1], right[0]) + dot(left[0], right[1]))


def decode_tile(band, tables):
    wide = dot3(halves(band), tables[3], (1, 0))
    return dot3(tables[1], halves(wide), (1, 0))


def read_tables(refs):
    return [(refs[2 * k][...], refs[2 * k + 1][...]) for k in range(4)]


def grad_kernel(factor, subs, hidden_t, error, momentum, *refs):
    residue, band_t = refs[8:]
    tables = read_tables(refs)
    kept_t = TILE // SPAN * BAND
    for k in range(subs):
        at = slice(k * TILE, (k + 1) * TILE)
        grad = jnp.dot(hidden_t[...], error[:, at], preferred_element_type=F32)
        moved = 0.999 * momentum[0, :, at] + factor * grad
        squeezed = dot3(tables[0], halves(moved), (1, 0))
        band = dot3(halves(squeezed), tables[2], (1, 0))
        band_t[k * kept_t : (k + 1) * kept_t, :] = band.T
        residue[0, :, at] = moved - decode_tile(band, tables)


def whole(a):
    return pl.BlockSpec(a.shape, lambda i: (0,) * a.ndim)


def grad_step(hidden_t, error, momentum, tables, factor):
    units, rows = hidden_t.shape
    width = error.shape[1]
    subs = 3 if width // TILE % 3 == 0 else 1
    step = TILE * subs
    tiles = width // step
    kept = units // SPAN * BAND
    kept_t = step // SPAN * BAND
    return pl.pallas_call(
        functools.partial(grad_kernel, factor, subs),
        grid=(tiles,),
        in_specs=[
            whole(hidden_t),
            pl.BlockSpec((rows, step), lambda i: (0, i)),
            pl.BlockSpec((1, units, step), lambda i: (0, 0, i)),
        ]
        + [whole(t) for t in tables],
        out_specs=[
            pl.BlockSpec((1, units, step), lambda i: (0, 0, i)),
            pl.BlockSpec((kept_t, kept), lambda i: (i, 0)),
        ],
        out_shape=[
            jax.ShapeDtypeStruct((1, units, width), F32),
            jax.ShapeDtypeStruct((tiles * kept_t, kept), F32),
        ],
        name="grad_step",
    )(hidden_t, error, momentum, *tables)


def update_kernel(replicas, subs, bands, *refs):
    update = refs[8]
    tables = read_tables(refs)
    kept_t = TILE // SPAN * BAND
    for k in range(subs):
        band = bands[k * kept_t : (k + 1) * kept_t, :].T
        tile = decode_tile(band, tables) * (1.0 / replicas)
        update[:, k * TILE : (k + 1) * TILE] = tile.astype(BF)


def update_step(bands, tables, units, width, replicas):
    rows_t, kept = bands.shape
    subs = 3 if width // TILE % 3 == 0 else 1
    step = TILE * subs
    tiles = width // step
    return pl.pallas_call(
        functools.partial(update_kernel, replicas, subs),
        grid=(tiles,),
        in_specs=[pl.BlockSpec((rows_t // tiles, kept), lambda i: (i, 0))]
        + [whole(t) for t in tables],
        out_specs=pl.BlockSpec((units, step), lambda i: (0, i)),
        out_shape=jax.ShapeDtypeStruct((units, width), BF),
        name="update_step",
    )(bands, *tables)


def make_tables(units):
    left = block_table(units // SPAN)
    right = block_table(TILE // SPAN)
    pieces = []
    for table in (left, left.T, right.T, right):
        high = table.astype(BF)
        pieces += [high, (table - high.astype(np.float32)).astype(BF)]
    return [jnp.asarray(np.ascontiguousarray(p)) for p in pieces]


def remote(src, dst, send, recv, axis, peer):
    return pltpu.make_async_remote_copy(
        src_ref=src,
        dst_ref=dst,
        send_sem=send,
        recv_sem=recv,
        device_id={axis: peer},
        device_id_type=pl.DeviceIdType.MESH,
    )


def split_kernel(
    factor, replicas, tokens_hbm, target_hbm, combine_hbm, filled, gate_hbm, up_hbm, down_hbm,
    momentum_hbm, *refs
):
    tables_hbm, (state, update) = refs[:8], refs[8:10]
    (
        tok, target, combine, combine_x, weight, gate, up, gate_y, up_y, down, hidden, hidden_t,
        kept, sent, came, lent, given, bands,
    ) = refs[10:28]
    tables_vmem = refs[28:36]
    send, recv, local = refs[36:39]
    me, place = lax.axis_index("narrow"), lax.axis_index("wide")
    x_peer = me + 1 - 2 * (me % 2)
    y_peer = (me + 2) % 4
    twin = place + 1 - 2 * (place % 2)
    z_peer = place + 2 - 4 * (place // 2 % 2)
    others = [(place + k) % replicas for k in range(1, replicas)]
    quarter = place % 4
    rows, width = target.shape
    units = gate.shape[1]
    deep, flat = width // 4, units // 4
    cut = deep // CUTS
    chunks = width // TILE
    tiles = units // TILE
    parts = 2 * CUTS * tiles

    sizes = [1, 1, parts, parts, 2] + [chunks] * 6
    starts = [sum(sizes[:k]) for k in range(len(sizes))]

    def link(kind, group, index, src, dst, axis, peer):
        return remote(src, dst, send.at[kind], recv.at[starts[group] + index], axis, peer)

    def sent_all(kind, ref):
        link(kind, 0, 0, ref, ref, "narrow", x_peer).wait_send()

    def cols(c):
        if isinstance(c, int):
            return pl.ds(c * TILE, TILE)
        return pl.ds(pl.multiple_of(c * TILE, TILE), TILE)

    def token_copy():
        return link(0, 0, 0, tokens_hbm, tok.at[pl.ds(rows, rows)], "narrow", x_peer)

    def combine_copy():
        return link(1, 1, 0, combine_hbm, combine_x, "narrow", x_peer)

    def piece(k, ref, owner):
        first = pl.multiple_of(owner * deep + k % CUTS * cut, 16)
        return ref.at[pl.ds(first, cut), cols(k // (2 * CUTS))]

    def weight_copy(kind, k):
        mine, theirs = ((gate_hbm, gate_y), (up_hbm, up_y))[k // CUTS % 2]
        if kind == 2:
            there = piece(k, theirs, quarter)
            return link(2, 2, k, piece(k, mine, quarter), there, "narrow", y_peer)
        if kind == 5:
            there = piece(k, theirs, (quarter + 2) % 4)
            return link(5, 4, k // (parts // 2), there, there, "wide", twin)
        here = piece(k, theirs, quarter)
        if kind == 3:
            return link(3, 3, k, here, here, "wide", z_peer)
        return link(4, 4, k // (parts // 2), here, here, "wide", twin)

    def down_piece(c, ref, first, owner):
        return ref.at[pl.ds(pl.multiple_of(first + owner * flat, 16), flat), cols(c)]

    def down_copy(kind, c):
        if kind == 6:
            src = down_piece(c, down_hbm, 0, quarter)
            return link(6, 5, c, src, down_piece(c, down, units, quarter), "narrow", y_peer)
        if kind == 9:
            there = down_piece(c, down, units, (quarter + 2) % 4)
            return link(9, 7, c, there, there, "wide", twin)
        here = down_piece(c, down, units, quarter)
        if kind == 7:
            return link(7, 6, c, here, here, "wide", z_peer)
        return link(8, 7, c, here, here, "wide", twin)

    def half_copy(k, c):
        src, dst = sent.at[pl.ds(k * rows, rows), cols(c)], came.at[pl.ds(k * rows, rows), cols(c)]
        return link(10, 8, c, src, dst, "narrow", x_peer)

    def halves_copy(c):
        return link(10, 8, c, sent.at[:, cols(c)], came.at[:, cols(c)], "narrow", x_peer)

    def grad_copy(c):
        return link(11, 9, c, lent.at[:, cols(c)], given.at[:, cols(c)], "narrow", y_peer)

    kept_t = TILE // SPAN * BAND

    def band_rows(c):
        return pl.ds(pl.multiple_of(c * kept_t, kept_t), kept_t)

    def band_copy(k, c):
        mine = bands.at[place, band_rows(c)]
        return link(12, 10, c, mine, mine, "wide", others[k])

    def bands_copy(c):
        there = bands.at[pl.ds(0, replicas - 1), band_rows(c)]
        return link(12, 10, c, there, there, "wide", others[0])

    def load(k, src, dst):
        return pltpu.make_async_copy(src, dst, local.at[k])

    barrier = pltpu.get_barrier_semaphore()
    for axis, peer in [("narrow", x_peer), ("narrow", y_peer)] + [("wide", p) for p in others]:
        pl.semaphore_signal(
            barrier, inc=1, device_id={axis: peer}, device_id_type=pl.DeviceIdType.MESH
        )
    loads = [
        load(0, tokens_hbm, tok.at[pl.ds(0, rows)]),
        load(1, gate_hbm, gate),
        load(2, up_hbm, up),
        load(3, combine_hbm, combine),
        load(4, down_hbm, down.at[pl.ds(0, units)]),
        load(5, target_hbm, target),
        load(6, momentum_hbm, state),
    ]
    loads += [load(7 + k, s, d) for k, (s, d) in enumerate(zip(tables_hbm, tables_vmem))]
    for copy in loads:
        copy.start()
    pl.semaphore_wait(barrier, 1 + replicas)
    combine_copy().start()
    token_copy().start()
    for k in range(parts):
        weight_copy(2, k).start()

    @pl.loop(0, chunks)
    def _(c):
        down_copy(6, c).start()

    def expert(first, count, gates, ups, base, t):
        block = tok[first : first + count, :]
        gated = jnp.dot(block, gates[:, cols(t)], preferred_element_type=F32)
        raised = jnp.dot(block, ups[:, cols(t)], preferred_element_type=F32)
        value = gated / (1.0 + jnp.exp(-gated)) * raised
        at = slice(base + t * TILE, base + (t + 1) * TILE)
        hidden[first : first + count, at] = value.astype(BF)
        hidden_t[at, first : first + count] = value.T.astype(BF)

    def pass_weight(k):
        weight_copy(2, k).wait_recv()
        weight_copy(3, k).start()
        weight_copy(4, k).start()

    def share_weight(k):
        weight_copy(3, k).wait_recv()
        weight_copy(5, k).start()

    all_pieces = gate_y.at[pl.ds(0, 2 * deep)]

    def take_weights(k):
        link(4, 4, k, all_pieces, all_pieces, "wide", twin).wait_recv()

    def pass_down(c):
        down_copy(6, c).wait_recv()
        down_copy(7, c).start()
        down_copy(8, c).start()

    def share_down(c):
        down_copy(7, c).wait_recv()
        down_copy(9, c).start()

    def take_down(c):
        both = down.at[pl.ds(units, 2 * flat), cols(c)]
        link(8, 7, c, both, both, "wide", twin).wait_recv()

    def wide_weight(k):
        return jnp.concatenate([weight[k]] * (TILE // weight.shape[2]), axis=1)

    def peer_half(c):
        part = jnp.dot(hidden[rows:, :], down[:, cols(c)], preferred_element_type=F32)
        sent[rows:, cols(c)] = part.astype(BF)
        half_copy(1, c).start()
        scale = wide_weight(1)
        kept[rows:, cols(c)] = scale * (scale * part)

    def own_half(c):
        part = jnp.dot(hidden[:rows, :], down[:, cols(c)], preferred_element_type=F32)
        scale = wide_weight(0)
        value = scale * (scale * part - target[:, cols(c)].astype(F32))
        sent[:rows, cols(c)] = value.astype(BF)
        half_copy(0, c).start()
        kept[:rows, cols(c)] = value

    def lend(c):
        halves_copy(c).wait_recv()
        scale = wide_weight(0)
        mine = kept[:rows, cols(c)] + scale * (scale * came[rows:, cols(c)].astype(F32))
        theirs = kept[rows:, cols(c)] + came[:rows, cols(c)].astype(F32)
        error = jnp.concatenate([mine.astype(BF), theirs.astype(BF)], axis=0)
        grad = jnp.dot(hidden_t[units:, :], error, preferred_element_type=F32)
        lent[:, cols(c)] = (factor * grad).astype(BF)
        grad_copy(c).start()
        grad = jnp.dot(hidden_t[:units, :], error, preferred_element_type=F32)
        state[0, :, cols(c)] = 0.999 * state[0, :, cols(c)] + factor * grad

    tables = lambda: [(tables_vmem[2 * k][...], tables_vmem[2 * k + 1][...]) for k in range(4)]

    def gradient(c):
        grad_copy(c).wait_recv()
        moved = state[0, :, cols(c)] + given[:, cols(c)].astype(F32)
        table = tables()
        squeezed = dot3(table[0], halves(moved), (1, 0))
        band = dot3(halves(squeezed), table[2], (1, 0))
        bands[place, band_rows(c), :] = band.T.astype(BF)
        for k in range(replicas - 1):
            band_copy(k, c).start()
        state[0, :, cols(c)] = moved - decode_tile(band, table)

    def shared(c):
        bands_copy(c).wait_recv()
        total = bands[0, band_rows(c), :].astype(F32)
        for k in range(1, replicas):
            total = total + bands[k, band_rows(c), :].astype(F32)
        tile = decode_tile(total.T, tables()) * (1.0 / replicas)
        update[:, cols(c)] = tile.astype(BF)

    for k in range(3):
        loads[k].wait()
    for t in range(tiles):
        expert(0, rows, gate, up, 0, t)
    first = parts // 2
    behind = 3
    for k in range(first + behind):
        pass_weight(k)
        if k >= behind:
            share_weight(k - behind)
    take_weights(0)
    expert(0, rows, gate_y, up_y, units, 0)
    for k in range(first + behind, parts - 1):
        share_weight(k - behind)
        pass_weight(k)
    share_weight(parts - 1 - behind)
    loads[3].wait()
    combine_copy().wait_recv()
    for k, (owner, ref) in enumerate(((me, combine), (x_peer, combine_x))):
        row_ids = owner * rows + lax.broadcasted_iota(jnp.int32, (1, rows), 1)
        value = ref[...].astype(F32).reshape(1, rows)
        live = jnp.where(row_ids < filled[0], value, 0.0)
        weight[k] = jnp.broadcast_to(live, (weight.shape[2], rows)).T
    token_copy().wait_recv()
    expert(rows, rows, gate, up, 0, 0)
    pass_weight(parts - 1)
    share_weight(parts - 3)
    share_weight(parts - 2)
    pass_down(0)
    expert(rows, rows, gate, up, 0, 1)
    pass_down(1)
    share_weight(parts - 1)
    expert(rows, rows, gate_y, up_y, units, 0)
    take_weights(1)
    expert(rows, rows, gate_y, up_y, units, 1)
    for copy in loads[4:]:
        copy.wait()
    pass_down(2)
    share_down(0)
    take_down(0)
    peer_half(0)
    expert(0, rows, gate_y, up_y, units, 1)
    own_half(0)
    share_down(1)
    pass_down(3)
    take_down(1)
    peer_half(1)
    own_half(1)
    share_down(2)

    combine_copy().wait_send()
    token_copy().wait_send()
    for kind in range(2, 6):
        sent_all(kind, all_pieces)

    lag, rest = 1, 2

    @pl.loop(0, chunks + lag + rest)
    def _(c):
        @pl.when(c < chunks)
        def _():
            lend(c)

        @pl.when(c + 4 < chunks)
        def _():
            pass_down(c + 4)

        @pl.when(c + 3 < chunks)
        def _():
            share_down(c + 3)

        @pl.when(c + 2 < chunks)
        def _():
            take_down(c + 2)
            peer_half(c + 2)
            own_half(c + 2)

        @pl.when((c >= lag) & (c < chunks + lag))
        def _():
            gradient(c - lag)

        @pl.when(c >= lag + rest)
        def _():
            shared(c - lag - rest)

    for kind in range(6, 10):
        sent_all(kind, down.at[pl.ds(0, flat)])
    sent_all(10, sent)
    sent_all(11, lent)
    sent_all(12, bands.at[pl.ds(0, replicas - 1)])


def split_step(
    tokens, target, combine, filled, w_gate, w_up, w_down, momentum, tables, factor, replicas
):
    rows, width = tokens.shape
    units = w_down.shape[0]
    hbm = pl.BlockSpec(memory_space=pl.ANY)
    block = lambda *shape: pltpu.VMEM(shape, BF)
    chunks = width // TILE
    count = 4 + 4 * CUTS * (units // TILE) + 6 * chunks
    return pl.pallas_call(
        functools.partial(split_kernel, factor, replicas),
        in_specs=[hbm] * 3 + [pl.BlockSpec(memory_space=pltpu.SMEM)] + [hbm] * 12,
        out_specs=[pl.BlockSpec(memory_space=pltpu.VMEM)] * 2,
        out_shape=[pltpu.VMEM((1, units, width), F32), block(units, width)],
        scratch_shapes=[
            block(2 * rows, width), block(rows, width), block(rows), block(rows),
            pltpu.VMEM((2, rows, 128), F32),
            block(width, units), block(width, units), block(width, units), block(width, units),
            block(2 * units, width), block(2 * rows, 2 * units), block(2 * units, 2 * rows),
            pltpu.VMEM((2 * rows, width), F32), block(2 * rows, width), block(2 * rows, width),
            block(units, width), block(units, width),
            block(replicas, width // SPAN * BAND, units // SPAN * BAND),
        ]
        + [block(*t.shape) for t in tables]
        + [
            pltpu.SemaphoreType.DMA((13,)), pltpu.SemaphoreType.DMA((count,)),
            pltpu.SemaphoreType.DMA((15,)),
        ],
        compiler_params=pltpu.CompilerParams(
            collective_id=0, has_side_effects=True, vmem_limit_bytes=48 << 20
        ),
        name="split_step",
    )(tokens, target, combine, filled, w_gate, w_up, w_down, momentum, *tables)


def forward(tokens, target, combine, filled, w_gate, w_up, w_down):
    local_rows = tokens.shape[0]
    piece = lax.all_gather(tokens, "narrow", axis=0, tiled=True)
    gate_proj = jnp.dot(piece, w_gate, preferred_element_type=F32)
    up_proj = jnp.dot(piece, w_up, preferred_element_type=F32)
    hidden = (jax.nn.silu(gate_proj) * up_proj).astype(BF)
    summed = lax.psum_scatter(
        jnp.dot(hidden, w_down, preferred_element_type=F32).astype(BF),
        "narrow",
        scatter_dimension=0,
        tiled=True,
    ).astype(F32)
    weight = combine.astype(F32)[:, None]
    row_ids = lax.axis_index("narrow") * local_rows + jnp.arange(local_rows, dtype=jnp.int32)
    error = jnp.where(
        (row_ids < filled[0])[:, None], weight * (weight * summed - target.astype(F32)), 0.0
    ).astype(BF)
    return hidden.T, lax.all_gather(error, "narrow", axis=0, tiled=True)


def body(tokens, target, combine, filled, w_gate, w_up, w_down, momentum):
    units, width = w_down.shape
    narrow, replicas = lax.axis_size("narrow"), lax.axis_size("wide")
    total_rows = tokens.shape[0] * narrow
    tables = make_tables(units)
    factor = 1.0 / math.sqrt(total_rows)
    fits = units == 2 * TILE and width % (64 * CUTS) == 0 and tokens.shape[0] % 128 == 0
    if narrow == 4 and replicas % 4 == 0 and fits:
        return split_step(
            tokens, target, combine, filled, w_gate, w_up, w_down, momentum, tables, factor,
            replicas,
        )
    hidden_t, errors = forward(tokens, target, combine, filled, w_gate, w_up, w_down)
    residue, band = grad_step(hidden_t, errors, momentum, tables, factor)
    bands = lax.all_gather(band.astype(BF)[None], "wide", axis=0, tiled=True)
    total = jnp.sum(bands.astype(F32), axis=0)
    return residue, update_step(total, tables, units, width, replicas)


def solution(mesh):
    in_specs = (
        P(("wide", "narrow"), None),
        P(("wide", "narrow"), None),
        P(("wide", "narrow")),
        P("wide"),
        P(None, "narrow"),
        P(None, "narrow"),
        P("narrow", None),
        P("wide", "narrow", None),
    )
    out_specs = (P("wide", "narrow", None), P("narrow", None))
    return jax.shard_map(body, mesh=mesh, in_specs=in_specs, out_specs=out_specs, check_vma=False)
```

```python
import functools
import math

import jax
import jax.numpy as jnp
import numpy as np
from jax import lax
from jax.experimental import pallas as pl
from jax.experimental.pallas import tpu as pltpu
from jax.sharding import PartitionSpec as P

SPAN = 64
BAND = 16
TILE = 256
CUTS = 4
BF = jnp.bfloat16
F32 = jnp.float32


def block_table(blocks):
    row = np.arange(blocks * BAND)[:, None]
    col = np.arange(blocks * SPAN)[None, :]
    factor = np.where(row % BAND == 0, math.sqrt(1.0 / SPAN), math.sqrt(2.0 / SPAN))
    value = factor * np.cos(math.pi * (2.0 * (col % SPAN) + 1.0) * (row % BAND) / (2.0 * SPAN))
    return np.where(row // BAND == col // SPAN, value, 0.0).astype(np.float32)


def halves(value):
    high = value.astype(BF)
    return high, (value - high.astype(F32)).astype(BF)


def dot3(left, right, contract):
    dims = (((contract[0],), (contract[1],)), ((), ()))
    dot = functools.partial(lax.dot_general, dimension_numbers=dims, preferred_element_type=F32)
    return dot(left[0], right[0]) + (dot(left[1], right[0]) + dot(left[0], right[1]))


def decode_tile(band, tables):
    wide = dot3(halves(band), tables[3], (1, 0))
    return dot3(tables[1], halves(wide), (1, 0))


def read_tables(refs):
    return [(refs[2 * k][...], refs[2 * k + 1][...]) for k in range(4)]


def grad_kernel(factor, subs, hidden_t, error, momentum, *refs):
    residue, band_t = refs[8:]
    tables = read_tables(refs)
    kept_t = TILE // SPAN * BAND
    for k in range(subs):
        at = slice(k * TILE, (k + 1) * TILE)
        grad = jnp.dot(hidden_t[...], error[:, at], preferred_element_type=F32)
        moved = 0.999 * momentum[0, :, at] + factor * grad
        squeezed = dot3(tables[0], halves(moved), (1, 0))
        band = dot3(halves(squeezed), tables[2], (1, 0))
        band_t[k * kept_t : (k + 1) * kept_t, :] = band.T
        residue[0, :, at] = moved - decode_tile(band, tables)


def whole(a):
    return pl.BlockSpec(a.shape, lambda i: (0,) * a.ndim)


def grad_step(hidden_t, error, momentum, tables, factor):
    units, rows = hidden_t.shape
    width = error.shape[1]
    subs = 3 if width // TILE % 3 == 0 else 1
    step = TILE * subs
    tiles = width // step
    kept = units // SPAN * BAND
    kept_t = step // SPAN * BAND
    return pl.pallas_call(
        functools.partial(grad_kernel, factor, subs),
        grid=(tiles,),
        in_specs=[
            whole(hidden_t),
            pl.BlockSpec((rows, step), lambda i: (0, i)),
            pl.BlockSpec((1, units, step), lambda i: (0, 0, i)),
        ]
        + [whole(t) for t in tables],
        out_specs=[
            pl.BlockSpec((1, units, step), lambda i: (0, 0, i)),
            pl.BlockSpec((kept_t, kept), lambda i: (i, 0)),
        ],
        out_shape=[
            jax.ShapeDtypeStruct((1, units, width), F32),
            jax.ShapeDtypeStruct((tiles * kept_t, kept), F32),
        ],
        name="grad_step",
    )(hidden_t, error, momentum, *tables)


def update_kernel(replicas, subs, bands, *refs):
    update = refs[8]
    tables = read_tables(refs)
    kept_t = TILE // SPAN * BAND
    for k in range(subs):
        band = bands[k * kept_t : (k + 1) * kept_t, :].T
        tile = decode_tile(band, tables) * (1.0 / replicas)
        update[:, k * TILE : (k + 1) * TILE] = tile.astype(BF)


def update_step(bands, tables, units, width, replicas):
    rows_t, kept = bands.shape
    subs = 3 if width // TILE % 3 == 0 else 1
    step = TILE * subs
    tiles = width // step
    return pl.pallas_call(
        functools.partial(update_kernel, replicas, subs),
        grid=(tiles,),
        in_specs=[pl.BlockSpec((rows_t // tiles, kept), lambda i: (i, 0))]
        + [whole(t) for t in tables],
        out_specs=pl.BlockSpec((units, step), lambda i: (0, i)),
        out_shape=jax.ShapeDtypeStruct((units, width), BF),
        name="update_step",
    )(bands, *tables)


def make_tables(units):
    left = block_table(units // SPAN)
    right = block_table(TILE // SPAN)
    pieces = []
    for table in (left, left.T, right.T, right):
        high = table.astype(BF)
        pieces += [high, (table - high.astype(np.float32)).astype(BF)]
    return [jnp.asarray(np.ascontiguousarray(p)) for p in pieces]


def remote(src, dst, send, recv, axis, peer):
    return pltpu.make_async_remote_copy(
        src_ref=src,
        dst_ref=dst,
        send_sem=send,
        recv_sem=recv,
        device_id={axis: peer},
        device_id_type=pl.DeviceIdType.MESH,
    )


def split_kernel(
    factor, replicas, tokens_hbm, target_hbm, combine_hbm, filled, gate_hbm, up_hbm, down_hbm,
    momentum_hbm, *refs
):
    tables_hbm, (state, update) = refs[:8], refs[8:10]
    (
        tok, target, combine, combine_x, weight, gate, up, gate_y, up_y, down, hidden, hidden_t,
        kept, sent, came, lent, given, bands,
    ) = refs[10:28]
    tables_vmem = refs[28:36]
    send, recv, local = refs[36:39]
    me, place = lax.axis_index("narrow"), lax.axis_index("wide")
    x_peer = me + 1 - 2 * (me % 2)
    y_peer = (me + 2) % 4
    twin = place + 1 - 2 * (place % 2)
    z_peer = place + 2 - 4 * (place // 2 % 2)
    others = [(place + k) % replicas for k in range(1, replicas)]
    quarter = place % 4
    rows, width = target.shape
    units = gate.shape[1]
    deep, flat = width // 4, units // 4
    cut = deep // CUTS
    chunks = width // TILE
    tiles = units // TILE
    parts = 2 * CUTS * tiles

    slim = TILE // 2
    sizes = [1, 1, parts, parts, 2] + [chunks] * 3 + [2 * chunks] + [chunks] * 2
    starts = [sum(sizes[:k]) for k in range(len(sizes))]

    def link(kind, group, index, src, dst, axis, peer):
        return remote(src, dst, send.at[kind], recv.at[starts[group] + index], axis, peer)

    def sent_all(kind, ref):
        link(kind, 0, 0, ref, ref, "narrow", x_peer).wait_send()

    def cols(c):
        if isinstance(c, int):
            return pl.ds(c * TILE, TILE)
        return pl.ds(pl.multiple_of(c * TILE, TILE), TILE)

    def token_copy():
        return link(0, 0, 0, tokens_hbm, tok.at[pl.ds(rows, rows)], "narrow", x_peer)

    def combine_copy():
        return link(1, 1, 0, combine_hbm, combine_x, "narrow", x_peer)

    def piece(k, ref, owner):
        first = pl.multiple_of(owner * deep + k % CUTS * cut, 16)
        return ref.at[pl.ds(first, cut), cols(k // (2 * CUTS))]

    def weight_copy(kind, k):
        mine, theirs = ((gate_hbm, gate_y), (up_hbm, up_y))[k // CUTS % 2]
        if kind == 2:
            there = piece(k, theirs, quarter)
            return link(2, 2, k, piece(k, mine, quarter), there, "narrow", y_peer)
        if kind == 5:
            there = piece(k, theirs, (quarter + 2) % 4)
            return link(5, 4, k // (parts // 2), there, there, "wide", twin)
        here = piece(k, theirs, quarter)
        if kind == 3:
            return link(3, 3, k, here, here, "wide", z_peer)
        return link(4, 4, k // (parts // 2), here, here, "wide", twin)

    def down_piece(c, ref, first, owner):
        return ref.at[pl.ds(pl.multiple_of(first + owner * flat, 16), flat), cols(c)]

    def down_copy(kind, c):
        if kind == 6:
            src = down_piece(c, down_hbm, 0, quarter)
            return link(6, 5, c, src, down_piece(c, down, units, quarter), "narrow", y_peer)
        if kind == 9:
            there = down_piece(c, down, units, (quarter + 2) % 4)
            return link(9, 7, c, there, there, "wide", twin)
        here = down_piece(c, down, units, quarter)
        if kind == 7:
            return link(7, 6, c, here, here, "wide", z_peer)
        return link(8, 7, c, here, here, "wide", twin)

    def slim_cols(c):
        if isinstance(c, int):
            return pl.ds(c * slim, slim)
        return pl.ds(pl.multiple_of(c * slim, slim), slim)

    def half_copy(k, c):
        part = pl.ds(k * rows, rows)
        src, dst = sent.at[part, slim_cols(c)], came.at[part, slim_cols(c)]
        return link(10, 8, c, src, dst, "narrow", x_peer)

    def halves_copy(c):
        at = slim_cols(c)
        return link(10, 8, c, sent.at[:, at], came.at[:, at], "narrow", x_peer)

    def slim_grad_copy(c):
        at = slim_cols(c)
        return link(11, 9, c // 2, lent.at[:, at], given.at[:, at], "narrow", y_peer)

    def grad_copy(c):
        return link(11, 9, c, lent.at[:, cols(c)], given.at[:, cols(c)], "narrow", y_peer)

    kept_t = TILE // SPAN * BAND

    def band_rows(c):
        return pl.ds(pl.multiple_of(c * kept_t, kept_t), kept_t)

    def band_copy(k, c):
        mine = bands.at[place, band_rows(c)]
        return link(12, 10, c, mine, mine, "wide", others[k])

    def bands_copy(c):
        there = bands.at[pl.ds(0, replicas - 1), band_rows(c)]
        return link(12, 10, c, there, there, "wide", others[0])

    def load(k, src, dst):
        return pltpu.make_async_copy(src, dst, local.at[k])

    barrier = pltpu.get_barrier_semaphore()
    for axis, peer in [("narrow", x_peer), ("narrow", y_peer)] + [("wide", p) for p in others]:
        pl.semaphore_signal(
            barrier, inc=1, device_id={axis: peer}, device_id_type=pl.DeviceIdType.MESH
        )
    loads = [
        load(0, tokens_hbm, tok.at[pl.ds(0, rows)]),
        load(1, gate_hbm, gate),
        load(2, up_hbm, up),
        load(3, combine_hbm, combine),
        load(4, down_hbm, down.at[pl.ds(0, units)]),
        load(5, target_hbm, target),
        load(6, momentum_hbm, state),
    ]
    loads += [load(7 + k, s, d) for k, (s, d) in enumerate(zip(tables_hbm, tables_vmem))]
    for copy in loads:
        copy.start()
    pl.semaphore_wait(barrier, 1 + replicas)
    combine_copy().start()
    token_copy().start()
    for k in range(parts):
        weight_copy(2, k).start()

    @pl.loop(0, chunks)
    def _(c):
        down_copy(6, c).start()

    def expert(first, count, gates, ups, base, t):
        block = tok[first : first + count, :]
        gated = jnp.dot(block, gates[:, cols(t)], preferred_element_type=F32)
        raised = jnp.dot(block, ups[:, cols(t)], preferred_element_type=F32)
        value = gated / (1.0 + jnp.exp(-gated)) * raised
        at = slice(base + t * TILE, base + (t + 1) * TILE)
        hidden[first : first + count, at] = value.astype(BF)
        hidden_t[at, first : first + count] = value.T.astype(BF)

    def pass_weight(k):
        weight_copy(2, k).wait_recv()
        weight_copy(3, k).start()
        weight_copy(4, k).start()

    def share_weight(k):
        weight_copy(3, k).wait_recv()
        weight_copy(5, k).start()

    all_pieces = gate_y.at[pl.ds(0, 2 * deep)]

    def take_weights(k):
        link(4, 4, k, all_pieces, all_pieces, "wide", twin).wait_recv()

    def pass_down(c):
        down_copy(6, c).wait_recv()
        down_copy(7, c).start()
        down_copy(8, c).start()

    def share_down(c):
        down_copy(7, c).wait_recv()
        down_copy(9, c).start()

    def take_down(c):
        both = down.at[pl.ds(units, 2 * flat), cols(c)]
        link(8, 7, c, both, both, "wide", twin).wait_recv()

    def wide_weight(k):
        return jnp.concatenate([weight[k]] * (TILE // weight.shape[2]), axis=1)

    def peer_half(c):
        part = jnp.dot(hidden[rows:, :], down[:, cols(c)], preferred_element_type=F32)
        sent[rows:, cols(c)] = part.astype(BF)
        half_copy(1, 2 * c).start()
        scale = wide_weight(1)
        kept[rows:, cols(c)] = scale * (scale * part)

    def own_half(c):
        part = jnp.dot(hidden[:rows, :], down[:, cols(c)], preferred_element_type=F32)
        scale = wide_weight(0)
        value = scale * (scale * part - target[:, cols(c)].astype(F32))
        sent[:rows, cols(c)] = value.astype(BF)
        half_copy(0, 2 * c).start()
        half_copy(1, 2 * c + 1).start()
        half_copy(0, 2 * c + 1).start()
        kept[:rows, cols(c)] = value

    def lend(c):
        at = slim_cols(c)
        halves_copy(c).wait_recv()
        scale = weight[0]
        mine = kept[:rows, at] + scale * (scale * came[rows:, at].astype(F32))
        theirs = kept[rows:, at] + came[:rows, at].astype(F32)
        error = jnp.concatenate([mine.astype(BF), theirs.astype(BF)], axis=0)
        grad = jnp.dot(hidden_t[units:, :], error, preferred_element_type=F32)
        lent[:, at] = (factor * grad).astype(BF)
        slim_grad_copy(c).start()
        grad = jnp.dot(hidden_t[:units, :], error, preferred_element_type=F32)
        state[0, :, at] = 0.999 * state[0, :, at] + factor * grad

    tables = lambda: [(tables_vmem[2 * k][...], tables_vmem[2 * k + 1][...]) for k in range(4)]

    def gradient(c):
        grad_copy(c).wait_recv()
        moved = state[0, :, cols(c)] + given[:, cols(c)].astype(F32)
        table = tables()
        squeezed = dot3(table[0], halves(moved), (1, 0))
        band = dot3(halves(squeezed), table[2], (1, 0))
        bands[place, band_rows(c), :] = band.T.astype(BF)
        for k in range(replicas - 1):
            band_copy(k, c).start()
        state[0, :, cols(c)] = moved - decode_tile(band, table)

    def shared(c):
        bands_copy(c).wait_recv()
        total = bands[0, band_rows(c), :].astype(F32)
        for k in range(1, replicas):
            total = total + bands[k, band_rows(c), :].astype(F32)
        tile = decode_tile(total.T, tables()) * (1.0 / replicas)
        update[:, cols(c)] = tile.astype(BF)

    for k in range(3):
        loads[k].wait()
    for t in range(tiles):
        expert(0, rows, gate, up, 0, t)
    first = parts // 2
    behind = 3
    for k in range(first + behind):
        pass_weight(k)
        if k >= behind:
            share_weight(k - behind)
    take_weights(0)
    expert(0, rows, gate_y, up_y, units, 0)
    for k in range(first + behind, parts - 1):
        share_weight(k - behind)
        pass_weight(k)
    share_weight(parts - 1 - behind)
    loads[3].wait()
    combine_copy().wait_recv()
    for k, (owner, ref) in enumerate(((me, combine), (x_peer, combine_x))):
        row_ids = owner * rows + lax.broadcasted_iota(jnp.int32, (1, rows), 1)
        value = ref[...].astype(F32).reshape(1, rows)
        live = jnp.where(row_ids < filled[0], value, 0.0)
        weight[k] = jnp.broadcast_to(live, (weight.shape[2], rows)).T
    token_copy().wait_recv()
    expert(rows, rows, gate, up, 0, 0)
    pass_weight(parts - 1)
    share_weight(parts - 3)
    share_weight(parts - 2)
    pass_down(0)
    expert(rows, rows, gate, up, 0, 1)
    pass_down(1)
    share_weight(parts - 1)
    expert(rows, rows, gate_y, up_y, units, 0)
    take_weights(1)
    expert(rows, rows, gate_y, up_y, units, 1)
    for copy in loads[4:]:
        copy.wait()
    pass_down(2)
    share_down(0)
    take_down(0)
    peer_half(0)
    expert(0, rows, gate_y, up_y, units, 1)
    own_half(0)
    share_down(1)
    pass_down(3)
    take_down(1)
    peer_half(1)
    own_half(1)
    share_down(2)

    combine_copy().wait_send()
    token_copy().wait_send()
    for kind in range(2, 6):
        sent_all(kind, all_pieces)

    lag, rest = 1, 2

    @pl.loop(0, chunks + lag + rest)
    def _(c):
        @pl.when(c < chunks)
        def _():
            lend(2 * c)

        @pl.when(c + 4 < chunks)
        def _():
            pass_down(c + 4)

        @pl.when(c + 3 < chunks)
        def _():
            share_down(c + 3)

        @pl.when(c + 2 < chunks)
        def _():
            take_down(c + 2)
            peer_half(c + 2)
            own_half(c + 2)

        @pl.when(c < chunks)
        def _():
            lend(2 * c + 1)

        @pl.when((c >= lag) & (c < chunks + lag))
        def _():
            gradient(c - lag)

        @pl.when(c >= lag + rest)
        def _():
            shared(c - lag - rest)

    for kind in range(6, 10):
        sent_all(kind, down.at[pl.ds(0, flat)])
    sent_all(10, sent)
    sent_all(11, lent)
    sent_all(12, bands.at[pl.ds(0, replicas - 1)])


def store_kernel(state, update, state_hbm, update_hbm, local):
    half = update.shape[0] // 2
    copies = [pltpu.make_async_copy(update, update_hbm, local.at[2])]
    for k in range(2):
        part = pl.ds(k * half, half)
        copies += [pltpu.make_async_copy(state.at[0, part], state_hbm.at[0, part], local.at[k])]
    for copy in copies:
        copy.start()
    for copy in copies:
        copy.wait()


def store_step(state, update):
    vmem, hbm = pl.BlockSpec(memory_space=pltpu.VMEM), pl.BlockSpec(memory_space=pl.ANY)
    return pl.pallas_call(
        store_kernel,
        in_specs=[vmem] * 2,
        out_specs=[hbm] * 2,
        out_shape=[jax.ShapeDtypeStruct(a.shape, a.dtype) for a in (state, update)],
        scratch_shapes=[pltpu.SemaphoreType.DMA((3,))],
        compiler_params=pltpu.CompilerParams(vmem_limit_bytes=4 << 20),
        name="store_step",
    )(state, update)


def split_step(
    tokens, target, combine, filled, w_gate, w_up, w_down, momentum, tables, factor, replicas
):
    rows, width = tokens.shape
    units = w_down.shape[0]
    hbm = pl.BlockSpec(memory_space=pl.ANY)
    block = lambda *shape: pltpu.VMEM(shape, BF)
    chunks = width // TILE
    count = 4 + 4 * CUTS * (units // TILE) + 7 * chunks
    return pl.pallas_call(
        functools.partial(split_kernel, factor, replicas),
        in_specs=[hbm] * 3 + [pl.BlockSpec(memory_space=pltpu.SMEM)] + [hbm] * 12,
        out_specs=[pl.BlockSpec(memory_space=pltpu.VMEM)] * 2,
        out_shape=[pltpu.VMEM((1, units, width), F32), block(units, width)],
        scratch_shapes=[
            block(2 * rows, width), block(rows, width), block(rows), block(rows),
            pltpu.VMEM((2, rows, 128), F32),
            block(width, units), block(width, units), block(width, units), block(width, units),
            block(2 * units, width), block(2 * rows, 2 * units), block(2 * units, 2 * rows),
            pltpu.VMEM((2 * rows, width), F32), block(2 * rows, width), block(2 * rows, width),
            block(units, width), block(units, width),
            block(replicas, width // SPAN * BAND, units // SPAN * BAND),
        ]
        + [block(*t.shape) for t in tables]
        + [
            pltpu.SemaphoreType.DMA((13,)), pltpu.SemaphoreType.DMA((count,)),
            pltpu.SemaphoreType.DMA((15,)),
        ],
        compiler_params=pltpu.CompilerParams(
            collective_id=0, has_side_effects=True, vmem_limit_bytes=48 << 20
        ),
        name="split_step",
    )(tokens, target, combine, filled, w_gate, w_up, w_down, momentum, *tables)


def forward(tokens, target, combine, filled, w_gate, w_up, w_down):
    local_rows = tokens.shape[0]
    piece = lax.all_gather(tokens, "narrow", axis=0, tiled=True)
    gate_proj = jnp.dot(piece, w_gate, preferred_element_type=F32)
    up_proj = jnp.dot(piece, w_up, preferred_element_type=F32)
    hidden = (jax.nn.silu(gate_proj) * up_proj).astype(BF)
    summed = lax.psum_scatter(
        jnp.dot(hidden, w_down, preferred_element_type=F32).astype(BF),
        "narrow",
        scatter_dimension=0,
        tiled=True,
    ).astype(F32)
    weight = combine.astype(F32)[:, None]
    row_ids = lax.axis_index("narrow") * local_rows + jnp.arange(local_rows, dtype=jnp.int32)
    error = jnp.where(
        (row_ids < filled[0])[:, None], weight * (weight * summed - target.astype(F32)), 0.0
    ).astype(BF)
    return hidden.T, lax.all_gather(error, "narrow", axis=0, tiled=True)


def body(tokens, target, combine, filled, w_gate, w_up, w_down, momentum):
    units, width = w_down.shape
    narrow, replicas = lax.axis_size("narrow"), lax.axis_size("wide")
    total_rows = tokens.shape[0] * narrow
    tables = make_tables(units)
    factor = 1.0 / math.sqrt(total_rows)
    fits = units == 2 * TILE and width % (64 * CUTS) == 0 and tokens.shape[0] % 128 == 0
    if narrow == 4 and replicas % 4 == 0 and fits:
        state, update = split_step(
            tokens, target, combine, filled, w_gate, w_up, w_down, momentum, tables, factor,
            replicas,
        )
        return store_step(state, update)
    hidden_t, errors = forward(tokens, target, combine, filled, w_gate, w_up, w_down)
    residue, band = grad_step(hidden_t, errors, momentum, tables, factor)
    bands = lax.all_gather(band.astype(BF)[None], "wide", axis=0, tiled=True)
    total = jnp.sum(bands.astype(F32), axis=0)
    return residue, update_step(total, tables, units, width, replicas)


def solution(mesh):
    in_specs = (
        P(("wide", "narrow"), None),
        P(("wide", "narrow"), None),
        P(("wide", "narrow")),
        P("wide"),
        P(None, "narrow"),
        P(None, "narrow"),
        P("narrow", None),
        P("wide", "narrow", None),
    )
    out_specs = (P("wide", "narrow", None), P("narrow", None))
    return jax.shard_map(body, mesh=mesh, in_specs=in_specs, out_specs=out_specs, check_vma=False)
```

```python
import functools
import math

import jax
import jax.numpy as jnp
import numpy as np
from jax import lax
from jax.experimental import pallas as pl
from jax.experimental.pallas import tpu as pltpu
from jax.sharding import PartitionSpec as P

SPAN = 64
BAND = 16
TILE = 256
CUTS = 4
BF = jnp.bfloat16
F32 = jnp.float32


def block_table(blocks):
    row = np.arange(blocks * BAND)[:, None]
    col = np.arange(blocks * SPAN)[None, :]
    factor = np.where(row % BAND == 0, math.sqrt(1.0 / SPAN), math.sqrt(2.0 / SPAN))
    value = factor * np.cos(math.pi * (2.0 * (col % SPAN) + 1.0) * (row % BAND) / (2.0 * SPAN))
    return np.where(row // BAND == col // SPAN, value, 0.0).astype(np.float32)


def halves(value):
    high = value.astype(BF)
    return high, (value - high.astype(F32)).astype(BF)


def dot3(left, right, contract):
    dims = (((contract[0],), (contract[1],)), ((), ()))
    dot = functools.partial(lax.dot_general, dimension_numbers=dims, preferred_element_type=F32)
    return dot(left[0], right[0]) + (dot(left[1], right[0]) + dot(left[0], right[1]))


def decode_tile(band, tables):
    wide = dot3(halves(band), tables[3], (1, 0))
    return dot3(tables[1], halves(wide), (1, 0))


def read_tables(refs):
    return [(refs[2 * k][...], refs[2 * k + 1][...]) for k in range(4)]


def grad_kernel(factor, subs, hidden_t, error, momentum, *refs):
    residue, band_t = refs[8:]
    tables = read_tables(refs)
    kept_t = TILE // SPAN * BAND
    for k in range(subs):
        at = slice(k * TILE, (k + 1) * TILE)
        grad = jnp.dot(hidden_t[...], error[:, at], preferred_element_type=F32)
        moved = 0.999 * momentum[0, :, at] + factor * grad
        squeezed = dot3(tables[0], halves(moved), (1, 0))
        band = dot3(halves(squeezed), tables[2], (1, 0))
        band_t[k * kept_t : (k + 1) * kept_t, :] = band.T
        residue[0, :, at] = moved - decode_tile(band, tables)


def whole(a):
    return pl.BlockSpec(a.shape, lambda i: (0,) * a.ndim)


def grad_step(hidden_t, error, momentum, tables, factor):
    units, rows = hidden_t.shape
    width = error.shape[1]
    subs = 3 if width // TILE % 3 == 0 else 1
    step = TILE * subs
    tiles = width // step
    kept = units // SPAN * BAND
    kept_t = step // SPAN * BAND
    return pl.pallas_call(
        functools.partial(grad_kernel, factor, subs),
        grid=(tiles,),
        in_specs=[
            whole(hidden_t),
            pl.BlockSpec((rows, step), lambda i: (0, i)),
            pl.BlockSpec((1, units, step), lambda i: (0, 0, i)),
        ]
        + [whole(t) for t in tables],
        out_specs=[
            pl.BlockSpec((1, units, step), lambda i: (0, 0, i)),
            pl.BlockSpec((kept_t, kept), lambda i: (i, 0)),
        ],
        out_shape=[
            jax.ShapeDtypeStruct((1, units, width), F32),
            jax.ShapeDtypeStruct((tiles * kept_t, kept), F32),
        ],
        name="grad_step",
    )(hidden_t, error, momentum, *tables)


def update_kernel(replicas, subs, bands, *refs):
    update = refs[8]
    tables = read_tables(refs)
    kept_t = TILE // SPAN * BAND
    for k in range(subs):
        band = bands[k * kept_t : (k + 1) * kept_t, :].T
        tile = decode_tile(band, tables) * (1.0 / replicas)
        update[:, k * TILE : (k + 1) * TILE] = tile.astype(BF)


def update_step(bands, tables, units, width, replicas):
    rows_t, kept = bands.shape
    subs = 3 if width // TILE % 3 == 0 else 1
    step = TILE * subs
    tiles = width // step
    return pl.pallas_call(
        functools.partial(update_kernel, replicas, subs),
        grid=(tiles,),
        in_specs=[pl.BlockSpec((rows_t // tiles, kept), lambda i: (i, 0))]
        + [whole(t) for t in tables],
        out_specs=pl.BlockSpec((units, step), lambda i: (0, i)),
        out_shape=jax.ShapeDtypeStruct((units, width), BF),
        name="update_step",
    )(bands, *tables)


def make_tables(units):
    left = block_table(units // SPAN)
    right = block_table(TILE // SPAN)
    pieces = []
    for table in (left, left.T, right.T, right):
        high = table.astype(BF)
        pieces += [high, (table - high.astype(np.float32)).astype(BF)]
    return [jnp.asarray(np.ascontiguousarray(p)) for p in pieces]


def remote(src, dst, send, recv, axis, peer):
    return pltpu.make_async_remote_copy(
        src_ref=src,
        dst_ref=dst,
        send_sem=send,
        recv_sem=recv,
        device_id={axis: peer},
        device_id_type=pl.DeviceIdType.MESH,
    )


def split_kernel(
    factor, replicas, tokens_hbm, target_hbm, combine_hbm, filled, gate_hbm, up_hbm, down_hbm,
    momentum_hbm, *refs
):
    tables_hbm, (state, update) = refs[:8], refs[8:10]
    (
        tok, target, combine, combine_x, weight, gate, up, gate_y, up_y, down, hidden, hidden_t,
        kept, sent, came, lent, given, bands,
    ) = refs[10:28]
    tables_vmem = refs[28:36]
    send, recv, local = refs[36:39]
    me, place = lax.axis_index("narrow"), lax.axis_index("wide")
    x_peer = me + 1 - 2 * (me % 2)
    y_peer = (me + 2) % 4
    twin = place + 1 - 2 * (place % 2)
    z_peer = place + 2 - 4 * (place // 2 % 2)
    others = [(place + k) % replicas for k in range(1, replicas)]
    quarter = place % 4
    rows, width = target.shape
    units = gate.shape[1]
    deep, flat = width // 4, units // 4
    cut = deep // CUTS
    chunks = width // TILE
    tiles = units // TILE
    parts = 2 * CUTS * tiles

    slim = TILE // 2
    sizes = [1, 1, parts, parts, 2] + [chunks] * 3 + [2 * chunks] + [chunks] * 2
    starts = [sum(sizes[:k]) for k in range(len(sizes))]

    def link(kind, group, index, src, dst, axis, peer):
        return remote(src, dst, send.at[kind], recv.at[starts[group] + index], axis, peer)

    def sent_all(kind, ref):
        link(kind, 0, 0, ref, ref, "narrow", x_peer).wait_send()

    def cols(c):
        if isinstance(c, int):
            return pl.ds(c * TILE, TILE)
        return pl.ds(pl.multiple_of(c * TILE, TILE), TILE)

    def token_copy():
        return link(0, 0, 0, tokens_hbm, tok.at[pl.ds(rows, rows)], "narrow", x_peer)

    def combine_copy():
        return link(1, 1, 0, combine_hbm, combine_x, "narrow", x_peer)

    def piece(k, ref, owner):
        first = pl.multiple_of(owner * deep + k % CUTS * cut, 16)
        return ref.at[pl.ds(first, cut), cols(k // (2 * CUTS))]

    def weight_copy(kind, k):
        mine, theirs = ((gate_hbm, gate_y), (up_hbm, up_y))[k // CUTS % 2]
        if kind == 2:
            there = piece(k, theirs, quarter)
            return link(2, 2, k, piece(k, mine, quarter), there, "narrow", y_peer)
        if kind == 5:
            there = piece(k, theirs, (quarter + 2) % 4)
            return link(5, 4, k // (parts // 2), there, there, "wide", twin)
        here = piece(k, theirs, quarter)
        if kind == 3:
            return link(3, 3, k, here, here, "wide", z_peer)
        return link(4, 4, k // (parts // 2), here, here, "wide", twin)

    def down_piece(c, ref, first, owner):
        return ref.at[pl.ds(pl.multiple_of(first + owner * flat, 16), flat), cols(c)]

    def down_copy(kind, c):
        if kind == 6:
            src = down_piece(c, down_hbm, 0, quarter)
            return link(6, 5, c, src, down_piece(c, down, units, quarter), "narrow", y_peer)
        if kind == 9:
            there = down_piece(c, down, units, (quarter + 2) % 4)
            return link(9, 7, c, there, there, "wide", twin)
        here = down_piece(c, down, units, quarter)
        if kind == 7:
            return link(7, 6, c, here, here, "wide", z_peer)
        return link(8, 7, c, here, here, "wide", twin)

    def slim_cols(c):
        if isinstance(c, int):
            return pl.ds(c * slim, slim)
        return pl.ds(pl.multiple_of(c * slim, slim), slim)

    def half_copy(k, c):
        part = pl.ds(k * rows, rows)
        src, dst = sent.at[part, slim_cols(c)], came.at[part, slim_cols(c)]
        return link(10, 8, c, src, dst, "narrow", x_peer)

    def halves_copy(c):
        at = slim_cols(c)
        return link(10, 8, c, sent.at[:, at], came.at[:, at], "narrow", x_peer)

    def slim_grad_copy(c):
        at = slim_cols(c)
        return link(11, 9, c // 2, lent.at[:, at], given.at[:, at], "narrow", y_peer)

    def grad_copy(c):
        return link(11, 9, c, lent.at[:, cols(c)], given.at[:, cols(c)], "narrow", y_peer)

    kept_t = TILE // SPAN * BAND

    def band_rows(c):
        return pl.ds(pl.multiple_of(c * kept_t, kept_t), kept_t)

    def band_copy(k, c):
        mine = bands.at[place, band_rows(c)]
        return link(12, 10, c, mine, mine, "wide", others[k])

    def bands_copy(c):
        there = bands.at[pl.ds(0, replicas - 1), band_rows(c)]
        return link(12, 10, c, there, there, "wide", others[0])

    def load(k, src, dst):
        return pltpu.make_async_copy(src, dst, local.at[k])

    barrier = pltpu.get_barrier_semaphore()
    for axis, peer in [("narrow", x_peer), ("narrow", y_peer)] + [("wide", p) for p in others]:
        pl.semaphore_signal(
            barrier, inc=1, device_id={axis: peer}, device_id_type=pl.DeviceIdType.MESH
        )
    loads = [
        load(0, tokens_hbm, tok.at[pl.ds(0, rows)]),
        load(1, gate_hbm, gate),
        load(2, up_hbm, up),
        load(3, combine_hbm, combine),
        load(4, down_hbm, down.at[pl.ds(0, units)]),
        load(5, target_hbm, target),
        load(6, momentum_hbm, state),
    ]
    loads += [load(7 + k, s, d) for k, (s, d) in enumerate(zip(tables_hbm, tables_vmem))]
    for copy in loads:
        copy.start()
    pl.semaphore_wait(barrier, 1 + replicas)
    combine_copy().start()
    token_copy().start()
    for k in range(parts):
        weight_copy(2, k).start()

    @pl.loop(0, chunks)
    def _(c):
        down_copy(6, c).start()

    def expert(first, count, gates, ups, base, t):
        block = tok[first : first + count, :]
        gated = jnp.dot(block, gates[:, cols(t)], preferred_element_type=F32)
        raised = jnp.dot(block, ups[:, cols(t)], preferred_element_type=F32)
        value = gated / (1.0 + jnp.exp(-gated)) * raised
        at = slice(base + t * TILE, base + (t + 1) * TILE)
        hidden[first : first + count, at] = value.astype(BF)
        hidden_t[at, first : first + count] = value.T.astype(BF)

    def pass_weight(k):
        weight_copy(2, k).wait_recv()
        weight_copy(3, k).start()
        weight_copy(4, k).start()

    def share_weight(k):
        weight_copy(3, k).wait_recv()
        weight_copy(5, k).start()

    all_pieces = gate_y.at[pl.ds(0, 2 * deep)]

    def take_weights(k):
        link(4, 4, k, all_pieces, all_pieces, "wide", twin).wait_recv()

    def pass_down(c):
        down_copy(6, c).wait_recv()
        down_copy(7, c).start()
        down_copy(8, c).start()

    def share_down(c):
        down_copy(7, c).wait_recv()
        down_copy(9, c).start()

    def take_down(c):
        both = down.at[pl.ds(units, 2 * flat), cols(c)]
        link(8, 7, c, both, both, "wide", twin).wait_recv()

    def wide_weight(k):
        return jnp.concatenate([weight[k]] * (TILE // weight.shape[2]), axis=1)

    def peer_half(c):
        part = jnp.dot(hidden[rows:, :], down[:, cols(c)], preferred_element_type=F32)
        sent[rows:, cols(c)] = part.astype(BF)
        half_copy(1, 2 * c).start()
        scale = wide_weight(1)
        kept[rows:, cols(c)] = scale * (scale * part)

    def own_half(c):
        part = jnp.dot(hidden[:rows, :], down[:, cols(c)], preferred_element_type=F32)
        scale = wide_weight(0)
        value = scale * (scale * part - target[:, cols(c)].astype(F32))
        sent[:rows, cols(c)] = value.astype(BF)
        half_copy(0, 2 * c).start()
        half_copy(1, 2 * c + 1).start()
        half_copy(0, 2 * c + 1).start()
        kept[:rows, cols(c)] = value

    def lend(c):
        at = slim_cols(c)
        halves_copy(c).wait_recv()
        scale = weight[0]
        mine = kept[:rows, at] + scale * (scale * came[rows:, at].astype(F32))
        theirs = kept[rows:, at] + came[:rows, at].astype(F32)
        error = jnp.concatenate([mine.astype(BF), theirs.astype(BF)], axis=0)
        grad = jnp.dot(hidden_t[units:, :], error, preferred_element_type=F32)
        lent[:, at] = (factor * grad).astype(BF)
        slim_grad_copy(c).start()
        grad = jnp.dot(hidden_t[:units, :], error, preferred_element_type=F32)
        state[0, :, at] = 0.999 * state[0, :, at] + factor * grad

    tables = lambda: [(tables_vmem[2 * k][...], tables_vmem[2 * k + 1][...]) for k in range(4)]

    def gradient(c):
        grad_copy(c).wait_recv()
        moved = state[0, :, cols(c)] + given[:, cols(c)].astype(F32)
        table = tables()
        squeezed = dot3(table[0], halves(moved), (1, 0))
        band = dot3(halves(squeezed), table[2], (1, 0))
        bands[place, band_rows(c), :] = band.T.astype(BF)
        for k in range(replicas - 1):
            band_copy(k, c).start()
        state[0, :, cols(c)] = moved - decode_tile(band, table)

    def shared(c):
        bands_copy(c).wait_recv()
        total = bands[0, band_rows(c), :].astype(F32)
        for k in range(1, replicas):
            total = total + bands[k, band_rows(c), :].astype(F32)
        tile = decode_tile(total.T, tables()) * (1.0 / replicas)
        update[:, cols(c)] = tile.astype(BF)

    for k in range(3):
        loads[k].wait()
    for t in range(tiles):
        expert(0, rows, gate, up, 0, t)
    first = parts // 2
    behind = 3
    for k in range(first + behind):
        pass_weight(k)
        if k >= behind:
            share_weight(k - behind)
    take_weights(0)
    expert(0, rows, gate_y, up_y, units, 0)
    for k in range(first + behind, parts - 1):
        share_weight(k - behind)
        pass_weight(k)
    loads[3].wait()
    combine_copy().wait_recv()
    for k, (owner, ref) in enumerate(((me, combine), (x_peer, combine_x))):
        row_ids = owner * rows + lax.broadcasted_iota(jnp.int32, (1, rows), 1)
        value = ref[...].astype(F32).reshape(1, rows)
        live = jnp.where(row_ids < filled[0], value, 0.0)
        weight[k] = jnp.broadcast_to(live, (weight.shape[2], rows)).T
    share_weight(parts - 1 - behind)
    pass_weight(parts - 1)
    token_copy().wait_recv()
    expert(rows, rows, gate, up, 0, 0)
    share_weight(parts - 3)
    pass_down(0)
    expert(rows, rows, gate, up, 0, 1)
    share_weight(parts - 2)
    pass_down(1)
    expert(rows, rows, gate_y, up_y, units, 0)
    share_weight(parts - 1)
    pass_down(2)
    share_down(0)
    take_weights(1)
    expert(rows, rows, gate_y, up_y, units, 1)
    for copy in loads[4:]:
        copy.wait()
    take_down(0)
    peer_half(0)
    expert(0, rows, gate_y, up_y, units, 1)
    own_half(0)
    share_down(1)
    pass_down(3)
    take_down(1)
    peer_half(1)
    own_half(1)
    share_down(2)

    combine_copy().wait_send()
    token_copy().wait_send()
    for kind in range(2, 6):
        sent_all(kind, all_pieces)

    lag, rest = 1, 2

    @pl.loop(0, chunks + lag + rest)
    def _(c):
        @pl.when(c < chunks)
        def _():
            lend(2 * c)

        @pl.when(c + 4 < chunks)
        def _():
            pass_down(c + 4)

        @pl.when(c + 3 < chunks)
        def _():
            share_down(c + 3)

        @pl.when(c + 2 < chunks)
        def _():
            take_down(c + 2)
            peer_half(c + 2)
            own_half(c + 2)

        @pl.when(c < chunks)
        def _():
            lend(2 * c + 1)

        @pl.when((c >= lag) & (c < chunks + lag))
        def _():
            gradient(c - lag)

        @pl.when(c >= lag + rest)
        def _():
            shared(c - lag - rest)

    for kind in range(6, 10):
        sent_all(kind, down.at[pl.ds(0, flat)])
    sent_all(10, sent)
    sent_all(11, lent)
    sent_all(12, bands.at[pl.ds(0, replicas - 1)])


def store_kernel(state, update, state_hbm, update_hbm, local):
    half = update.shape[0] // 2
    copies = [pltpu.make_async_copy(update, update_hbm, local.at[2])]
    for k in range(2):
        part = pl.ds(k * half, half)
        copies += [pltpu.make_async_copy(state.at[0, part], state_hbm.at[0, part], local.at[k])]
    for copy in copies:
        copy.start()
    for copy in copies:
        copy.wait()


def store_step(state, update):
    vmem, hbm = pl.BlockSpec(memory_space=pltpu.VMEM), pl.BlockSpec(memory_space=pl.ANY)
    return pl.pallas_call(
        store_kernel,
        in_specs=[vmem] * 2,
        out_specs=[hbm] * 2,
        out_shape=[jax.ShapeDtypeStruct(a.shape, a.dtype) for a in (state, update)],
        scratch_shapes=[pltpu.SemaphoreType.DMA((3,))],
        compiler_params=pltpu.CompilerParams(vmem_limit_bytes=4 << 20),
        name="store_step",
    )(state, update)


def split_step(
    tokens, target, combine, filled, w_gate, w_up, w_down, momentum, tables, factor, replicas
):
    rows, width = tokens.shape
    units = w_down.shape[0]
    hbm = pl.BlockSpec(memory_space=pl.ANY)
    block = lambda *shape: pltpu.VMEM(shape, BF)
    chunks = width // TILE
    count = 4 + 4 * CUTS * (units // TILE) + 7 * chunks
    return pl.pallas_call(
        functools.partial(split_kernel, factor, replicas),
        in_specs=[hbm] * 3 + [pl.BlockSpec(memory_space=pltpu.SMEM)] + [hbm] * 12,
        out_specs=[pl.BlockSpec(memory_space=pltpu.VMEM)] * 2,
        out_shape=[pltpu.VMEM((1, units, width), F32), block(units, width)],
        scratch_shapes=[
            block(2 * rows, width), block(rows, width), block(rows), block(rows),
            pltpu.VMEM((2, rows, 128), F32),
            block(width, units), block(width, units), block(width, units), block(width, units),
            block(2 * units, width), block(2 * rows, 2 * units), block(2 * units, 2 * rows),
            pltpu.VMEM((2 * rows, width), F32), block(2 * rows, width), block(2 * rows, width),
            block(units, width), block(units, width),
            block(replicas, width // SPAN * BAND, units // SPAN * BAND),
        ]
        + [block(*t.shape) for t in tables]
        + [
            pltpu.SemaphoreType.DMA((13,)), pltpu.SemaphoreType.DMA((count,)),
            pltpu.SemaphoreType.DMA((15,)),
        ],
        compiler_params=pltpu.CompilerParams(
            collective_id=0, has_side_effects=True, vmem_limit_bytes=48 << 20
        ),
        name="split_step",
    )(tokens, target, combine, filled, w_gate, w_up, w_down, momentum, *tables)


def forward(tokens, target, combine, filled, w_gate, w_up, w_down):
    local_rows = tokens.shape[0]
    piece = lax.all_gather(tokens, "narrow", axis=0, tiled=True)
    gate_proj = jnp.dot(piece, w_gate, preferred_element_type=F32)
    up_proj = jnp.dot(piece, w_up, preferred_element_type=F32)
    hidden = (jax.nn.silu(gate_proj) * up_proj).astype(BF)
    summed = lax.psum_scatter(
        jnp.dot(hidden, w_down, preferred_element_type=F32).astype(BF),
        "narrow",
        scatter_dimension=0,
        tiled=True,
    ).astype(F32)
    weight = combine.astype(F32)[:, None]
    row_ids = lax.axis_index("narrow") * local_rows + jnp.arange(local_rows, dtype=jnp.int32)
    error = jnp.where(
        (row_ids < filled[0])[:, None], weight * (weight * summed - target.astype(F32)), 0.0
    ).astype(BF)
    return hidden.T, lax.all_gather(error, "narrow", axis=0, tiled=True)


def body(tokens, target, combine, filled, w_gate, w_up, w_down, momentum):
    units, width = w_down.shape
    narrow, replicas = lax.axis_size("narrow"), lax.axis_size("wide")
    total_rows = tokens.shape[0] * narrow
    tables = make_tables(units)
    factor = 1.0 / math.sqrt(total_rows)
    fits = units == 2 * TILE and width % (64 * CUTS) == 0 and tokens.shape[0] % 128 == 0
    if narrow == 4 and replicas % 4 == 0 and fits:
        state, update = split_step(
            tokens, target, combine, filled, w_gate, w_up, w_down, momentum, tables, factor,
            replicas,
        )
        return store_step(state, update)
    hidden_t, errors = forward(tokens, target, combine, filled, w_gate, w_up, w_down)
    residue, band = grad_step(hidden_t, errors, momentum, tables, factor)
    bands = lax.all_gather(band.astype(BF)[None], "wide", axis=0, tiled=True)
    total = jnp.sum(bands.astype(F32), axis=0)
    return residue, update_step(total, tables, units, width, replicas)


def solution(mesh):
    in_specs = (
        P(("wide", "narrow"), None),
        P(("wide", "narrow"), None),
        P(("wide", "narrow")),
        P("wide"),
        P(None, "narrow"),
        P(None, "narrow"),
        P("narrow", None),
        P("wide", "narrow", None),
    )
    out_specs = (P("wide", "narrow", None), P("narrow", None))
    return jax.shard_map(body, mesh=mesh, in_specs=in_specs, out_specs=out_specs, check_vma=False)
```

```python
import functools
import math

import jax
import jax.numpy as jnp
import numpy as np
from jax import lax
from jax.experimental import pallas as pl
from jax.experimental.pallas import tpu as pltpu
from jax.sharding import PartitionSpec as P

SPAN = 64
BAND = 16
TILE = 256
CUTS = 4
BF = jnp.bfloat16
F32 = jnp.float32


def block_table(blocks):
    row = np.arange(blocks * BAND)[:, None]
    col = np.arange(blocks * SPAN)[None, :]
    factor = np.where(row % BAND == 0, math.sqrt(1.0 / SPAN), math.sqrt(2.0 / SPAN))
    value = factor * np.cos(math.pi * (2.0 * (col % SPAN) + 1.0) * (row % BAND) / (2.0 * SPAN))
    return np.where(row // BAND == col // SPAN, value, 0.0).astype(np.float32)


def halves(value):
    high = value.astype(BF)
    return high, (value - high.astype(F32)).astype(BF)


def dot3(left, right, contract):
    dims = (((contract[0],), (contract[1],)), ((), ()))
    dot = functools.partial(lax.dot_general, dimension_numbers=dims, preferred_element_type=F32)
    return dot(left[0], right[0]) + (dot(left[1], right[0]) + dot(left[0], right[1]))


def decode_tile(band, tables):
    wide = dot3(halves(band), tables[3], (1, 0))
    return dot3(tables[1], halves(wide), (1, 0))


def read_tables(refs):
    return [(refs[2 * k][...], refs[2 * k + 1][...]) for k in range(4)]


def grad_kernel(factor, subs, hidden_t, error, momentum, *refs):
    residue, band_t = refs[8:]
    tables = read_tables(refs)
    kept_t = TILE // SPAN * BAND
    for k in range(subs):
        at = slice(k * TILE, (k + 1) * TILE)
        grad = jnp.dot(hidden_t[...], error[:, at], preferred_element_type=F32)
        moved = 0.999 * momentum[0, :, at] + factor * grad
        squeezed = dot3(tables[0], halves(moved), (1, 0))
        band = dot3(halves(squeezed), tables[2], (1, 0))
        band_t[k * kept_t : (k + 1) * kept_t, :] = band.T
        residue[0, :, at] = moved - decode_tile(band, tables)


def whole(a):
    return pl.BlockSpec(a.shape, lambda i: (0,) * a.ndim)


def grad_step(hidden_t, error, momentum, tables, factor):
    units, rows = hidden_t.shape
    width = error.shape[1]
    subs = 3 if width // TILE % 3 == 0 else 1
    step = TILE * subs
    tiles = width // step
    kept = units // SPAN * BAND
    kept_t = step // SPAN * BAND
    return pl.pallas_call(
        functools.partial(grad_kernel, factor, subs),
        grid=(tiles,),
        in_specs=[
            whole(hidden_t),
            pl.BlockSpec((rows, step), lambda i: (0, i)),
            pl.BlockSpec((1, units, step), lambda i: (0, 0, i)),
        ]
        + [whole(t) for t in tables],
        out_specs=[
            pl.BlockSpec((1, units, step), lambda i: (0, 0, i)),
            pl.BlockSpec((kept_t, kept), lambda i: (i, 0)),
        ],
        out_shape=[
            jax.ShapeDtypeStruct((1, units, width), F32),
            jax.ShapeDtypeStruct((tiles * kept_t, kept), F32),
        ],
        name="grad_step",
    )(hidden_t, error, momentum, *tables)


def update_kernel(replicas, subs, bands, *refs):
    update = refs[8]
    tables = read_tables(refs)
    kept_t = TILE // SPAN * BAND
    for k in range(subs):
        band = bands[k * kept_t : (k + 1) * kept_t, :].T
        tile = decode_tile(band, tables) * (1.0 / replicas)
        update[:, k * TILE : (k + 1) * TILE] = tile.astype(BF)


def update_step(bands, tables, units, width, replicas):
    rows_t, kept = bands.shape
    subs = 3 if width // TILE % 3 == 0 else 1
    step = TILE * subs
    tiles = width // step
    return pl.pallas_call(
        functools.partial(update_kernel, replicas, subs),
        grid=(tiles,),
        in_specs=[pl.BlockSpec((rows_t // tiles, kept), lambda i: (i, 0))]
        + [whole(t) for t in tables],
        out_specs=pl.BlockSpec((units, step), lambda i: (0, i)),
        out_shape=jax.ShapeDtypeStruct((units, width), BF),
        name="update_step",
    )(bands, *tables)


def make_tables(units):
    left = block_table(units // SPAN)
    right = block_table(TILE // SPAN)
    pieces = []
    for table in (left, left.T, right.T, right):
        high = table.astype(BF)
        pieces += [high, (table - high.astype(np.float32)).astype(BF)]
    return [jnp.asarray(np.ascontiguousarray(p)) for p in pieces]


def remote(src, dst, send, recv, axis, peer):
    return pltpu.make_async_remote_copy(
        src_ref=src,
        dst_ref=dst,
        send_sem=send,
        recv_sem=recv,
        device_id={axis: peer},
        device_id_type=pl.DeviceIdType.MESH,
    )


def split_kernel(
    factor, replicas, tokens_hbm, target_hbm, combine_hbm, filled, gate_hbm, up_hbm, down_hbm,
    momentum_hbm, *refs
):
    tables_hbm, (state, update) = refs[:8], refs[8:10]
    (
        tok, target, combine, combine_x, weight, gate, up, gate_y, up_y, down, hidden, hidden_t,
        kept, sent, came, lent, given, bands, early, early_x, own_band,
    ) = refs[10:31]
    tables_vmem = refs[31:39]
    send, recv, local = refs[39:42]
    me, place = lax.axis_index("narrow"), lax.axis_index("wide")
    x_peer = me + 1 - 2 * (me % 2)
    y_peer = (me + 2) % 4
    twin = place + 1 - 2 * (place % 2)
    z_peer = place + 2 - 4 * (place // 2 % 2)
    others = [(place + k) % replicas for k in range(1, replicas)]
    quarter = place % 4
    rows, width = target.shape
    units = gate.shape[1]
    deep, flat = width // 4, units // 4
    cut = deep // CUTS
    chunks = width // TILE
    tiles = units // TILE
    parts = 2 * CUTS * tiles

    slim = TILE // 2
    sizes = [1, 1, parts, parts, 2] + [chunks] * 3 + [2 * chunks] + [chunks] * 2 + [1]
    starts = [sum(sizes[:k]) for k in range(len(sizes))]

    def link(kind, group, index, src, dst, axis, peer):
        return remote(src, dst, send.at[kind], recv.at[starts[group] + index], axis, peer)

    def sent_all(kind, ref):
        link(kind, 0, 0, ref, ref, "narrow", x_peer).wait_send()

    def cols(c):
        if isinstance(c, int):
            return pl.ds(c * TILE, TILE)
        return pl.ds(pl.multiple_of(c * TILE, TILE), TILE)

    def token_copy():
        return link(0, 0, 0, tokens_hbm, tok.at[pl.ds(rows, rows)], "narrow", x_peer)

    def combine_copy():
        return link(1, 1, 0, combine_hbm, combine_x, "narrow", x_peer)

    def piece(k, ref, owner):
        first = pl.multiple_of(owner * deep + k % CUTS * cut, 16)
        return ref.at[pl.ds(first, cut), cols(k // (2 * CUTS))]

    def weight_copy(kind, k):
        mine, theirs = ((gate_hbm, gate_y), (up_hbm, up_y))[k // CUTS % 2]
        if kind == 2:
            there = piece(k, theirs, quarter)
            return link(2, 2, k, piece(k, mine, quarter), there, "narrow", y_peer)
        if kind == 5:
            there = piece(k, theirs, (quarter + 2) % 4)
            return link(5, 4, k // (parts // 2), there, there, "wide", twin)
        here = piece(k, theirs, quarter)
        if kind == 3:
            return link(3, 3, k, here, here, "wide", z_peer)
        return link(4, 4, k // (parts // 2), here, here, "wide", twin)

    def down_piece(c, ref, first, owner):
        return ref.at[pl.ds(pl.multiple_of(first + owner * flat, 16), flat), cols(c)]

    def down_copy(kind, c):
        if kind == 6:
            src = down_piece(c, down_hbm, 0, quarter)
            return link(6, 5, c, src, down_piece(c, down, units, quarter), "narrow", y_peer)
        if kind == 9:
            there = down_piece(c, down, units, (quarter + 2) % 4)
            return link(9, 7, c, there, there, "wide", twin)
        here = down_piece(c, down, units, quarter)
        if kind == 7:
            return link(7, 6, c, here, here, "wide", z_peer)
        return link(8, 7, c, here, here, "wide", twin)

    def slim_cols(c):
        if isinstance(c, int):
            return pl.ds(c * slim, slim)
        return pl.ds(pl.multiple_of(c * slim, slim), slim)

    def half_copy(k, c):
        part = pl.ds(k * rows, rows)
        src, dst = sent.at[part, slim_cols(c)], came.at[part, slim_cols(c)]
        return link(10, 8, c, src, dst, "narrow", x_peer)

    def halves_copy(c):
        at = slim_cols(c)
        return link(10, 8, c, sent.at[:, at], came.at[:, at], "narrow", x_peer)

    def slim_grad_copy(c):
        at = slim_cols(c)
        return link(11, 9, c // 2, lent.at[:, at], given.at[:, at], "narrow", y_peer)

    def grad_copy(c):
        return link(11, 9, c, lent.at[:, cols(c)], given.at[:, cols(c)], "narrow", y_peer)

    kept_t = TILE // SPAN * BAND

    def band_rows(c):
        return pl.ds(pl.multiple_of(c * kept_t, kept_t), kept_t)

    def band_copy(k, c):
        mine = bands.at[place, band_rows(c)]
        return link(12, 10, c, mine, mine, "wide", others[k])

    def bands_copy(c):
        there = bands.at[pl.ds(0, replicas - 1), band_rows(c)]
        return link(12, 10, c, there, there, "wide", others[0])

    def early_copy():
        return link(13, 11, 0, early, early_x, "narrow", y_peer)

    def load(k, src, dst):
        return pltpu.make_async_copy(src, dst, local.at[k])

    barrier = pltpu.get_barrier_semaphore()
    for axis, peer in [("narrow", x_peer), ("narrow", y_peer)] + [("wide", p) for p in others]:
        pl.semaphore_signal(
            barrier, inc=1, device_id={axis: peer}, device_id_type=pl.DeviceIdType.MESH
        )
    loads = [
        load(0, tokens_hbm, tok.at[pl.ds(0, rows)]),
        load(1, gate_hbm, gate),
        load(2, up_hbm, up),
        load(3, combine_hbm, combine),
        load(4, down_hbm, down.at[pl.ds(0, units)]),
        load(5, target_hbm, target),
        load(6, momentum_hbm, state),
    ]
    loads += [load(7 + k, s, d) for k, (s, d) in enumerate(zip(tables_hbm, tables_vmem))]
    for copy in loads:
        copy.start()
    pl.semaphore_wait(barrier, 1 + replicas)
    combine_copy().start()
    token_copy().start()
    for k in range(parts):
        weight_copy(2, k).start()

    @pl.loop(0, chunks)
    def _(c):
        down_copy(6, c).start()

    def expert(first, count, gates, ups, base, t):
        block = tok[first : first + count, :]
        gated = jnp.dot(block, gates[:, cols(t)], preferred_element_type=F32)
        raised = jnp.dot(block, ups[:, cols(t)], preferred_element_type=F32)
        value = gated / (1.0 + jnp.exp(-gated)) * raised
        at = slice(base + t * TILE, base + (t + 1) * TILE)
        hidden[first : first + count, at] = value.astype(BF)
        hidden_t[at, first : first + count] = value.T.astype(BF)

    def pass_weight(k):
        weight_copy(2, k).wait_recv()
        weight_copy(3, k).start()
        weight_copy(4, k).start()

    def share_weight(k):
        weight_copy(3, k).wait_recv()
        weight_copy(5, k).start()

    all_pieces = gate_y.at[pl.ds(0, 2 * deep)]

    def take_weights(k):
        link(4, 4, k, all_pieces, all_pieces, "wide", twin).wait_recv()

    def pass_down(c):
        down_copy(6, c).wait_recv()
        down_copy(7, c).start()
        down_copy(8, c).start()

    def share_down(c):
        down_copy(7, c).wait_recv()
        down_copy(9, c).start()

    def take_down(c):
        both = down.at[pl.ds(units, 2 * flat), cols(c)]
        link(8, 7, c, both, both, "wide", twin).wait_recv()

    def wide_weight(k):
        return jnp.concatenate([weight[k]] * (TILE // weight.shape[2]), axis=1)

    def peer_half(c):
        part = jnp.dot(hidden[rows:, :], down[:, cols(c)], preferred_element_type=F32)
        sent[rows:, cols(c)] = part.astype(BF)
        half_copy(1, 2 * c).start()
        scale = wide_weight(1)
        kept[rows:, cols(c)] = scale * (scale * part)

    def own_half(c):
        part = jnp.dot(hidden[:rows, :], down[:, cols(c)], preferred_element_type=F32)
        scale = wide_weight(0)
        value = scale * (scale * part - target[:, cols(c)].astype(F32))
        sent[:rows, cols(c)] = value.astype(BF)
        half_copy(0, 2 * c).start()
        half_copy(1, 2 * c + 1).start()
        half_copy(0, 2 * c + 1).start()
        kept[:rows, cols(c)] = value

    tables = lambda: [(tables_vmem[2 * k][...], tables_vmem[2 * k + 1][...]) for k in range(4)]

    def encode(value):
        table = tables()
        squeezed = dot3(table[0], halves(value), (1, 0))
        return dot3(halves(squeezed), table[2], (1, 0))

    last = chunks - 1

    def lend(c):
        at = slim_cols(c)
        halves_copy(c).wait_recv()
        scale = weight[0]
        mine = kept[:rows, at] + scale * (scale * came[rows:, at].astype(F32))
        theirs = kept[rows:, at] + came[:rows, at].astype(F32)
        error = jnp.concatenate([mine.astype(BF), theirs.astype(BF)], axis=0)
        grad = jnp.dot(hidden_t[units:, :], error, preferred_element_type=F32)
        lent[:, at] = (factor * grad).astype(BF)

        @pl.when(c == 2 * last + 1)
        def _():
            early[...] = encode(lent[:, cols(last)].astype(F32)).T.astype(BF)
            early_copy().start()

        slim_grad_copy(c).start()
        grad = jnp.dot(hidden_t[:units, :], error, preferred_element_type=F32)
        state[0, :, at] = 0.999 * state[0, :, at] + factor * grad

        @pl.when(c == 2 * last + 1)
        def _():
            own_band[...] = encode(state[0, :, cols(last)]).T

    def send_band(c, value):
        bands[place, band_rows(c), :] = value.astype(BF)
        for k in range(replicas - 1):
            band_copy(k, c).start()

    def gradient(c):
        grad_copy(c).wait_recv()
        moved = state[0, :, cols(c)] + given[:, cols(c)].astype(F32)
        band = encode(moved)

        @pl.when(c != last)
        def _():
            send_band(c, band.T)

        state[0, :, cols(c)] = moved - decode_tile(band, tables())

    def shared(c):
        bands_copy(c).wait_recv()
        total = bands[0, band_rows(c), :].astype(F32)
        for k in range(1, replicas):
            total = total + bands[k, band_rows(c), :].astype(F32)
        tile = decode_tile(total.T, tables()) * (1.0 / replicas)
        update[:, cols(c)] = tile.astype(BF)

    for k in range(3):
        loads[k].wait()
    for t in range(tiles):
        expert(0, rows, gate, up, 0, t)
    first = parts // 2
    behind = 3
    for k in range(first + behind):
        pass_weight(k)
        if k >= behind:
            share_weight(k - behind)
    take_weights(0)
    expert(0, rows, gate_y, up_y, units, 0)
    for k in range(first + behind, parts - 1):
        share_weight(k - behind)
        pass_weight(k)
    loads[3].wait()
    combine_copy().wait_recv()
    for k, (owner, ref) in enumerate(((me, combine), (x_peer, combine_x))):
        row_ids = owner * rows + lax.broadcasted_iota(jnp.int32, (1, rows), 1)
        value = ref[...].astype(F32).reshape(1, rows)
        live = jnp.where(row_ids < filled[0], value, 0.0)
        weight[k] = jnp.broadcast_to(live, (weight.shape[2], rows)).T
    share_weight(parts - 1 - behind)
    pass_weight(parts - 1)
    token_copy().wait_recv()
    expert(rows, rows, gate, up, 0, 0)
    share_weight(parts - 3)
    pass_down(0)
    expert(rows, rows, gate, up, 0, 1)
    share_weight(parts - 2)
    pass_down(1)
    expert(rows, rows, gate_y, up_y, units, 0)
    share_weight(parts - 1)
    pass_down(2)
    share_down(0)
    take_weights(1)
    expert(rows, rows, gate_y, up_y, units, 1)
    for copy in loads[4:]:
        copy.wait()
    take_down(0)
    peer_half(0)
    expert(0, rows, gate_y, up_y, units, 1)
    own_half(0)
    share_down(1)
    pass_down(3)
    take_down(1)
    peer_half(1)
    own_half(1)
    share_down(2)

    combine_copy().wait_send()
    token_copy().wait_send()
    for kind in range(2, 6):
        sent_all(kind, all_pieces)

    lag, rest = 1, 1

    @pl.loop(0, chunks + lag + rest)
    def _(c):
        @pl.when(c < chunks)
        def _():
            lend(2 * c)

        @pl.when(c + 4 < chunks)
        def _():
            pass_down(c + 4)

        @pl.when(c + 3 < chunks)
        def _():
            share_down(c + 3)

        @pl.when(c + 2 < chunks)
        def _():
            take_down(c + 2)
            peer_half(c + 2)
            own_half(c + 2)

        @pl.when(c == last)
        def _():
            gradient(c - lag)

        @pl.when(c < chunks)
        def _():
            lend(2 * c + 1)

        @pl.when((c >= lag) & (c < chunks + lag) & (c != last))
        def _():
            gradient(c - lag)

        @pl.when(c == last)
        def _():
            early_copy().wait_recv()
            send_band(last, own_band[...] + early_x[...].astype(F32))

        @pl.when(c >= lag + rest)
        def _():
            shared(c - lag - rest)

    for kind in range(6, 10):
        sent_all(kind, down.at[pl.ds(0, flat)])
    early_copy().wait_send()
    sent_all(10, sent)
    sent_all(11, lent)
    sent_all(12, bands.at[pl.ds(0, replicas - 1)])


def store_kernel(state, update, state_hbm, update_hbm, local):
    half = update.shape[0] // 2
    copies = [pltpu.make_async_copy(update, update_hbm, local.at[2])]
    for k in range(2):
        part = pl.ds(k * half, half)
        copies += [pltpu.make_async_copy(state.at[0, part], state_hbm.at[0, part], local.at[k])]
    for copy in copies:
        copy.start()
    for copy in copies:
        copy.wait()


def store_step(state, update):
    vmem, hbm = pl.BlockSpec(memory_space=pltpu.VMEM), pl.BlockSpec(memory_space=pl.ANY)
    return pl.pallas_call(
        store_kernel,
        in_specs=[vmem] * 2,
        out_specs=[hbm] * 2,
        out_shape=[jax.ShapeDtypeStruct(a.shape, a.dtype) for a in (state, update)],
        scratch_shapes=[pltpu.SemaphoreType.DMA((3,))],
        compiler_params=pltpu.CompilerParams(vmem_limit_bytes=4 << 20),
        name="store_step",
    )(state, update)


def split_step(
    tokens, target, combine, filled, w_gate, w_up, w_down, momentum, tables, factor, replicas
):
    rows, width = tokens.shape
    units = w_down.shape[0]
    hbm = pl.BlockSpec(memory_space=pl.ANY)
    block = lambda *shape: pltpu.VMEM(shape, BF)
    chunks = width // TILE
    count = 5 + 4 * CUTS * (units // TILE) + 7 * chunks
    band_shape = (TILE // SPAN * BAND, units // SPAN * BAND)
    return pl.pallas_call(
        functools.partial(split_kernel, factor, replicas),
        in_specs=[hbm] * 3 + [pl.BlockSpec(memory_space=pltpu.SMEM)] + [hbm] * 12,
        out_specs=[pl.BlockSpec(memory_space=pltpu.VMEM)] * 2,
        out_shape=[pltpu.VMEM((1, units, width), F32), block(units, width)],
        scratch_shapes=[
            block(2 * rows, width), block(rows, width), block(rows), block(rows),
            pltpu.VMEM((2, rows, 128), F32),
            block(width, units), block(width, units), block(width, units), block(width, units),
            block(2 * units, width), block(2 * rows, 2 * units), block(2 * units, 2 * rows),
            pltpu.VMEM((2 * rows, width), F32), block(2 * rows, width), block(2 * rows, width),
            block(units, width), block(units, width),
            block(replicas, width // SPAN * BAND, units // SPAN * BAND),
            block(*band_shape), block(*band_shape), pltpu.VMEM(band_shape, F32),
        ]
        + [block(*t.shape) for t in tables]
        + [
            pltpu.SemaphoreType.DMA((14,)), pltpu.SemaphoreType.DMA((count,)),
            pltpu.SemaphoreType.DMA((15,)),
        ],
        compiler_params=pltpu.CompilerParams(
            collective_id=0, has_side_effects=True, vmem_limit_bytes=48 << 20
        ),
        name="split_step",
    )(tokens, target, combine, filled, w_gate, w_up, w_down, momentum, *tables)


def forward(tokens, target, combine, filled, w_gate, w_up, w_down):
    local_rows = tokens.shape[0]
    piece = lax.all_gather(tokens, "narrow", axis=0, tiled=True)
    gate_proj = jnp.dot(piece, w_gate, preferred_element_type=F32)
    up_proj = jnp.dot(piece, w_up, preferred_element_type=F32)
    hidden = (jax.nn.silu(gate_proj) * up_proj).astype(BF)
    summed = lax.psum_scatter(
        jnp.dot(hidden, w_down, preferred_element_type=F32).astype(BF),
        "narrow",
        scatter_dimension=0,
        tiled=True,
    ).astype(F32)
    weight = combine.astype(F32)[:, None]
    row_ids = lax.axis_index("narrow") * local_rows + jnp.arange(local_rows, dtype=jnp.int32)
    error = jnp.where(
        (row_ids < filled[0])[:, None], weight * (weight * summed - target.astype(F32)), 0.0
    ).astype(BF)
    return hidden.T, lax.all_gather(error, "narrow", axis=0, tiled=True)


def body(tokens, target, combine, filled, w_gate, w_up, w_down, momentum):
    units, width = w_down.shape
    narrow, replicas = lax.axis_size("narrow"), lax.axis_size("wide")
    total_rows = tokens.shape[0] * narrow
    tables = make_tables(units)
    factor = 1.0 / math.sqrt(total_rows)
    fits = units == 2 * TILE and width % (64 * CUTS) == 0 and tokens.shape[0] % 128 == 0
    if narrow == 4 and replicas % 4 == 0 and fits:
        state, update = split_step(
            tokens, target, combine, filled, w_gate, w_up, w_down, momentum, tables, factor,
            replicas,
        )
        return store_step(state, update)
    hidden_t, errors = forward(tokens, target, combine, filled, w_gate, w_up, w_down)
    residue, band = grad_step(hidden_t, errors, momentum, tables, factor)
    bands = lax.all_gather(band.astype(BF)[None], "wide", axis=0, tiled=True)
    total = jnp.sum(bands.astype(F32), axis=0)
    return residue, update_step(total, tables, units, width, replicas)


def solution(mesh):
    in_specs = (
        P(("wide", "narrow"), None),
        P(("wide", "narrow"), None),
        P(("wide", "narrow")),
        P("wide"),
        P(None, "narrow"),
        P(None, "narrow"),
        P("narrow", None),
        P("wide", "narrow", None),
    )
    out_specs = (P("wide", "narrow", None), P("narrow", None))
    return jax.shard_map(body, mesh=mesh, in_specs=in_specs, out_specs=out_specs, check_vma=False)
```

```python
import functools
import math

import jax
import jax.numpy as jnp
import numpy as np
from jax import lax
from jax.experimental import pallas as pl
from jax.experimental.pallas import tpu as pltpu
from jax.sharding import PartitionSpec as P

SPAN = 64
BAND = 16
TILE = 256
CUTS = 4
BF = jnp.bfloat16
F32 = jnp.float32


def block_table(blocks):
    row = np.arange(blocks * BAND)[:, None]
    col = np.arange(blocks * SPAN)[None, :]
    factor = np.where(row % BAND == 0, math.sqrt(1.0 / SPAN), math.sqrt(2.0 / SPAN))
    value = factor * np.cos(math.pi * (2.0 * (col % SPAN) + 1.0) * (row % BAND) / (2.0 * SPAN))
    return np.where(row // BAND == col // SPAN, value, 0.0).astype(np.float32)


def halves(value):
    high = value.astype(BF)
    return high, (value - high.astype(F32)).astype(BF)


def dot3(left, right, contract):
    dims = (((contract[0],), (contract[1],)), ((), ()))
    dot = functools.partial(lax.dot_general, dimension_numbers=dims, preferred_element_type=F32)
    return dot(left[0], right[0]) + (dot(left[1], right[0]) + dot(left[0], right[1]))


def decode_tile(band, tables):
    wide = dot3(halves(band), tables[3], (1, 0))
    return dot3(tables[1], halves(wide), (1, 0))


def read_tables(refs):
    return [(refs[2 * k][...], refs[2 * k + 1][...]) for k in range(4)]


def grad_kernel(factor, subs, hidden_t, error, momentum, *refs):
    residue, band_t = refs[8:]
    tables = read_tables(refs)
    kept_t = TILE // SPAN * BAND
    for k in range(subs):
        at = slice(k * TILE, (k + 1) * TILE)
        grad = jnp.dot(hidden_t[...], error[:, at], preferred_element_type=F32)
        moved = 0.999 * momentum[0, :, at] + factor * grad
        squeezed = dot3(tables[0], halves(moved), (1, 0))
        band = dot3(halves(squeezed), tables[2], (1, 0))
        band_t[k * kept_t : (k + 1) * kept_t, :] = band.T
        residue[0, :, at] = moved - decode_tile(band, tables)


def whole(a):
    return pl.BlockSpec(a.shape, lambda i: (0,) * a.ndim)


def grad_step(hidden_t, error, momentum, tables, factor):
    units, rows = hidden_t.shape
    width = error.shape[1]
    subs = 3 if width // TILE % 3 == 0 else 1
    step = TILE * subs
    tiles = width // step
    kept = units // SPAN * BAND
    kept_t = step // SPAN * BAND
    return pl.pallas_call(
        functools.partial(grad_kernel, factor, subs),
        grid=(tiles,),
        in_specs=[
            whole(hidden_t),
            pl.BlockSpec((rows, step), lambda i: (0, i)),
            pl.BlockSpec((1, units, step), lambda i: (0, 0, i)),
        ]
        + [whole(t) for t in tables],
        out_specs=[
            pl.BlockSpec((1, units, step), lambda i: (0, 0, i)),
            pl.BlockSpec((kept_t, kept), lambda i: (i, 0)),
        ],
        out_shape=[
            jax.ShapeDtypeStruct((1, units, width), F32),
            jax.ShapeDtypeStruct((tiles * kept_t, kept), F32),
        ],
        name="grad_step",
    )(hidden_t, error, momentum, *tables)


def update_kernel(replicas, subs, bands, *refs):
    update = refs[8]
    tables = read_tables(refs)
    kept_t = TILE // SPAN * BAND
    for k in range(subs):
        band = bands[k * kept_t : (k + 1) * kept_t, :].T
        tile = decode_tile(band, tables) * (1.0 / replicas)
        update[:, k * TILE : (k + 1) * TILE] = tile.astype(BF)


def update_step(bands, tables, units, width, replicas):
    rows_t, kept = bands.shape
    subs = 3 if width // TILE % 3 == 0 else 1
    step = TILE * subs
    tiles = width // step
    return pl.pallas_call(
        functools.partial(update_kernel, replicas, subs),
        grid=(tiles,),
        in_specs=[pl.BlockSpec((rows_t // tiles, kept), lambda i: (i, 0))]
        + [whole(t) for t in tables],
        out_specs=pl.BlockSpec((units, step), lambda i: (0, i)),
        out_shape=jax.ShapeDtypeStruct((units, width), BF),
        name="update_step",
    )(bands, *tables)


def make_tables(units):
    left = block_table(units // SPAN)
    right = block_table(TILE // SPAN)
    pieces = []
    for table in (left, left.T, right.T, right):
        high = table.astype(BF)
        pieces += [high, (table - high.astype(np.float32)).astype(BF)]
    return [jnp.asarray(np.ascontiguousarray(p)) for p in pieces]


def remote(src, dst, send, recv, axis, peer):
    return pltpu.make_async_remote_copy(
        src_ref=src,
        dst_ref=dst,
        send_sem=send,
        recv_sem=recv,
        device_id={axis: peer},
        device_id_type=pl.DeviceIdType.MESH,
    )


def split_kernel(
    factor, replicas, tokens_hbm, target_hbm, combine_hbm, filled, gate_hbm, up_hbm, down_hbm,
    momentum_hbm, *refs
):
    tables_hbm, (state, update) = refs[:8], refs[8:10]
    (
        tok, target, combine, combine_x, weight, gate, up, gate_y, up_y, down, hidden, hidden_t,
        kept, sent, came, lent, given, bands, early, early_x, own_band,
    ) = refs[10:31]
    tables_vmem = refs[31:39]
    send, recv, local = refs[39:42]
    me, place = lax.axis_index("narrow"), lax.axis_index("wide")
    x_peer = me + 1 - 2 * (me % 2)
    y_peer = (me + 2) % 4
    twin = place + 1 - 2 * (place % 2)
    z_peer = place + 2 - 4 * (place // 2 % 2)
    others = [(place + k) % replicas for k in range(1, replicas)]
    quarter = place % 4
    rows, width = target.shape
    units = gate.shape[1]
    deep, flat = width // 4, units // 4
    cut = deep // CUTS
    chunks = width // TILE
    tiles = units // TILE
    parts = 2 * CUTS * tiles

    slim = TILE // 2
    sizes = [1, 1, parts, parts, 2] + [chunks] * 3 + [2 * chunks] + [chunks] * 2 + [2]
    starts = [sum(sizes[:k]) for k in range(len(sizes))]

    def link(kind, group, index, src, dst, axis, peer):
        return remote(src, dst, send.at[kind], recv.at[starts[group] + index], axis, peer)

    def sent_all(kind, ref):
        link(kind, 0, 0, ref, ref, "narrow", x_peer).wait_send()

    def cols(c):
        if isinstance(c, int):
            return pl.ds(c * TILE, TILE)
        return pl.ds(pl.multiple_of(c * TILE, TILE), TILE)

    def token_copy():
        return link(0, 0, 0, tokens_hbm, tok.at[pl.ds(rows, rows)], "narrow", x_peer)

    def combine_copy():
        return link(1, 1, 0, combine_hbm, combine_x, "narrow", x_peer)

    def piece(k, ref, owner):
        first = pl.multiple_of(owner * deep + k % CUTS * cut, 16)
        return ref.at[pl.ds(first, cut), cols(k // (2 * CUTS))]

    def weight_copy(kind, k):
        mine, theirs = ((gate_hbm, gate_y), (up_hbm, up_y))[k // CUTS % 2]
        if kind == 2:
            there = piece(k, theirs, quarter)
            return link(2, 2, k, piece(k, mine, quarter), there, "narrow", y_peer)
        if kind == 5:
            there = piece(k, theirs, (quarter + 2) % 4)
            return link(5, 4, k // (parts // 2), there, there, "wide", twin)
        here = piece(k, theirs, quarter)
        if kind == 3:
            return link(3, 3, k, here, here, "wide", z_peer)
        return link(4, 4, k // (parts // 2), here, here, "wide", twin)

    def down_piece(c, ref, first, owner):
        return ref.at[pl.ds(pl.multiple_of(first + owner * flat, 16), flat), cols(c)]

    def down_copy(kind, c):
        if kind == 6:
            src = down_piece(c, down_hbm, 0, quarter)
            return link(6, 5, c, src, down_piece(c, down, units, quarter), "narrow", y_peer)
        if kind == 9:
            there = down_piece(c, down, units, (quarter + 2) % 4)
            return link(9, 7, c, there, there, "wide", twin)
        here = down_piece(c, down, units, quarter)
        if kind == 7:
            return link(7, 6, c, here, here, "wide", z_peer)
        return link(8, 7, c, here, here, "wide", twin)

    def slim_cols(c):
        if isinstance(c, int):
            return pl.ds(c * slim, slim)
        return pl.ds(pl.multiple_of(c * slim, slim), slim)

    def half_copy(k, c):
        part = pl.ds(k * rows, rows)
        src, dst = sent.at[part, slim_cols(c)], came.at[part, slim_cols(c)]
        return link(10, 8, c, src, dst, "narrow", x_peer)

    def halves_copy(c):
        at = slim_cols(c)
        return link(10, 8, c, sent.at[:, at], came.at[:, at], "narrow", x_peer)

    def slim_grad_copy(c):
        at = slim_cols(c)
        return link(11, 9, c // 2, lent.at[:, at], given.at[:, at], "narrow", y_peer)

    def grad_copy(c):
        return link(11, 9, c, lent.at[:, cols(c)], given.at[:, cols(c)], "narrow", y_peer)

    kept_t = TILE // SPAN * BAND

    def band_rows(c):
        return pl.ds(pl.multiple_of(c * kept_t, kept_t), kept_t)

    def band_copy(k, c):
        mine = bands.at[place, band_rows(c)]
        return link(12, 10, c, mine, mine, "wide", others[k])

    def bands_copy(c):
        there = bands.at[pl.ds(0, replicas - 1), band_rows(c)]
        return link(12, 10, c, there, there, "wide", others[0])

    def early_copy(h):
        return link(13, 11, h, early.at[h], early_x.at[h], "narrow", y_peer)

    def load(k, src, dst):
        return pltpu.make_async_copy(src, dst, local.at[k])

    barrier = pltpu.get_barrier_semaphore()
    for axis, peer in [("narrow", x_peer), ("narrow", y_peer)] + [("wide", p) for p in others]:
        pl.semaphore_signal(
            barrier, inc=1, device_id={axis: peer}, device_id_type=pl.DeviceIdType.MESH
        )
    loads = [
        load(0, tokens_hbm, tok.at[pl.ds(0, rows)]),
        load(1, gate_hbm, gate),
        load(2, up_hbm, up),
        load(3, combine_hbm, combine),
        load(4, down_hbm, down.at[pl.ds(0, units)]),
        load(5, target_hbm, target),
        load(6, momentum_hbm, state),
    ]
    loads += [load(7 + k, s, d) for k, (s, d) in enumerate(zip(tables_hbm, tables_vmem))]
    for copy in loads:
        copy.start()
    pl.semaphore_wait(barrier, 1 + replicas)
    combine_copy().start()
    token_copy().start()
    for k in range(parts):
        weight_copy(2, k).start()

    @pl.loop(0, chunks)
    def _(c):
        down_copy(6, c).start()

    def expert(first, count, gates, ups, base, t):
        block = tok[first : first + count, :]
        gated = jnp.dot(block, gates[:, cols(t)], preferred_element_type=F32)
        raised = jnp.dot(block, ups[:, cols(t)], preferred_element_type=F32)
        value = gated / (1.0 + jnp.exp(-gated)) * raised
        at = slice(base + t * TILE, base + (t + 1) * TILE)
        hidden[first : first + count, at] = value.astype(BF)
        hidden_t[at, first : first + count] = value.T.astype(BF)

    def pass_weight(k):
        weight_copy(2, k).wait_recv()
        weight_copy(3, k).start()
        weight_copy(4, k).start()

    def share_weight(k):
        weight_copy(3, k).wait_recv()
        weight_copy(5, k).start()

    all_pieces = gate_y.at[pl.ds(0, 2 * deep)]

    def take_weights(k):
        link(4, 4, k, all_pieces, all_pieces, "wide", twin).wait_recv()

    def pass_down(c):
        down_copy(6, c).wait_recv()
        down_copy(7, c).start()
        down_copy(8, c).start()

    def share_down(c):
        down_copy(7, c).wait_recv()
        down_copy(9, c).start()

    def take_down(c):
        both = down.at[pl.ds(units, 2 * flat), cols(c)]
        link(8, 7, c, both, both, "wide", twin).wait_recv()

    def wide_weight(k):
        return jnp.concatenate([weight[k]] * (TILE // weight.shape[2]), axis=1)

    def peer_half(c):
        part = jnp.dot(hidden[rows:, :], down[:, cols(c)], preferred_element_type=F32)
        sent[rows:, cols(c)] = part.astype(BF)
        half_copy(1, 2 * c).start()
        scale = wide_weight(1)
        kept[rows:, cols(c)] = scale * (scale * part)

    def own_half(c):
        part = jnp.dot(hidden[:rows, :], down[:, cols(c)], preferred_element_type=F32)
        scale = wide_weight(0)
        value = scale * (scale * part - target[:, cols(c)].astype(F32))
        sent[:rows, cols(c)] = value.astype(BF)
        half_copy(0, 2 * c).start()
        half_copy(1, 2 * c + 1).start()
        half_copy(0, 2 * c + 1).start()
        kept[:rows, cols(c)] = value

    tables = lambda: [(tables_vmem[2 * k][...], tables_vmem[2 * k + 1][...]) for k in range(4)]

    def encode(value):
        table = tables()
        width = value.shape[1]
        right = tuple(part[:width, : width // SPAN * BAND] for part in table[2])
        squeezed = dot3(table[0], halves(value), (1, 0))
        return dot3(halves(squeezed), right, (1, 0))

    last = chunks - 1

    def lend(c):
        at = slim_cols(c)
        halves_copy(c).wait_recv()
        scale = weight[0]
        mine = kept[:rows, at] + scale * (scale * came[rows:, at].astype(F32))
        theirs = kept[rows:, at] + came[:rows, at].astype(F32)
        error = jnp.concatenate([mine.astype(BF), theirs.astype(BF)], axis=0)
        grad = jnp.dot(hidden_t[units:, :], error, preferred_element_type=F32)
        lent[:, at] = (factor * grad).astype(BF)

        for h in range(2):

            @pl.when(c == 2 * last + h)
            def _():
                part = lent[:, slim_cols(2 * last + h)].astype(F32)
                early[h] = encode(part).T.astype(BF)
                early_copy(h).start()

        slim_grad_copy(c).start()
        grad = jnp.dot(hidden_t[:units, :], error, preferred_element_type=F32)
        state[0, :, at] = 0.999 * state[0, :, at] + factor * grad

        for h in range(2):

            @pl.when(c == 2 * last + h)
            def _():
                own_band[h] = encode(state[0, :, slim_cols(2 * last + h)]).T

    def send_band(c, value):
        bands[place, band_rows(c), :] = value.astype(BF)
        for k in range(replicas - 1):
            band_copy(k, c).start()

    def send_last(h):
        early_copy(h).wait_recv()
        at = pl.ds(last * kept_t + h * (kept_t // 2), kept_t // 2)
        bands[place, at, :] = (own_band[h] + early_x[h].astype(F32)).astype(BF)
        mine = bands.at[place, at]
        for k in range(replicas - 1):
            link(12, 10, last, mine, mine, "wide", others[k]).start()

    def gradient(c):
        grad_copy(c).wait_recv()
        moved = state[0, :, cols(c)] + given[:, cols(c)].astype(F32)
        band = encode(moved)

        @pl.when(c != last)
        def _():
            send_band(c, band.T)

        state[0, :, cols(c)] = moved - decode_tile(band, tables())

    def shared(c):
        bands_copy(c).wait_recv()
        total = bands[0, band_rows(c), :].astype(F32)
        for k in range(1, replicas):
            total = total + bands[k, band_rows(c), :].astype(F32)
        tile = decode_tile(total.T, tables()) * (1.0 / replicas)
        update[:, cols(c)] = tile.astype(BF)

    for k in range(3):
        loads[k].wait()
    for t in range(tiles):
        expert(0, rows, gate, up, 0, t)
    first = parts // 2
    behind = 3
    for k in range(first + behind):
        pass_weight(k)
        if k >= behind:
            share_weight(k - behind)
    take_weights(0)
    expert(0, rows, gate_y, up_y, units, 0)
    for k in range(first + behind, parts - 1):
        share_weight(k - behind)
        pass_weight(k)
    loads[3].wait()
    combine_copy().wait_recv()
    for k, (owner, ref) in enumerate(((me, combine), (x_peer, combine_x))):
        row_ids = owner * rows + lax.broadcasted_iota(jnp.int32, (1, rows), 1)
        value = ref[...].astype(F32).reshape(1, rows)
        live = jnp.where(row_ids < filled[0], value, 0.0)
        weight[k] = jnp.broadcast_to(live, (weight.shape[2], rows)).T
    share_weight(parts - 1 - behind)
    pass_weight(parts - 1)
    token_copy().wait_recv()
    expert(rows, rows, gate, up, 0, 0)
    share_weight(parts - 3)
    pass_down(0)
    expert(rows, rows, gate, up, 0, 1)
    share_weight(parts - 2)
    pass_down(1)
    expert(rows, rows, gate_y, up_y, units, 0)
    share_weight(parts - 1)
    pass_down(2)
    share_down(0)
    take_weights(1)
    expert(rows, rows, gate_y, up_y, units, 1)
    for copy in loads[4:]:
        copy.wait()
    take_down(0)
    peer_half(0)
    expert(0, rows, gate_y, up_y, units, 1)
    own_half(0)
    share_down(1)
    pass_down(3)
    take_down(1)
    peer_half(1)
    own_half(1)
    share_down(2)

    combine_copy().wait_send()
    token_copy().wait_send()
    for kind in range(2, 6):
        sent_all(kind, all_pieces)

    lag, rest = 1, 1

    @pl.loop(0, chunks + lag + rest)
    def _(c):
        @pl.when(c < chunks)
        def _():
            lend(2 * c)

        @pl.when(c + 4 < chunks)
        def _():
            pass_down(c + 4)

        @pl.when(c + 3 < chunks)
        def _():
            share_down(c + 3)

        @pl.when(c + 2 < chunks)
        def _():
            take_down(c + 2)
            peer_half(c + 2)
            own_half(c + 2)

        @pl.when(c == last)
        def _():
            gradient(c - lag)

        @pl.when(c < chunks)
        def _():
            lend(2 * c + 1)

        @pl.when(c == chunks)
        def _():
            shared(c - lag - rest)

        @pl.when((c >= lag) & (c < chunks + lag) & (c != last))
        def _():
            gradient(c - lag)

        @pl.when(c == last)
        def _():
            send_last(0)
            send_last(1)

        @pl.when((c >= lag + rest) & (c != chunks))
        def _():
            shared(c - lag - rest)

    for kind in range(6, 10):
        sent_all(kind, down.at[pl.ds(0, flat)])
    sent_all(13, early)
    sent_all(10, sent)
    sent_all(11, lent)
    sent_all(12, bands.at[pl.ds(0, replicas - 1)])


def store_kernel(state, update, state_hbm, update_hbm, local):
    half = update.shape[0] // 2
    copies = [pltpu.make_async_copy(update, update_hbm, local.at[2])]
    for k in range(2):
        part = pl.ds(k * half, half)
        copies += [pltpu.make_async_copy(state.at[0, part], state_hbm.at[0, part], local.at[k])]
    for copy in copies:
        copy.start()
    for copy in copies:
        copy.wait()


def store_step(state, update):
    vmem, hbm = pl.BlockSpec(memory_space=pltpu.VMEM), pl.BlockSpec(memory_space=pl.ANY)
    return pl.pallas_call(
        store_kernel,
        in_specs=[vmem] * 2,
        out_specs=[hbm] * 2,
        out_shape=[jax.ShapeDtypeStruct(a.shape, a.dtype) for a in (state, update)],
        scratch_shapes=[pltpu.SemaphoreType.DMA((3,))],
        compiler_params=pltpu.CompilerParams(vmem_limit_bytes=4 << 20),
        name="store_step",
    )(state, update)


def split_step(
    tokens, target, combine, filled, w_gate, w_up, w_down, momentum, tables, factor, replicas
):
    rows, width = tokens.shape
    units = w_down.shape[0]
    hbm = pl.BlockSpec(memory_space=pl.ANY)
    block = lambda *shape: pltpu.VMEM(shape, BF)
    chunks = width // TILE
    count = 6 + 4 * CUTS * (units // TILE) + 7 * chunks
    band_shape = (2, TILE // 2 // SPAN * BAND, units // SPAN * BAND)
    return pl.pallas_call(
        functools.partial(split_kernel, factor, replicas),
        in_specs=[hbm] * 3 + [pl.BlockSpec(memory_space=pltpu.SMEM)] + [hbm] * 12,
        out_specs=[pl.BlockSpec(memory_space=pltpu.VMEM)] * 2,
        out_shape=[pltpu.VMEM((1, units, width), F32), block(units, width)],
        scratch_shapes=[
            block(2 * rows, width), block(rows, width), block(rows), block(rows),
            pltpu.VMEM((2, rows, 128), F32),
            block(width, units), block(width, units), block(width, units), block(width, units),
            block(2 * units, width), block(2 * rows, 2 * units), block(2 * units, 2 * rows),
            pltpu.VMEM((2 * rows, width), F32), block(2 * rows, width), block(2 * rows, width),
            block(units, width), block(units, width),
            block(replicas, width // SPAN * BAND, units // SPAN * BAND),
            block(*band_shape), block(*band_shape), pltpu.VMEM(band_shape, F32),
        ]
        + [block(*t.shape) for t in tables]
        + [
            pltpu.SemaphoreType.DMA((14,)), pltpu.SemaphoreType.DMA((count,)),
            pltpu.SemaphoreType.DMA((15,)),
        ],
        compiler_params=pltpu.CompilerParams(
            collective_id=0, has_side_effects=True, vmem_limit_bytes=48 << 20
        ),
        name="split_step",
    )(tokens, target, combine, filled, w_gate, w_up, w_down, momentum, *tables)


def forward(tokens, target, combine, filled, w_gate, w_up, w_down):
    local_rows = tokens.shape[0]
    piece = lax.all_gather(tokens, "narrow", axis=0, tiled=True)
    gate_proj = jnp.dot(piece, w_gate, preferred_element_type=F32)
    up_proj = jnp.dot(piece, w_up, preferred_element_type=F32)
    hidden = (jax.nn.silu(gate_proj) * up_proj).astype(BF)
    summed = lax.psum_scatter(
        jnp.dot(hidden, w_down, preferred_element_type=F32).astype(BF),
        "narrow",
        scatter_dimension=0,
        tiled=True,
    ).astype(F32)
    weight = combine.astype(F32)[:, None]
    row_ids = lax.axis_index("narrow") * local_rows + jnp.arange(local_rows, dtype=jnp.int32)
    error = jnp.where(
        (row_ids < filled[0])[:, None], weight * (weight * summed - target.astype(F32)), 0.0
    ).astype(BF)
    return hidden.T, lax.all_gather(error, "narrow", axis=0, tiled=True)


def body(tokens, target, combine, filled, w_gate, w_up, w_down, momentum):
    units, width = w_down.shape
    narrow, replicas = lax.axis_size("narrow"), lax.axis_size("wide")
    total_rows = tokens.shape[0] * narrow
    tables = make_tables(units)
    factor = 1.0 / math.sqrt(total_rows)
    fits = units == 2 * TILE and width % (64 * CUTS) == 0 and tokens.shape[0] % 128 == 0
    if narrow == 4 and replicas % 4 == 0 and fits:
        state, update = split_step(
            tokens, target, combine, filled, w_gate, w_up, w_down, momentum, tables, factor,
            replicas,
        )
        return store_step(state, update)
    hidden_t, errors = forward(tokens, target, combine, filled, w_gate, w_up, w_down)
    residue, band = grad_step(hidden_t, errors, momentum, tables, factor)
    bands = lax.all_gather(band.astype(BF)[None], "wide", axis=0, tiled=True)
    total = jnp.sum(bands.astype(F32), axis=0)
    return residue, update_step(total, tables, units, width, replicas)


def solution(mesh):
    in_specs = (
        P(("wide", "narrow"), None),
        P(("wide", "narrow"), None),
        P(("wide", "narrow")),
        P("wide"),
        P(None, "narrow"),
        P(None, "narrow"),
        P("narrow", None),
        P("wide", "narrow", None),
    )
    out_specs = (P("wide", "narrow", None), P("narrow", None))
    return jax.shard_map(body, mesh=mesh, in_specs=in_specs, out_specs=out_specs, check_vma=False)
```

```python
import functools
import math

import jax
import jax.numpy as jnp
import numpy as np
from jax import lax
from jax.experimental import pallas as pl
from jax.experimental.pallas import tpu as pltpu
from jax.sharding import PartitionSpec as P

SPAN = 64
BAND = 16
TILE = 256
CUTS = 4
BF = jnp.bfloat16
F32 = jnp.float32


def block_table(blocks):
    row = np.arange(blocks * BAND)[:, None]
    col = np.arange(blocks * SPAN)[None, :]
    factor = np.where(row % BAND == 0, math.sqrt(1.0 / SPAN), math.sqrt(2.0 / SPAN))
    value = factor * np.cos(math.pi * (2.0 * (col % SPAN) + 1.0) * (row % BAND) / (2.0 * SPAN))
    return np.where(row // BAND == col // SPAN, value, 0.0).astype(np.float32)


def halves(value):
    high = value.astype(BF)
    return high, (value - high.astype(F32)).astype(BF)


def dot3(left, right, contract):
    dims = (((contract[0],), (contract[1],)), ((), ()))
    dot = functools.partial(lax.dot_general, dimension_numbers=dims, preferred_element_type=F32)
    return dot(left[0], right[0]) + (dot(left[1], right[0]) + dot(left[0], right[1]))


def decode_tile(band, tables):
    wide = dot3(halves(band), tables[3], (1, 0))
    return dot3(tables[1], halves(wide), (1, 0))


def read_tables(refs):
    return [(refs[2 * k][...], refs[2 * k + 1][...]) for k in range(4)]


def grad_kernel(factor, subs, hidden_t, error, momentum, *refs):
    residue, band_t = refs[8:]
    tables = read_tables(refs)
    kept_t = TILE // SPAN * BAND
    for k in range(subs):
        at = slice(k * TILE, (k + 1) * TILE)
        grad = jnp.dot(hidden_t[...], error[:, at], preferred_element_type=F32)
        moved = 0.999 * momentum[0, :, at] + factor * grad
        squeezed = dot3(tables[0], halves(moved), (1, 0))
        band = dot3(halves(squeezed), tables[2], (1, 0))
        band_t[k * kept_t : (k + 1) * kept_t, :] = band.T
        residue[0, :, at] = moved - decode_tile(band, tables)


def whole(a):
    return pl.BlockSpec(a.shape, lambda i: (0,) * a.ndim)


def grad_step(hidden_t, error, momentum, tables, factor):
    units, rows = hidden_t.shape
    width = error.shape[1]
    subs = 3 if width // TILE % 3 == 0 else 1
    step = TILE * subs
    tiles = width // step
    kept = units // SPAN * BAND
    kept_t = step // SPAN * BAND
    return pl.pallas_call(
        functools.partial(grad_kernel, factor, subs),
        grid=(tiles,),
        in_specs=[
            whole(hidden_t),
            pl.BlockSpec((rows, step), lambda i: (0, i)),
            pl.BlockSpec((1, units, step), lambda i: (0, 0, i)),
        ]
        + [whole(t) for t in tables],
        out_specs=[
            pl.BlockSpec((1, units, step), lambda i: (0, 0, i)),
            pl.BlockSpec((kept_t, kept), lambda i: (i, 0)),
        ],
        out_shape=[
            jax.ShapeDtypeStruct((1, units, width), F32),
            jax.ShapeDtypeStruct((tiles * kept_t, kept), F32),
        ],
        name="grad_step",
    )(hidden_t, error, momentum, *tables)


def update_kernel(replicas, subs, bands, *refs):
    update = refs[8]
    tables = read_tables(refs)
    kept_t = TILE // SPAN * BAND
    for k in range(subs):
        band = bands[k * kept_t : (k + 1) * kept_t, :].T
        tile = decode_tile(band, tables) * (1.0 / replicas)
        update[:, k * TILE : (k + 1) * TILE] = tile.astype(BF)


def update_step(bands, tables, units, width, replicas):
    rows_t, kept = bands.shape
    subs = 3 if width // TILE % 3 == 0 else 1
    step = TILE * subs
    tiles = width // step
    return pl.pallas_call(
        functools.partial(update_kernel, replicas, subs),
        grid=(tiles,),
        in_specs=[pl.BlockSpec((rows_t // tiles, kept), lambda i: (i, 0))]
        + [whole(t) for t in tables],
        out_specs=pl.BlockSpec((units, step), lambda i: (0, i)),
        out_shape=jax.ShapeDtypeStruct((units, width), BF),
        name="update_step",
    )(bands, *tables)


def make_tables(units):
    left = block_table(units // SPAN)
    right = block_table(TILE // SPAN)
    pieces = []
    for table in (left, left.T, right.T, right):
        high = table.astype(BF)
        pieces += [high, (table - high.astype(np.float32)).astype(BF)]
    return [jnp.asarray(np.ascontiguousarray(p)) for p in pieces]


def remote(src, dst, send, recv, axis, peer):
    return pltpu.make_async_remote_copy(
        src_ref=src,
        dst_ref=dst,
        send_sem=send,
        recv_sem=recv,
        device_id={axis: peer},
        device_id_type=pl.DeviceIdType.MESH,
    )


def split_kernel(
    factor, replicas, tokens_hbm, target_hbm, combine_hbm, filled, gate_hbm, up_hbm, down_hbm,
    momentum_hbm, *refs
):
    tables_hbm, (state, update) = refs[:8], refs[8:10]
    (
        tok, target, combine, combine_x, weight, gate, up, gate_y, up_y, down, hidden, hidden_t,
        kept, sent, came, lent, given, bands, early, early_x, own_band,
    ) = refs[10:31]
    tables_vmem = refs[31:39]
    send, recv, local = refs[39:42]
    me, place = lax.axis_index("narrow"), lax.axis_index("wide")
    x_peer = me + 1 - 2 * (me % 2)
    y_peer = (me + 2) % 4
    twin = place + 1 - 2 * (place % 2)
    z_peer = place + 2 - 4 * (place // 2 % 2)
    others = [(place + k) % replicas for k in range(1, replicas)]
    quarter = place % 4
    rows, width = target.shape
    units = gate.shape[1]
    deep, flat = width // 4, units // 4
    cut = deep // CUTS
    chunks = width // TILE
    tiles = units // TILE
    parts = 2 * CUTS * tiles

    slim = TILE // 2
    sizes = [1, 1, parts, parts, 2] + [chunks] * 3 + [2 * chunks] + [chunks] * 2 + [2]
    starts = [sum(sizes[:k]) for k in range(len(sizes))]

    def link(kind, group, index, src, dst, axis, peer):
        return remote(src, dst, send.at[kind], recv.at[starts[group] + index], axis, peer)

    def sent_all(kind, ref):
        link(kind, 0, 0, ref, ref, "narrow", x_peer).wait_send()

    def cols(c):
        if isinstance(c, int):
            return pl.ds(c * TILE, TILE)
        return pl.ds(pl.multiple_of(c * TILE, TILE), TILE)

    def token_copy():
        return link(0, 0, 0, tokens_hbm, tok.at[pl.ds(rows, rows)], "narrow", x_peer)

    def combine_copy():
        return link(1, 1, 0, combine_hbm, combine_x, "narrow", x_peer)

    def piece(k, ref, owner):
        first = pl.multiple_of(owner * deep + k % CUTS * cut, 16)
        return ref.at[pl.ds(first, cut), cols(k // (2 * CUTS))]

    def weight_copy(kind, k):
        mine, theirs = ((gate_hbm, gate_y), (up_hbm, up_y))[k // CUTS % 2]
        if kind == 2:
            there = piece(k, theirs, quarter)
            return link(2, 2, k, piece(k, mine, quarter), there, "narrow", y_peer)
        if kind == 5:
            there = piece(k, theirs, (quarter + 2) % 4)
            return link(5, 4, k // (parts // 2), there, there, "wide", twin)
        here = piece(k, theirs, quarter)
        if kind == 3:
            return link(3, 3, k, here, here, "wide", z_peer)
        return link(4, 4, k // (parts // 2), here, here, "wide", twin)

    def down_piece(c, ref, first, owner):
        return ref.at[pl.ds(pl.multiple_of(first + owner * flat, 16), flat), cols(c)]

    def down_copy(kind, c):
        if kind == 6:
            src = down_piece(c, down_hbm, 0, quarter)
            return link(6, 5, c, src, down_piece(c, down, units, quarter), "narrow", y_peer)
        if kind == 9:
            there = down_piece(c, down, units, (quarter + 2) % 4)
            return link(9, 7, c, there, there, "wide", twin)
        here = down_piece(c, down, units, quarter)
        if kind == 7:
            return link(7, 6, c, here, here, "wide", z_peer)
        return link(8, 7, c, here, here, "wide", twin)

    def slim_cols(c):
        if isinstance(c, int):
            return pl.ds(c * slim, slim)
        return pl.ds(pl.multiple_of(c * slim, slim), slim)

    def half_copy(k, c):
        part = pl.ds(k * rows, rows)
        src, dst = sent.at[part, slim_cols(c)], came.at[part, slim_cols(c)]
        return link(10, 8, c, src, dst, "narrow", x_peer)

    def halves_copy(c):
        at = slim_cols(c)
        return link(10, 8, c, sent.at[:, at], came.at[:, at], "narrow", x_peer)

    def slim_grad_copy(c):
        at = slim_cols(c)
        return link(11, 9, c // 2, lent.at[:, at], given.at[:, at], "narrow", y_peer)

    def grad_copy(c):
        return link(11, 9, c, lent.at[:, cols(c)], given.at[:, cols(c)], "narrow", y_peer)

    kept_t = TILE // SPAN * BAND

    def band_rows(c):
        return pl.ds(pl.multiple_of(c * kept_t, kept_t), kept_t)

    def band_copy(k, c):
        mine = bands.at[place, band_rows(c)]
        return link(12, 10, c, mine, mine, "wide", others[k])

    def bands_copy(c):
        there = bands.at[pl.ds(0, replicas - 1), band_rows(c)]
        return link(12, 10, c, there, there, "wide", others[0])

    def early_copy(h):
        return link(13, 11, h, early.at[h], early_x.at[h], "narrow", y_peer)

    def load(k, src, dst):
        return pltpu.make_async_copy(src, dst, local.at[k])

    barrier = pltpu.get_barrier_semaphore()
    for axis, peer in [("narrow", x_peer), ("narrow", y_peer)] + [("wide", p) for p in others]:
        pl.semaphore_signal(
            barrier, inc=1, device_id={axis: peer}, device_id_type=pl.DeviceIdType.MESH
        )
    loads = [
        load(0, tokens_hbm, tok.at[pl.ds(0, rows)]),
        load(1, gate_hbm, gate),
        load(2, up_hbm, up),
        load(3, combine_hbm, combine),
        load(4, down_hbm, down.at[pl.ds(0, units)]),
        load(5, target_hbm, target),
        load(6, momentum_hbm, state),
    ]
    loads += [load(7 + k, s, d) for k, (s, d) in enumerate(zip(tables_hbm, tables_vmem))]
    for copy in loads:
        copy.start()
    pl.semaphore_wait(barrier, 1 + replicas)
    combine_copy().start()
    token_copy().start()
    for k in range(parts):
        weight_copy(2, k).start()

    @pl.loop(0, chunks)
    def _(c):
        down_copy(6, c).start()

    def expert(first, count, gates, ups, base, t):
        block = tok[first : first + count, :]
        gated = jnp.dot(block, gates[:, cols(t)], preferred_element_type=F32)
        raised = jnp.dot(block, ups[:, cols(t)], preferred_element_type=F32)
        value = gated / (1.0 + jnp.exp(-gated)) * raised
        at = slice(base + t * TILE, base + (t + 1) * TILE)
        hidden[first : first + count, at] = value.astype(BF)
        hidden_t[at, first : first + count] = value.T.astype(BF)

    def pass_weight(k):
        weight_copy(2, k).wait_recv()
        weight_copy(3, k).start()
        weight_copy(4, k).start()

    def share_weight(k):
        weight_copy(3, k).wait_recv()
        weight_copy(5, k).start()

    all_pieces = gate_y.at[pl.ds(0, 2 * deep)]

    def take_weights(k):
        link(4, 4, k, all_pieces, all_pieces, "wide", twin).wait_recv()

    def pass_down(c):
        down_copy(6, c).wait_recv()
        down_copy(7, c).start()
        down_copy(8, c).start()

    def share_down(c):
        down_copy(7, c).wait_recv()
        down_copy(9, c).start()

    def take_down(c):
        both = down.at[pl.ds(units, 2 * flat), cols(c)]
        link(8, 7, c, both, both, "wide", twin).wait_recv()

    def wide_weight(k):
        return jnp.concatenate([weight[k]] * (TILE // weight.shape[2]), axis=1)

    def peer_half(c):
        part = jnp.dot(hidden[rows:, :], down[:, cols(c)], preferred_element_type=F32)
        sent[rows:, cols(c)] = part.astype(BF)
        half_copy(1, 2 * c).start()
        scale = wide_weight(1)
        kept[rows:, cols(c)] = scale * (scale * part)

    def own_half(c):
        part = jnp.dot(hidden[:rows, :], down[:, cols(c)], preferred_element_type=F32)
        scale = wide_weight(0)
        value = scale * (scale * part - target[:, cols(c)].astype(F32))
        sent[:rows, cols(c)] = value.astype(BF)
        half_copy(0, 2 * c).start()
        half_copy(1, 2 * c + 1).start()
        half_copy(0, 2 * c + 1).start()
        kept[:rows, cols(c)] = value

    tables = lambda: [(tables_vmem[2 * k][...], tables_vmem[2 * k + 1][...]) for k in range(4)]

    def encode(value):
        table = tables()
        width = value.shape[1]
        right = tuple(part[:width, : width // SPAN * BAND] for part in table[2])
        squeezed = dot3(table[0], halves(value), (1, 0))
        return dot3(halves(squeezed), right, (1, 0))

    last = chunks - 1

    def lend(c):
        at = slim_cols(c)
        halves_copy(c).wait_recv()
        scale = weight[0]
        mine = kept[:rows, at] + scale * (scale * came[rows:, at].astype(F32))
        theirs = kept[rows:, at] + came[:rows, at].astype(F32)
        error = jnp.concatenate([mine.astype(BF), theirs.astype(BF)], axis=0)
        grad = jnp.dot(hidden_t[units:, :], error, preferred_element_type=F32)
        lent[:, at] = (factor * grad).astype(BF)

        for h in range(2):

            @pl.when(c == 2 * last + h)
            def _():
                part = lent[:, slim_cols(2 * last + h)].astype(F32)
                early[h] = encode(part).T.astype(BF)
                early_copy(h).start()

        slim_grad_copy(c).start()
        grad = jnp.dot(hidden_t[:units, :], error, preferred_element_type=F32)
        state[0, :, at] = 0.999 * state[0, :, at] + factor * grad

        for h in range(2):

            @pl.when(c == 2 * last + h)
            def _():
                own_band[h] = encode(state[0, :, slim_cols(2 * last + h)]).T

    def send_band(c, value):
        bands[place, band_rows(c), :] = value.astype(BF)
        for k in range(replicas - 1):
            band_copy(k, c).start()

    def send_last(h):
        early_copy(h).wait_recv()
        at = pl.ds(last * kept_t + h * (kept_t // 2), kept_t // 2)
        bands[place, at, :] = (own_band[h] + early_x[h].astype(F32)).astype(BF)
        mine = bands.at[place, at]
        for k in range(replicas - 1):
            link(12, 10, last, mine, mine, "wide", others[k]).start()

    def gradient(c):
        grad_copy(c).wait_recv()
        moved = state[0, :, cols(c)] + given[:, cols(c)].astype(F32)
        band = encode(moved)

        @pl.when(c != last)
        def _():
            send_band(c, band.T)

        state[0, :, cols(c)] = moved - decode_tile(band, tables())

    def shared(c):
        bands_copy(c).wait_recv()
        total = bands[0, band_rows(c), :].astype(F32)
        for k in range(1, replicas):
            total = total + bands[k, band_rows(c), :].astype(F32)
        tile = decode_tile(total.T, tables()) * (1.0 / replicas)
        update[:, cols(c)] = tile.astype(BF)

    for k in range(3):
        loads[k].wait()
    for t in range(tiles):
        expert(0, rows, gate, up, 0, t)
    first = parts // 2
    behind = 3
    for k in range(first + behind):
        pass_weight(k)
        if k >= behind:
            share_weight(k - behind)
    take_weights(0)
    expert(0, rows, gate_y, up_y, units, 0)
    for k in range(first + behind, parts - 1):
        share_weight(k - behind)
        pass_weight(k)
    for copy in loads[3:]:
        copy.wait()
    combine_copy().wait_recv()
    for k, (owner, ref) in enumerate(((me, combine), (x_peer, combine_x))):
        row_ids = owner * rows + lax.broadcasted_iota(jnp.int32, (1, rows), 1)
        value = ref[...].astype(F32).reshape(1, rows)
        live = jnp.where(row_ids < filled[0], value, 0.0)
        weight[k] = jnp.broadcast_to(live, (weight.shape[2], rows)).T
    share_weight(parts - 1 - behind)
    pass_weight(parts - 1)
    token_copy().wait_recv()
    expert(rows, rows, gate, up, 0, 0)
    share_weight(parts - 3)
    pass_down(0)
    expert(rows, rows, gate, up, 0, 1)
    share_weight(parts - 2)
    pass_down(1)
    expert(rows, rows, gate_y, up_y, units, 0)
    share_weight(parts - 1)
    pass_down(2)
    share_down(0)
    take_weights(1)
    expert(rows, rows, gate_y, up_y, units, 1)
    take_down(0)
    peer_half(0)
    expert(0, rows, gate_y, up_y, units, 1)
    own_half(0)
    share_down(1)
    pass_down(3)
    take_down(1)
    peer_half(1)
    own_half(1)
    share_down(2)

    combine_copy().wait_send()
    token_copy().wait_send()
    for kind in range(2, 6):
        sent_all(kind, all_pieces)

    lag, rest = 1, 1

    @pl.loop(0, chunks + lag + rest)
    def _(c):
        @pl.when(c < chunks)
        def _():
            lend(2 * c)

        @pl.when(c + 4 < chunks)
        def _():
            pass_down(c + 4)

        @pl.when(c + 3 < chunks)
        def _():
            share_down(c + 3)

        @pl.when(c + 2 < chunks)
        def _():
            take_down(c + 2)
            peer_half(c + 2)
            own_half(c + 2)

        @pl.when(c == last)
        def _():
            gradient(c - lag)

        @pl.when(c < chunks)
        def _():
            lend(2 * c + 1)

        @pl.when(c == chunks)
        def _():
            shared(c - lag - rest)

        @pl.when((c >= lag) & (c < chunks + lag) & (c != last))
        def _():
            gradient(c - lag)

        @pl.when(c == last)
        def _():
            send_last(0)
            send_last(1)

        @pl.when((c >= lag + rest) & (c != chunks))
        def _():
            shared(c - lag - rest)

    for kind in range(6, 10):
        sent_all(kind, down.at[pl.ds(0, flat)])
    sent_all(13, early)
    sent_all(10, sent)
    sent_all(11, lent)
    sent_all(12, bands.at[pl.ds(0, replicas - 1)])


def store_kernel(state, update, state_hbm, update_hbm, local):
    half = update.shape[0] // 2
    copies = [pltpu.make_async_copy(update, update_hbm, local.at[2])]
    for k in range(2):
        part = pl.ds(k * half, half)
        copies += [pltpu.make_async_copy(state.at[0, part], state_hbm.at[0, part], local.at[k])]
    for copy in copies:
        copy.start()
    for copy in copies:
        copy.wait()


def store_step(state, update):
    vmem, hbm = pl.BlockSpec(memory_space=pltpu.VMEM), pl.BlockSpec(memory_space=pl.ANY)
    return pl.pallas_call(
        store_kernel,
        in_specs=[vmem] * 2,
        out_specs=[hbm] * 2,
        out_shape=[jax.ShapeDtypeStruct(a.shape, a.dtype) for a in (state, update)],
        scratch_shapes=[pltpu.SemaphoreType.DMA((3,))],
        compiler_params=pltpu.CompilerParams(vmem_limit_bytes=4 << 20),
        name="store_step",
    )(state, update)


def split_step(
    tokens, target, combine, filled, w_gate, w_up, w_down, momentum, tables, factor, replicas
):
    rows, width = tokens.shape
    units = w_down.shape[0]
    hbm = pl.BlockSpec(memory_space=pl.ANY)
    block = lambda *shape: pltpu.VMEM(shape, BF)
    chunks = width // TILE
    count = 6 + 4 * CUTS * (units // TILE) + 7 * chunks
    band_shape = (2, TILE // 2 // SPAN * BAND, units // SPAN * BAND)
    return pl.pallas_call(
        functools.partial(split_kernel, factor, replicas),
        in_specs=[hbm] * 3 + [pl.BlockSpec(memory_space=pltpu.SMEM)] + [hbm] * 12,
        out_specs=[pl.BlockSpec(memory_space=pltpu.VMEM)] * 2,
        out_shape=[pltpu.VMEM((1, units, width), F32), block(units, width)],
        scratch_shapes=[
            block(2 * rows, width), block(rows, width), block(rows), block(rows),
            pltpu.VMEM((2, rows, 128), F32),
            block(width, units), block(width, units), block(width, units), block(width, units),
            block(2 * units, width), block(2 * rows, 2 * units), block(2 * units, 2 * rows),
            pltpu.VMEM((2 * rows, width), F32), block(2 * rows, width), block(2 * rows, width),
            block(units, width), block(units, width),
            block(replicas, width // SPAN * BAND, units // SPAN * BAND),
            block(*band_shape), block(*band_shape), pltpu.VMEM(band_shape, F32),
        ]
        + [block(*t.shape) for t in tables]
        + [
            pltpu.SemaphoreType.DMA((14,)), pltpu.SemaphoreType.DMA((count,)),
            pltpu.SemaphoreType.DMA((15,)),
        ],
        compiler_params=pltpu.CompilerParams(
            collective_id=0, has_side_effects=True, vmem_limit_bytes=48 << 20
        ),
        name="split_step",
    )(tokens, target, combine, filled, w_gate, w_up, w_down, momentum, *tables)


def forward(tokens, target, combine, filled, w_gate, w_up, w_down):
    local_rows = tokens.shape[0]
    piece = lax.all_gather(tokens, "narrow", axis=0, tiled=True)
    gate_proj = jnp.dot(piece, w_gate, preferred_element_type=F32)
    up_proj = jnp.dot(piece, w_up, preferred_element_type=F32)
    hidden = (jax.nn.silu(gate_proj) * up_proj).astype(BF)
    summed = lax.psum_scatter(
        jnp.dot(hidden, w_down, preferred_element_type=F32).astype(BF),
        "narrow",
        scatter_dimension=0,
        tiled=True,
    ).astype(F32)
    weight = combine.astype(F32)[:, None]
    row_ids = lax.axis_index("narrow") * local_rows + jnp.arange(local_rows, dtype=jnp.int32)
    error = jnp.where(
        (row_ids < filled[0])[:, None], weight * (weight * summed - target.astype(F32)), 0.0
    ).astype(BF)
    return hidden.T, lax.all_gather(error, "narrow", axis=0, tiled=True)


def body(tokens, target, combine, filled, w_gate, w_up, w_down, momentum):
    units, width = w_down.shape
    narrow, replicas = lax.axis_size("narrow"), lax.axis_size("wide")
    total_rows = tokens.shape[0] * narrow
    tables = make_tables(units)
    factor = 1.0 / math.sqrt(total_rows)
    fits = units == 2 * TILE and width % (64 * CUTS) == 0 and tokens.shape[0] % 128 == 0
    if narrow == 4 and replicas % 4 == 0 and fits:
        state, update = split_step(
            tokens, target, combine, filled, w_gate, w_up, w_down, momentum, tables, factor,
            replicas,
        )
        return store_step(state, update)
    hidden_t, errors = forward(tokens, target, combine, filled, w_gate, w_up, w_down)
    residue, band = grad_step(hidden_t, errors, momentum, tables, factor)
    bands = lax.all_gather(band.astype(BF)[None], "wide", axis=0, tiled=True)
    total = jnp.sum(bands.astype(F32), axis=0)
    return residue, update_step(total, tables, units, width, replicas)


def solution(mesh):
    in_specs = (
        P(("wide", "narrow"), None),
        P(("wide", "narrow"), None),
        P(("wide", "narrow")),
        P("wide"),
        P(None, "narrow"),
        P(None, "narrow"),
        P("narrow", None),
        P("wide", "narrow", None),
    )
    out_specs = (P("wide", "narrow", None), P("narrow", None))
    return jax.shard_map(body, mesh=mesh, in_specs=in_specs, out_specs=out_specs, check_vma=False)
```
